32 devices in a mesh: dp: 2 (over x), col: 4 (over y, core), row: 4 (over z).
Axes of the slice: x: 2, y: 2, z: 4, core: 2. Of those that a mesh axis runs over, the one named last changes fastest.
Arguments:
- tokens: bfloat16 [16, 2048, 512], P(('dp', 'row'), 'col'), may hold values from -6 to 6
- doc_lengths: int32 [16, 8], P(('dp', 'row')), may hold values from 1 to 1024, 2048 in all within a row
- norm_gain: float32 [512], replicated, may hold values from 0.25 to 1.75
- norm_shift: float32 [512], replicated, may hold values from -1 to 1
- qkv_weight: float32 [512, 1536], P('row', 'col'), may hold values from -0.25 to 0.25
- query_bias: float32 [512], replicated, may hold values from -2.5 to 2.5
- value_bias: float32 [512], replicated, may hold values from -0.5 to 0.5
- mix_weight: float32 [512, 512], P('row', 'col'), may hold values from -1 to 1
- mix_bias: float32 [512], replicated, may hold values from -1 to 1
- ffn_gain: float32 [512], replicated, may hold values from 0.25 to 1.75
- ffn_shift: float32 [512], replicated, may hold values from -1 to 1
- up_weight: float32 [512, 2048], P('row', 'col'), may hold values from -0.25 to 0.25
- up_bias: float32 [2048], replicated, may hold values from -2.5 to 2.5
- down_weight: float32 [2048, 512], P('row', 'col'), may hold values from -0.125 to 0.125
- down_bias: float32 [512], replicated, may hold values from -1 to 1
- cotangent: bfloat16 [16, 2048, 512], P(('dp', 'row'), 'col'), may hold values from -6 to 6
Outputs:
- layer_out: bfloat16 [16, 2048, 512], P(('dp', 'row'), 'col')
- tokens_grad: bfloat16 [16, 2048, 512], P(('dp', 'row'), 'col')
- qkv_grad: float32 [512, 1536], P('row', 'col')
- mix_grad: float32 [512, 512], P('row', 'col')
- up_grad: float32 [512, 2048], P('row', 'col')
- down_grad: float32 [2048, 512], P('row', 'col')
- vector_grads: float32 [8, 512], replicated
- hidden_grad: float32 [2048], replicated
The draws below stay inside these ranges and needn't reach their ends.
Inputs may be any that keep to these rules, and one draw needn't show every extreme that they name: `doc_lengths`: the 8 document lengths of a sequence sum to 2048; in every sequence the longest is 1024 tokens.
All inputs are finite; a program needn't handle non-finite values.
Results may differ from the reference program's by a relative error of at most 0.017.
Values may be sent and summed in bfloat16 or wider, within the bound.
No kernel may reach another device: no remote copies, remote signals or barrier semaphores. Data moves between devices by JAX's collectives and lax.ppermute only.
A program may use at most 128 MiB of HBM per device.

```python
import math
import jax
import jax.numpy as jnp
import numpy as np
from jax import lax

D = 512
HEADS = 8
HEAD_DIM = 64
FF = 2048
DOCS = 8
LENGTH = 2048
SEQ_ALL = 16


def spiked(entries, stream_key, source, target, shards_of, factor):
    owner, partner = [(jnp.arange(entries.shape[position]) // (entries.shape[position] // shards_of)).reshape([-1 if axis == position else 1 for axis in range(entries.ndim)]) for position in (source, target)]
    chosen = jax.random.permutation(stream_key, shards_of)[partner]
    strong = (owner == chosen) | (owner == (partner + shards_of // 2) % shards_of)
    return jnp.where(strong, factor * entries, entries)


def block_levels(key, extent, pieces, smallest, high):
    level = 1.0
    for dim, parts in pieces:
        heights = jax.random.uniform(jax.random.fold_in(jax.random.fold_in(key, 6), dim), (parts,), jnp.float32, smallest / len(pieces), high / len(pieces))
        level = level * jnp.repeat(jnp.exp(heights), extent[dim] // parts).reshape((-1,) + (1,) * (len(extent) - 1 - dim))
    return level


def length_profile(amount, total, bound, lean):
    loads = [(1 << 20) // math.isqrt(grade ** lean) + 1 for grade in range(2, amount + 1)]
    spare, given = total - bound - (amount - 1), [1] * (amount - 1)
    while spare > 0:
        movable = [i for i in range(amount - 1) if given[i] < bound]
        whole, budget = sum([loads[i] for i in movable]), spare
        for i in movable:
            addition = min(bound - given[i], max(1, budget * loads[i] // whole), spare)
            given[i] = given[i] + addition
            spare = spare - addition
    return np.array([bound] + given)


def uneven_parts(own_key, amount, total, most, slope):
    if amount == 2:
        one = jax.random.randint(own_key, (), max(1, total - most), min(most, total - 1) + 1)
        return jnp.stack([one, total - one])
    sizes = jnp.asarray(length_profile(amount, total, most, slope), jnp.int32)
    twos = (amount - 1) // 2
    source_of, sink = sizes[1:1 + 2 * twos:2], sizes[2:2 + 2 * twos:2]
    room = jnp.minimum(source_of - 1, most - sink)
    moved = jax.random.randint(jax.random.fold_in(own_key, 1), (twos,), 0, 1 << 20) % (room + 1)
    sizes = sizes.at[1:1 + 2 * twos:2].set(source_of - moved).at[2:2 + 2 * twos:2].set(sink + moved)
    return sizes[jax.random.permutation(jax.random.fold_in(own_key, 2), amount)]


def centred(rng, shape, width, limit, shards=(), held_as=jnp.bfloat16):
    drawn = width * jax.random.normal(rng, shape, jnp.float32)
    if shards:
        drawn = drawn * block_levels(rng, shape, shards, -0.22, 0.18)
    return jnp.clip(drawn, -limit, limit).astype(held_as)


def noise_with(rng, extent, width, most, cuts, heavy, kind=jnp.bfloat16):
    array = width * jax.random.normal(rng, extent, jnp.float32)
    if cuts:
        array = array * block_levels(rng, extent, cuts, -0.22, 0.18)
    return jnp.clip(spiked(array, jax.random.fold_in(rng, 3), *heavy), -most, most).astype(kind)


def setup_inputs(seed: int = 0) -> dict:
    streams_of = jax.random.split(jax.random.key(seed), 17)
    tokens = centred(streams_of[0], (SEQ_ALL, LENGTH, D), 1.0, 6.0, ((0, 8), (1, 4)))
    doc_lengths = jax.vmap(lambda own: uneven_parts(own, DOCS, LENGTH, LENGTH // 2, 1))(jax.random.split(streams_of[1], SEQ_ALL)).reshape((SEQ_ALL, DOCS)).astype(jnp.int32)
    norm_gain = jnp.clip(1.0 + 0.15 * jax.random.normal(streams_of[2], (D,), jnp.float32), 0.25, 1.75)
    norm_shift = centred(streams_of[3], (D,), 0.2, 1.0, (), jnp.float32)
    qkv_weight = centred(streams_of[4], (D, 3 * D), D ** -0.5, 0.25, ((0, 4), (1, 4)), jnp.float32)
    query_bias = centred(streams_of[5], (D,), 0.5, 2.5, (), jnp.float32)
    value_bias = centred(streams_of[6], (D,), 0.1, 0.5, (), jnp.float32)
    mix_weight = centred(streams_of[7], (D, D), (D // 16) ** -0.5, 1.0, ((0, 4), (1, 4)), jnp.float32)
    mix_bias = centred(streams_of[8], (D,), 0.2, 1.0, (), jnp.float32)
    ffn_gain = jnp.clip(1.0 + 0.15 * jax.random.normal(streams_of[9], (D,), jnp.float32), 0.25, 1.75)
    ffn_shift = centred(streams_of[10], (D,), 0.2, 1.0, (), jnp.float32)
    up_weight = centred(streams_of[11], (D, FF), D ** -0.5, 0.25, ((0, 4), (1, 4)), jnp.float32)
    up_bias = centred(streams_of[12], (FF,), 0.5, 2.5, (), jnp.float32)
    down_weight = centred(streams_of[13], (FF, D), FF ** -0.5, 0.125, ((0, 4), (1, 4)), jnp.float32)
    down_bias = centred(streams_of[14], (D,), 0.2, 1.0, (), jnp.float32)
    cotangent = noise_with(streams_of[15], (SEQ_ALL, LENGTH, D), 1.0, 6.0, ((0, 8), (1, 4)), (0, 2, 8, 2.0))
    return dict(tokens=tokens, doc_lengths=doc_lengths, norm_gain=norm_gain, norm_shift=norm_shift, qkv_weight=qkv_weight, query_bias=query_bias, value_bias=value_bias, mix_weight=mix_weight, mix_bias=mix_bias, ffn_gain=ffn_gain, ffn_shift=ffn_shift, up_weight=up_weight, up_bias=up_bias, down_weight=down_weight, down_bias=down_bias, cotangent=cotangent)


@jax.custom_vjp
def low(v):
    return lax.optimization_barrier(v.astype(jnp.bfloat16)).astype(jnp.float32)

@jax.custom_vjp
def low_back(v):
    return v

def low_keep(v):
    return (low(v), None)

def low_pass(kept, grad):
    return (grad,)

def back_keep(v):
    return (v, None)

def back_low(kept, grad):
    return (low(grad),)
low.defvjp(low_keep, low_pass)
low_back.defvjp(back_keep, back_low)
epsilon = 1e-05
masked_out = -1e+30
highest = lax.Precision.HIGHEST

def norm_layer(values, scale_vec, shift_vec):
    center = values - lax.optimization_barrier(jnp.mean(values, axis=-1, keepdims=True))
    spread = lax.optimization_barrier(jnp.mean(center * center, axis=-1, keepdims=True))
    return center * lax.rsqrt(spread + epsilon) * scale_vec + shift_vec

def segment_ids(lengths, full_len):
    doc_ends = jnp.cumsum(lengths, axis=-1).astype(jnp.int32)
    places = jnp.arange(full_len, dtype=jnp.int32)
    passed = places[None, :, None] >= doc_ends[:, None, :]
    return lax.optimization_barrier(jnp.sum(passed.astype(jnp.int32), axis=-1)).astype(jnp.int32)

def attend_rows(query_rows, seg_rows, key_rows, values, seg_seq):
    scores = jnp.einsum('qhd,khd->hqk', query_rows, key_rows, precision=highest) * HEAD_DIM ** (-0.5)
    scores = low_back(scores)
    same_doc = (seg_rows[:, None] == seg_seq[None, :])[None]
    masked = jnp.where(same_doc, scores, masked_out)
    largest = lax.optimization_barrier(jnp.max(masked, axis=-1, keepdims=True))
    weights = jnp.exp(masked - largest)
    probs_low = low(weights / lax.optimization_barrier(jnp.sum(weights, axis=-1, keepdims=True)))
    return jnp.einsum('hqk,khd->qhd', probs_low, values, precision=highest)

def layer_one(tokens_seq, seg_seq, params):
    gain_one, shift_one, qkv_w, query_b, value_b, mix_w, mix_b, gain_two, shift_two, up_w, up_b, down_w, down_b = params
    full_len = tokens_seq.shape[0]
    normed_one = low(norm_layer(tokens_seq, gain_one, shift_one))
    shifts = jnp.concatenate([query_b, jnp.zeros_like(query_b), value_b])
    qkv_rows = low(low_back(jnp.dot(normed_one, qkv_w, precision=highest) + shifts))
    split_rows = qkv_rows.reshape(full_len, 3, HEADS, HEAD_DIM)
    queries = split_rows[:, 0]
    key_rows = split_rows[:, 1]
    values = split_rows[:, 2]
    block_rows = min(512, full_len)
    blocks = full_len // block_rows
    query_blocks = queries.reshape(blocks, block_rows, HEADS, HEAD_DIM)
    seg_blocks = seg_seq.reshape(blocks, block_rows)
    checked = jax.checkpoint(attend_rows)

    def attend_block(items):
        return checked(items[0], items[1], key_rows, values, seg_seq)
    mixed_rows = lax.map(attend_block, (query_blocks, seg_blocks))
    mixed_rows = low(low_back(mixed_rows.reshape(full_len, HEADS * HEAD_DIM)))
    attn_out = low_back(jnp.dot(mixed_rows, mix_w, precision=highest) + mix_b)
    residual = tokens_seq + attn_out
    normed_two = low(norm_layer(residual, gain_two, shift_two))
    hidden = low_back(jnp.dot(normed_two, up_w, precision=highest) + up_b)
    active = low(jax.nn.gelu(hidden, approximate=False))
    ffn_out = low_back(jnp.dot(active, down_w, precision=highest) + down_b)
    return residual + ffn_out

def reference(tokens, doc_lengths, norm_gain, norm_shift, qkv_weight, query_bias, value_bias, mix_weight, mix_bias, ffn_gain, ffn_shift, up_weight, up_bias, down_weight, down_bias, cotangent):
    seg_all = segment_ids(doc_lengths, LENGTH)
    checked_layer = jax.checkpoint(layer_one)

    def whole(tokens_f, param_list):
        params = (param_list[0], param_list[1], low(param_list[2]), param_list[3], param_list[4], low(param_list[5]), param_list[6], param_list[7], param_list[8], low(param_list[9]), param_list[10], low(param_list[11]), param_list[12])

        def one_seq(carry, items):
            return (carry, checked_layer(items[0], items[1], params))
        unused, outputs = lax.scan(one_seq, None, (tokens_f, seg_all))
        return outputs
    param_list = (norm_gain, norm_shift, qkv_weight, query_bias, value_bias, mix_weight, mix_bias, ffn_gain, ffn_shift, up_weight, up_bias, down_weight, down_bias)
    layer_out, pull_back = jax.vjp(whole, tokens.astype(jnp.float32), param_list)
    grad_tokens, grad_params = pull_back(cotangent.astype(jnp.float32))
    vector_grads = jnp.stack([grad_params[0], grad_params[1], grad_params[3], grad_params[4], grad_params[6], grad_params[7], grad_params[8], grad_params[12]])
    return (layer_out.astype(jnp.bfloat16), grad_tokens.astype(jnp.bfloat16), grad_params[2], grad_params[5], grad_params[9], grad_params[11], vector_grads, grad_params[10])
```

```python
import functools

import jax
import jax.numpy as jnp
from jax import lax
from jax.experimental import pallas as pl
from jax.experimental.pallas import tpu as pltpu
from jax.sharding import PartitionSpec as P

HEAD_DIM = 64
EPS = 1e-05
NEG = -1e30
BF = jnp.bfloat16
F32 = jnp.float32
VM = pl.BlockSpec(memory_space=pltpu.VMEM)
SM = pl.BlockSpec(memory_space=pltpu.SMEM)
HBM = pl.BlockSpec(memory_space=pl.ANY)
TQ = 256
TK = 256
FC = 512
RT = 256
KEEP_LB = ((0, 1, 4), (1, 4, 5))
SEND_LB = ((2, 3, 5), (0, 2, 3))


def sds(shape, dtype):
    return jax.ShapeDtypeStruct(shape, dtype)


def call(kernel, name, ins, outs, scratch=(), flops=0, nbytes=0, trans=0, **kw):
    return pl.pallas_call(
        kernel,
        name=name,
        out_shape=tuple(o for o in outs),
        in_specs=[spec for _, spec in ins],
        out_specs=tuple(VM for _ in outs),
        scratch_shapes=list(scratch),
        compiler_params=pltpu.CompilerParams(vmem_limit_bytes=60 * 1024 * 1024, **kw),
        cost_estimate=pl.CostEstimate(flops=flops, bytes_accessed=nbytes, transcendentals=trans),
    )(*[a for a, _ in ins])


def nt(a, b):
    return lax.dot_general(a, b, (((1,), (1,)), ((), ())), preferred_element_type=F32)


def nn(a, b):
    return lax.dot_general(a, b, (((1,), (0,)), ((), ())), preferred_element_type=F32)


def tn(a, b):
    return lax.dot_general(a, b, (((0,), (0,)), ((), ())), preferred_element_type=F32)


def al(value, unit):
    return pl.multiple_of(value, unit)


def normed(v):
    mean = jnp.mean(v, axis=-1, keepdims=True)
    center = v - mean
    rstd = lax.rsqrt(jnp.mean(center * center, axis=-1, keepdims=True) + EPS)
    return center * rstd, rstd


class Geo:
    def __init__(self, dp, col, row, block_len, width, hidden):
        self.dp, self.C, self.R = dp, col, row
        self.G = col // 2
        self.BL = block_len
        self.L = block_len * col
        self.T = 2 * block_len
        self.D = width
        self.FF = hidden
        self.HL = width // self.G
        self.NH = self.HL // HEAD_DIM
        self.fast = (
            dp == 2 and col == 4 and row == 4 and width == 512 and hidden == 2048 and block_len % 256 == 0
        )

    def where(self, meta):
        col = meta[1]
        return col // self.G, col % self.G

    def block(self, s, g, e, d):
        half = s if e == 0 else 1 - s
        return half * self.G + lax.rem(g - d + self.G, self.G)


def norm_kernel(geo, meta, gain, shift, *refs):
    s, g = geo.where(meta)
    pieces, out = refs[:-1], refs[-1]
    for e in range(2):
        for d in range(geo.G):
            src = pieces[e * geo.G + d]
            base = geo.block(s, g, e, d) * geo.BL

            def step(i, carry):
                v = src[pl.ds(al(i * 128, 128), 128), :].astype(F32)
                xhat, _ = normed(v)
                out[pl.ds(al(base + i * 128, 128), 128), :] = (xhat * gain[...] + shift[...]).astype(BF)
                return carry

            lax.fori_loop(0, geo.BL // 128, step, 0, unroll=2)


def qkv_kernel(geo, meta, h1, bias, *refs):
    s, g = geo.where(meta)
    HL, D = geo.HL, geo.D
    if geo.fast:
        pieces, (q, k, v, wown, wscr, sem) = refs[:8], refs[8:]
        x, z = meta[0], meta[2]
        y, c = meta[1] // 2, meta[1] % 2
        copies = []
        for quad in range(4):
            yy = y if quad < 2 else 1 - y
            hh = x if quad % 2 == 0 else 1 - x
            for cc in range(2):
                cp = c if cc == 0 else 1 - c
                for d in range(4):
                    zz = lax.rem(z - d + 4, 4)
                    copies.append(
                        pltpu.make_async_copy(
                            pieces[quad * 2 + cc].at[d],
                            wscr.at[
                                pl.ds(al(zz * 128 + hh * 64, 64), 64),
                                pl.ds(al((2 * yy + cp) * 384, 128), 384),
                            ],
                            sem,
                        )
                    )
        for cpy in copies:
            cpy.start()
        for cpy in copies:
            cpy.wait()
    else:
        w, (q, k, v, wown) = refs[0], refs[1:]
        wscr = w
    for part in range(3):
        cols = pl.ds(al(part * D + g * HL, 128), HL)
        wown[:, part * HL : (part + 1) * HL] = wscr[:, cols]
    outs = (q, k, v)

    def step(i, carry):
        rows = pl.ds(al(i * 256, 256), 256)
        a = h1[rows, :]
        for part in range(3):
            cols = pl.ds(al(part * D + g * HL, 128), HL)
            res = nn(a, wown[:, part * HL : (part + 1) * HL]) + bias[:, cols]
            outs[part][rows, :] = res.astype(BF)
        return carry

    lax.fori_loop(0, geo.L // 256, step, 0)


def doc_ends(doc, s):
    ends, total = [], 0
    for i in range(8):
        total = total + doc[s, i]
        ends.append(total)
    return ends


def span_start(ends, t):
    best = 0
    for e in ends:
        best = jnp.where(e <= t, e, best)
    return best


def span_end(ends, t, full):
    best = full
    for e in reversed(ends):
        best = jnp.where(e > t, e, best)
    return best


def fill_segments(geo, ends, segk, segq):
    def step(i, carry):
        rows = lax.broadcasted_iota(jnp.int32, (TK, 128), 0) + i * TK
        cols = lax.broadcasted_iota(jnp.int32, (8, TQ), 1) + i * TQ
        a = jnp.zeros((TK, 128), jnp.int32)
        b = jnp.zeros((8, TQ), jnp.int32)
        for e in ends:
            a += (rows >= e).astype(jnp.int32)
            b += (cols >= e).astype(jnp.int32)
        segk[pl.ds(al(i * TK, TK), TK), :] = a
        segq[:, pl.ds(al(i * TQ, TQ), TQ)] = b
        return carry

    lax.fori_loop(0, geo.L // TK, step, 0)


def mask_bias(segk, segq, k0, q0):
    a = segk[pl.ds(k0, TK), :]
    b = segq[0:1, pl.ds(q0, TQ)]
    same = jnp.concatenate([a] * (TQ // 128), axis=1) == b
    return jnp.where(same, 0.0, NEG)


def head_mask(HL, h, rows):
    lane = lax.broadcasted_iota(jnp.int32, (rows, HL), 1)
    return (lane // HEAD_DIM) == h


def attn_kernel(geo, meta, doc, q, k, v, *refs):
    G, HL, NH, L, BL = geo.G, geo.HL, geo.NH, geo.L, geo.BL
    outs, lse = refs[:G], refs[G]
    vT, segk, segq, acc, stat = refs[G + 1 :]
    s, g = geo.where(meta)
    ends = doc_ends(doc, s)
    fill_segments(geo, ends, segk, segq)

    def flip(i, carry):
        rows = pl.ds(al(i * TK, TK), TK)
        vT[:, rows] = jnp.transpose(v[rows, :])
        return carry

    lax.fori_loop(0, L // TK, flip, 0)

    def q_step(i, carry):
        q0 = al(i * TQ, TQ)
        klo = span_start(ends, q0) // TK
        khi = (span_end(ends, q0 + TQ - 1, L) + TK - 1) // TK
        qt = q[pl.ds(q0, TQ), :] * jnp.asarray(HEAD_DIM ** (-0.5), BF)
        zero = jnp.zeros_like(qt)
        qm = [jnp.where(head_mask(HL, h, TQ), qt, zero) for h in range(NH)]
        acc[...] = jnp.zeros_like(acc)
        m0 = tuple(jnp.full((1, TQ), -3e38, F32) for _ in range(NH))
        l0 = tuple(jnp.zeros((1, TQ), F32) for _ in range(NH))

        def k_step(j, ml):
            ms, ls = ml
            k0 = al(j * TK, TK)
            kt = k[pl.ds(k0, TK), :]
            bias = mask_bias(segk, segq, k0, q0)
            new_m, new_l = [], []
            for h in range(NH):
                hs = slice(h * HEAD_DIM, (h + 1) * HEAD_DIM)
                st = nt(kt, qm[h]) + bias
                mn = jnp.maximum(ms[h], jnp.max(st, axis=0, keepdims=True))
                p = jnp.exp(st - mn)
                alpha = jnp.exp(ms[h] - mn)
                new_m.append(mn)
                new_l.append(alpha * ls[h] + jnp.sum(p, axis=0, keepdims=True))
                acc[hs, :] = acc[hs, :] * alpha + nn(vT[hs, pl.ds(k0, TK)], p.astype(BF))
            return tuple(new_m), tuple(new_l)

        ms, ls = lax.fori_loop(klo, khi, k_step, (m0, l0))
        for h in range(NH):
            hs = slice(h * HEAD_DIM, (h + 1) * HEAD_DIM)
            acc[hs, :] = acc[hs, :] * (1.0 / ls[h])
            lse[h : h + 1, pl.ds(q0, TQ)] = ms[h] + jnp.log(ls[h])
        res = jnp.transpose(acc[...]).astype(BF)
        b = q0 // BL
        half, gp = b // G, lax.rem(b, G)
        e = jnp.where(half == s, 0, 1)
        off = al(q0 - b * BL, TQ)
        for d in range(G):
            @pl.when(lax.rem(g - gp + G, G) == d)
            def _():
                outs[d][e, pl.ds(off, TQ), :] = res
        return carry

    lax.fori_loop(0, L // TQ, q_step, 0)


def attn_back_kernel(geo, meta, doc, q, k, v, lse, *refs):
    G, HL, NH, L, BL = geo.G, geo.HL, geo.NH, geo.L, geo.BL
    mixed, grads = refs[:G], refs[G : 2 * G]
    out = refs[2 * G]
    qm, gm, kT, dqT, delta, segk, segq, dk, dv = refs[2 * G + 1 :]
    s, g = geo.where(meta)
    ends = doc_ends(doc, s)
    fill_segments(geo, ends, segk, segq)
    scale = HEAD_DIM ** (-0.5)
    for e in range(2):
        for d in range(G):
            base = geo.block(s, g, e, d) * BL

            def load(i, carry):
                src = pl.ds(al(i * 256, 256), 256)
                dst = pl.ds(al(base + i * 256, 256), 256)
                gt = grads[d][e, src, :]
                zero = jnp.zeros_like(gt)
                prod = jnp.transpose(gt.astype(F32) * mixed[d][e, src, :].astype(F32))
                qt = q[dst, :] * jnp.asarray(scale, BF)
                for h in range(NH):
                    hs = slice(h * HEAD_DIM, (h + 1) * HEAD_DIM)
                    keep = head_mask(HL, h, 256)
                    gm[h, dst, :] = jnp.where(keep, gt, zero)
                    qm[h, dst, :] = jnp.where(keep, qt, zero)
                    delta[h : h + 1, dst] = jnp.sum(prod[hs, :], axis=0, keepdims=True)
                kT[:, dst] = jnp.transpose(k[dst, :])
                dqT[:, dst] = jnp.zeros((HL, 256), F32)
                return carry

            lax.fori_loop(0, BL // 256, load, 0)

    def k_step(j, carry):
        k0 = al(j * TK, TK)
        qlo = span_start(ends, k0) // TQ
        qhi = (span_end(ends, k0 + TK - 1, L) + TQ - 1) // TQ
        kt = k[pl.ds(k0, TK), :]
        vt = v[pl.ds(k0, TK), :]
        dk[...] = jnp.zeros_like(dk)
        dv[...] = jnp.zeros_like(dv)

        def q_step(i, c2):
            q0 = al(i * TQ, TQ)
            qs = pl.ds(q0, TQ)
            bias = mask_bias(segk, segq, k0, q0)
            for h in range(NH):
                hs = slice(h * HEAD_DIM, (h + 1) * HEAD_DIM)
                qh, gh = qm[h, qs, :], gm[h, qs, :]
                p = jnp.exp(nt(kt, qh) + (bias - lse[h : h + 1, qs]))
                ds = (p * (nt(vt, gh) - delta[h : h + 1, qs])).astype(BF)
                dv[...] += nn(p.astype(BF), gh)
                dk[...] += nn(ds, qh)
                dqT[hs, qs] += nn(kT[hs, pl.ds(k0, TK)], ds)
            return c2

        lax.fori_loop(qlo, qhi, q_step, 0)
        out[pl.ds(k0, TK), HL : 2 * HL] = dk[...].astype(BF)
        out[pl.ds(k0, TK), 2 * HL : 3 * HL] = dv[...].astype(BF)
        return carry

    lax.fori_loop(0, L // TK, k_step, 0)

    def last(i, carry):
        rows = pl.ds(al(i * TQ, TQ), TQ)
        out[rows, 0:HL] = (jnp.transpose(dqT[:, rows]) * scale).astype(BF)
        return carry

    lax.fori_loop(0, L // TQ, last, 0)


def gelu_parts(u):
    phi = 0.5 + 0.5 * lax.erf(u * (2.0 ** -0.5))
    pdf = jnp.exp(-0.5 * (u * u)) * 0.3989422804014327
    return phi, pdf


def ffn_kernel(geo, meta, *refs):
    G, HL, D, FF, BL, T = geo.G, geo.HL, geo.D, geo.FF, geo.BL, geo.T
    s, g = geo.where(meta)
    x0, x1, cot, cot1, mixb, gain, shift, upb, downb = refs[:9]
    refs = refs[9:]
    mixed, refs = refs[:G], refs[G:]
    nw = 8 if geo.fast else 3
    wts, refs = refs[:nw], refs[nw:]
    out_own, out_send, g_resid = refs[:3]
    refs = refs[3:]
    gmix, refs = refs[:G], refs[G:]
    ng = 2 if geo.fast else 3
    packs, refs = refs[:ng], refs[ng:]
    vec, refs = refs[0], refs[1:]
    resid, h2, ffn, gh2, act_s, gu_s, ga_s, mg = refs[:8]
    refs = refs[8:]
    if geo.fast:
        wo, wu, wd, wg, sems = refs
        x, z = meta[0], meta[2]
        y, c = meta[1] // 2, meta[1] % 2
        groups = [[], [], []]
        for quad in range(4):
            yy = y if quad < 2 else 1 - y
            hh = x if quad % 2 == 0 else 1 - x
            for cc in range(2):
                cl = 2 * yy + (c if cc == 0 else 1 - c)
                src = wts[quad * 2 + cc]
                for d in range(4):
                    zz = lax.rem(z - d + 4, 4)
                    groups[0].append(
                        pltpu.make_async_copy(
                            src.at[d, pl.ds(512, 64), :],
                            wo.at[pl.ds(al(zz * 128 + hh * 64, 64), 64), pl.ds(al(cl * 128, 128), 128)],
                            sems.at[0],
                        )
                    )
                    for b in range(4):
                        groups[1].append(
                            pltpu.make_async_copy(
                                src.at[d, pl.ds(b * 64, 64), :],
                                wu.at[
                                    pl.ds(al(zz * 128 + hh * 64, 64), 64),
                                    pl.ds(al(cl * 512 + b * 128, 128), 128),
                                ],
                                sems.at[1],
                            )
                        )
                    groups[2].append(
                        pltpu.make_async_copy(
                            src.at[d, pl.ds(256, 256), :],
                            wd.at[pl.ds(al(zz * 512 + hh * 256, 256), 256), pl.ds(al(cl * 128, 128), 128)],
                            sems.at[2],
                        )
                    )
        for group in groups:
            for cpy in group:
                cpy.start()
        for cpy in groups[0]:
            cpy.wait()
    else:
        wo, wu, wd = wts
        (wg,) = refs

    zrow = jnp.zeros((1, D), F32)
    vec[...] = jnp.zeros_like(vec)

    for e in range(2):
        xe = x0 if e == 0 else x1
        ce = cot if e == 0 else cot1

        def first(i, carry):
            rows = pl.ds(al(i * RT, RT), RT)
            to = pl.ds(al(e * BL + i * RT, RT), RT)
            r = xe[rows, :].astype(F32) + mixb[...]
            for d in range(G):
                gp = lax.rem(g - d + G, G)
                r = r + nn(mixed[d][e, rows, :], wo[pl.ds(al(gp * HL, 128), HL), :])
            resid[to, :] = r
            xhat, _ = normed(r)
            h2[to, :] = (xhat * gain[...] + shift[...]).astype(BF)
            ffn[to, :] = jnp.zeros((RT, D), F32)
            gh2[to, :] = jnp.zeros((RT, D), F32)
            return carry

        lax.fori_loop(0, BL // RT, first, 0)
    ga_s[0:BL, :] = cot[...]
    ga_s[BL:T, :] = cot1[...]
    if geo.fast:
        for group in groups[1:]:
            for cpy in group:
                cpy.wait()

    def chunk(f, carry):
        f0 = al(f * FC, FC)
        fs = pl.ds(f0, FC)

        def rows_step(i, hs):
            rows = pl.ds(al(i * RT, RT), RT)
            u = nn(h2[rows, :], wu[:, fs]) + upb[:, fs]
            phi, pdf = gelu_parts(u)
            act = (u * phi).astype(BF)
            gu = (nt(ga_s[rows, :], wd[fs, :]) * (phi + u * pdf)).astype(BF)
            act_s[rows, :] = act
            gu_s[rows, :] = gu
            ffn[rows, :] += nn(act, wd[fs, :])
            gh2[rows, :] += nt(gu, wu[:, fs])
            return hs + jnp.sum(gu.astype(F32), axis=0, keepdims=True)

        hsum = lax.fori_loop(0, T // RT, rows_step, jnp.zeros((1, FC), F32))
        per = D // FC
        vec[pl.ds(8 + f // per, 1), pl.ds(al(lax.rem(f, per) * FC, 128), FC)] = hsum
        dn = tn(act_s[...], ga_s[...])
        if geo.fast:
            wg[...] = dn.astype(BF)
            zr = lax.rem(f - z + 4, 4)
            for cr in range(2):
                for yr in range(2):
                    cl = 2 * (y if yr == 0 else 1 - y) + (c if cr == 0 else 1 - c)
                    for hr in range(2):
                        hh = x if hr == 0 else 1 - x
                        packs[cr][yr * 2 + hr, zr, 256:512, :] = wg[
                            pl.ds(al(hh * 256, 256), 256), pl.ds(al(cl * 128, 128), 128)
                        ]
        else:
            packs[1][fs, :] = dn.astype(BF)
        up = tn(h2[...], gu_s[...])
        if geo.fast:
            wg[...] = up.astype(BF)
            fy, fcr = f // 2, lax.rem(f, 2)
            yr = jnp.where(fy == y, 0, 1)
            for cr in range(2):
                @pl.when((fcr == c) if cr == 0 else (fcr != c))
                def _():
                    for hr in range(2):
                        hh = x if hr == 0 else 1 - x
                        for k in range(4):
                            zz = lax.rem(z + k, 4)
                            for b in range(4):
                                packs[cr][yr * 2 + hr, k, b * 64 : b * 64 + 64, :] = wg[
                                    pl.ds(al(zz * 128 + hh * 64, 64), 64), b * 128 : b * 128 + 128
                                ]
        else:
            packs[0][:, fs] = up.astype(BF)
        return carry

    lax.fori_loop(0, FF // FC, chunk, 0)

    sums = (zrow, zrow, zrow, zrow)
    for e in range(2):
        ce = cot if e == 0 else cot1
        oe = out_own if e == 0 else out_send

        def back(i, carry):
            mb, fg, fs_, db = carry
            rows = pl.ds(al(i * RT, RT), RT)
            to = pl.ds(al(e * BL + i * RT, RT), RT)
            r = resid[to, :]
            oe[rows, :] = (r + ffn[to, :] + downb[...]).astype(BF)
            xhat, rstd = normed(r)
            gh = gh2[to, :]
            ct = ce[rows, :].astype(F32)
            gx = gh * gain[...]
            gr = ct + rstd * (
                gx
                - jnp.mean(gx, axis=-1, keepdims=True)
                - xhat * jnp.mean(gx * xhat, axis=-1, keepdims=True)
            )
            g_resid[to, :] = gr
            ga = gr.astype(BF)
            gu_s[to, 0:D] = ga
            for d in range(G):
                gp = lax.rem(g + d, G)
                gmix[d][e, rows, :] = nt(ga, wo[pl.ds(al(gp * HL, 128), HL), :]).astype(BF)
            return (
                mb + jnp.sum(ga.astype(F32), axis=0, keepdims=True),
                fg + jnp.sum(gh * xhat, axis=0, keepdims=True),
                fs_ + jnp.sum(gh, axis=0, keepdims=True),
                db + jnp.sum(ct, axis=0, keepdims=True),
            )

        sums = lax.fori_loop(0, BL // RT, back, sums)
    for i in range(4):
        vec[4 + i : 5 + i, :] = sums[i]
    for d in range(G):
        gp = lax.rem(g - d + G, G)
        part = tn(mixed[d][0], gu_s[0:BL, 0:D]) + tn(mixed[d][1], gu_s[BL:T, 0:D])
        mg[pl.ds(al(gp * HL, 128), HL), :] = part.astype(BF)
    if geo.fast:
        for cr in range(2):
            for yr in range(2):
                cl = 2 * (y if yr == 0 else 1 - y) + (c if cr == 0 else 1 - c)
                for hr in range(2):
                    hh = x if hr == 0 else 1 - x
                    for k in range(4):
                        zz = lax.rem(z + k, 4)
                        packs[cr][yr * 2 + hr, k, 512:576, :] = mg[
                            pl.ds(al(zz * 128 + hh * 64, 64), 64), pl.ds(al(cl * 128, 128), 128)
                        ]
    else:
        packs[2][...] = mg[...]


def qkv_back_kernel(geo, meta, gq, h1, w, vec_in, gain, shift, *refs):
    G, HL, D, BL, L = geo.G, geo.HL, geo.D, geo.BL, geo.L
    s, g = geo.where(meta)
    pieces, refs = refs[: 2 * G], refs[2 * G :]
    ghs, refs = refs[:G], refs[G:]
    ng = 2 if geo.fast else 1
    packs, refs = refs[:ng], refs[ng:]
    vec, wg = refs
    vec[...] = vec_in[...]
    part = tn(h1[...], gq[...])
    wg[...] = part.astype(BF)
    if geo.fast:
        x, z, c = meta[0], meta[2], meta[1] % 2
        for cr, table in ((0, KEEP_LB), (1, SEND_LB)):
            for b in range(3):
                lb = jnp.where(c == 0, table[0][b], table[1][b])
                for hr in range(2):
                    hh = x if hr == 0 else 1 - x
                    for k in range(4):
                        zz = lax.rem(z + k, 4)
                        packs[cr][b, hr, k] = wg[
                            pl.ds(al(zz * 128 + hh * 64, 64), 64), pl.ds(al(lb * 128, 128), 128)
                        ]
    else:
        for p in range(3):
            packs[0][:, pl.ds(al(p * D + g * HL, 128), HL)] = wg[:, p * HL : (p + 1) * HL]
    zrow = jnp.zeros((1, D), F32)
    zh = jnp.zeros((1, HL), F32)
    sums = (zrow, zrow, zh, zh)
    for e in range(2):
        for d in range(G):
            base = geo.block(s, g, e, d) * BL
            src = pieces[e * G + d]

            def step(i, carry):
                ng_, ns, qb, vb = carry
                rows = pl.ds(al(i * RT, RT), RT)
                at = pl.ds(al(base + i * RT, RT), RT)
                xhat, _ = normed(src[rows, :].astype(F32))
                gt = gq[at, :]
                gh = nt(gt, w[...])
                ghs[d][e, rows, :] = gh.astype(ghs[d].dtype)
                return (
                    ng_ + jnp.sum(gh * xhat, axis=0, keepdims=True),
                    ns + jnp.sum(gh, axis=0, keepdims=True),
                    qb + jnp.sum(gt[:, 0:HL].astype(F32), axis=0, keepdims=True),
                    vb + jnp.sum(gt[:, 2 * HL : 3 * HL].astype(F32), axis=0, keepdims=True),
                )

            sums = lax.fori_loop(0, BL // RT, step, sums)
    vec[0:1, :] = sums[0]
    vec[1:2, :] = sums[1]
    cols = pl.ds(al(g * HL, 128), HL)
    vec[2:3, cols] = sums[2]
    vec[3:4, cols] = sums[3]


def last_kernel(geo, meta, gain, g_resid, gh, *refs):
    G, D, BL = geo.G, geo.D, geo.BL
    s, _ = geo.where(meta)
    recv, refs = refs[: G - 1], refs[G - 1 :]
    x0, x1, out, send = refs
    for e in range(2):
        xe = x0 if e == 0 else x1

        def step(i, carry):
            rows = pl.ds(al(i * RT, RT), RT)
            to = pl.ds(al(e * BL + i * RT, RT), RT)
            xhat, rstd = normed(xe[rows, :].astype(F32))
            total = gh[e, rows, :]
            for r in recv:
                total = total + r[e, rows, :].astype(F32)
            gx = total * gain[...]
            res = g_resid[to, :] + rstd * (
                gx
                - jnp.mean(gx, axis=-1, keepdims=True)
                - xhat * jnp.mean(gx * xhat, axis=-1, keepdims=True)
            )
            if e == 0:
                out[s, rows, :] = res.astype(BF)
            else:
                send[rows, :] = res.astype(BF)
            return carry

        lax.fori_loop(0, BL // RT, step, 0)


def core_sum_kernel(own, recv, *outs):
    for q in range(4):
        outs[q][...] = (own[q].astype(F32) + recv[q].astype(F32)).astype(BF)


def arrange_kernel(geo, meta, keep, recv, vec, vrecv, p0, p1, p2, p3, vout):
    y, c = meta[1] // 2, meta[1] % 2
    outs = (p0, p1, p2, p3)
    vout[...] = vec[...] + vrecv[...]
    for cs in range(2):
        mine = sorted((lb // 2) * 4 + 2 * cs + lb % 2 for lb in KEEP_LB[cs])
        theirs = sorted((lb // 2) * 4 + 2 * (1 - cs) + lb % 2 for lb in SEND_LB[1 - cs])
        for ys in range(2):
            @pl.when(jnp.logical_and(c == cs, y == ys))
            def _():
                for yr in range(2):
                    first = 3 * (2 * (ys ^ yr) + cs)
                    for o in range(3):
                        b = first + o
                        src, slot = (keep, mine.index(b)) if b in mine else (recv, theirs.index(b))
                        for hr in range(2):
                            outs[yr * 2 + hr][:, o * 64 : o * 64 + 64, :] = src[slot, hr]


def plane_sum_kernel(has_vec, a, b, c, d, *refs):
    if has_vec:
        va, vb, vc, vd = refs[:4]
        refs = refs[4:]
        refs[4][...] = (va[...] + vb[...]) + (vc[...] + vd[...])
    for k in range(4):
        refs[k][...] = (
            (a[k].astype(F32) + b[k].astype(F32)) + (c[k].astype(F32) + d[k].astype(F32))
        ).astype(BF)


def line_sum_kernel(has_vec, a, b, c, d, *refs):
    if has_vec:
        va, vb, vc, vd = refs[:4]
        refs = refs[4:]
        refs[1][...] = (va[...] + vc[...]) + (vb[...] + vd[...])
    refs[0][...] = (
        (a[...].astype(F32) + b[...].astype(F32)) + (c[...].astype(F32) + d[...].astype(F32))
    ).astype(BF)


def finish_kernel(meta, r, o, qr, qo, qkv, mix, up, down):
    x = meta[0]
    for src, qsrc, h in ((r, qr, x), (o, qo, 1 - x)):
        rows = pl.ds(al(h * 64, 64), 64)
        for b in range(4):
            up[rows, b * 128 : b * 128 + 128] = src[b * 64 : b * 64 + 64, :].astype(F32)
        down[pl.ds(al(h * 256, 256), 256), :] = src[256:512, :].astype(F32)
        mix[rows, :] = src[512:576, :].astype(F32)
        for b in range(3):
            qkv[rows, b * 128 : b * 128 + 128] = qsrc[b * 64 : b * 64 + 64, :].astype(F32)


def pack_kernel(meta, qkv, mix, up, down, first, rest):
    h = meta[0]
    rows = pl.ds(al(h * 64, 64), 64)
    first[...] = qkv[rows, :].astype(BF)
    for b in range(4):
        rest[b * 64 : b * 64 + 64, :] = up[rows, b * 128 : b * 128 + 128].astype(BF)
    rest[256:512, :] = down[pl.ds(al(h * 256, 256), 256), :].astype(BF)
    rest[512:576, :] = mix[rows, :].astype(BF)


def body(
    tokens,
    doc_lengths,
    norm_gain,
    norm_shift,
    qkv_weight,
    query_bias,
    value_bias,
    mix_weight,
    mix_bias,
    ffn_gain,
    ffn_shift,
    up_weight,
    up_bias,
    down_weight,
    down_bias,
    cotangent,
):
    DP, C, R = lax.axis_size("dp"), lax.axis_size("col"), lax.axis_size("row")
    _, BL, D = tokens.shape
    FF = up_bias.shape[0]
    geo = Geo(DP, C, R, BL, D, FF)
    G, HL, L, T = geo.G, geo.HL, geo.L, geo.T
    ix, ic, iz = lax.axis_index("dp"), lax.axis_index("col"), lax.axis_index("row")
    s = ic // G
    meta = jnp.stack([ix, ic, iz]).astype(jnp.int32)

    def swap_half(v):
        return lax.ppermute(v, "col", [(i, (i + G) % C) for i in range(C)])

    def turn(v, d):
        return lax.ppermute(v, "col", [(i, (i // G) * G + (i % G + d) % G) for i in range(C)])

    def plane(v, dx, dy):
        pairs = [
            (i * C + j, ((i + dx) % 2) * C + (j + dy * G) % C) for i in range(2) for j in range(C)
        ]
        return lax.ppermute(v, ("dp", "col"), pairs)

    def line(v, d):
        return lax.ppermute(v, "row", [(i, (i + d) % R) for i in range(R)])

    def row2(v):
        return v.reshape(1, v.shape[0])

    def pick(v, i):
        return lax.dynamic_index_in_dim(v, i, 0, keepdims=False)

    x0 = pick(tokens, s)
    x_send = pick(tokens, 1 - s)
    x1 = swap_half(x_send)
    if geo.fast:
        half_qkv, half_rest = call(
            pack_kernel,
            "pack",
            [(meta, SM), (qkv_weight, VM), (mix_weight, VM), (up_weight, VM), (down_weight, VM)],
            [sds((64, 384), BF), sds((576, 128), BF)],
            nbytes=2 << 20,
        )

        def spread(v):
            lines = jnp.stack([v] + [line(v, d) for d in range(1, 4)])
            quads = [lines, plane(lines, 1, 0), plane(lines, 0, 1), plane(lines, 1, 1)]
            return [p for q in quads for p in (q, turn(q, 1))]

        w_qkv = spread(half_qkv)
        w_rest = spread(half_rest)
    else:
        def whole(w):
            w = lax.all_gather(w.astype(BF), "row", axis=0, tiled=True)
            return lax.all_gather(w, "col", axis=1, tiled=True)

        w_qkv = [whole(qkv_weight)]
        w_rest = [whole(mix_weight), whole(up_weight), whole(down_weight)]
    pieces = [x0] + [turn(x0, d) for d in range(1, G)]
    pieces += [x1] + [turn(x1, d) for d in range(1, G)]
    gain1, shift1 = row2(norm_gain), row2(norm_shift)
    (h1,) = call(
        functools.partial(norm_kernel, geo),
        "norm_one",
        [(meta, SM), (gain1, VM), (shift1, VM)] + [(p, VM) for p in pieces],
        [sds((L, D), BF)],
        flops=L * D * 10,
        nbytes=L * D * 4,
    )
    bias = row2(jnp.concatenate([query_bias, jnp.zeros_like(query_bias), value_bias]))
    wspec = HBM if geo.fast else VM
    q, k, v, w_own = call(
        functools.partial(qkv_kernel, geo),
        "qkv",
        [(meta, SM), (h1, VM), (bias, VM)] + [(w, wspec) for w in w_qkv],
        [sds((L, HL), BF)] * 3 + [sds((D, 3 * HL), BF)],
        scratch=[pltpu.VMEM((D, 3 * D), BF), pltpu.SemaphoreType.DMA(())] if geo.fast else [],
        flops=2 * L * D * 3 * HL,
        nbytes=L * D * 2 + L * HL * 6 + D * D * 6,
    )
    attn = call(
        functools.partial(attn_kernel, geo),
        "attend",
        [(meta, SM), (doc_lengths, SM), (q, VM), (k, VM), (v, VM)],
        [sds((2, BL, HL), BF)] * G + [sds((8, L), F32)],
        scratch=[
            pltpu.VMEM((HL, L), BF),
            pltpu.VMEM((L, 128), jnp.int32),
            pltpu.VMEM((8, L), jnp.int32),
            pltpu.VMEM((HL, TQ), F32),
            pltpu.VMEM((8, TQ), F32),
        ],
        flops=2 * L * L * HL * 4,
        nbytes=L * HL * 8,
        trans=L * L * geo.NH // 2,
    )
    mixed_all, lse = attn[:G], attn[G]
    mixed = [mixed_all[0]] + [turn(mixed_all[G - d], d) for d in range(1, G)]
    cot0 = pick(cotangent, s)
    cot1 = swap_half(pick(cotangent, 1 - s))
    packs_out = [sds((4, 4, 576, 128), BF)] * 2 if geo.fast else [sds((D, FF), BF), sds((FF, D), BF), sds((D, D), BF)]
    weights_scr = (
        [
            pltpu.VMEM((D, D), BF),
            pltpu.VMEM((D, FF), BF),
            pltpu.VMEM((FF, D), BF),
            pltpu.VMEM((FC, FC), BF),
            pltpu.SemaphoreType.DMA((3,)),
        ]
        if geo.fast
        else [pltpu.VMEM((8, 128), BF)]
    )
    res = call(
        functools.partial(ffn_kernel, geo),
        "ffn",
        [(meta, SM), (x0, VM), (x1, VM), (cot0, VM), (cot1, VM)]
        + [(row2(a), VM) for a in (mix_bias, ffn_gain, ffn_shift, up_bias, down_bias)]
        + [(m, VM) for m in mixed]
        + [(w, wspec) for w in w_rest],
        [sds((BL, D), BF), sds((BL, D), BF), sds((T, D), F32)]
        + [sds((2, BL, HL), BF)] * G
        + packs_out
        + [sds((16, D), F32)],
        scratch=[
            pltpu.VMEM((T, D), F32),
            pltpu.VMEM((T, D), BF),
            pltpu.VMEM((T, D), F32),
            pltpu.VMEM((T, D), F32),
            pltpu.VMEM((T, FC), BF),
            pltpu.VMEM((T, FC), BF),
            pltpu.VMEM((T, D), BF),
            pltpu.VMEM((D, D), BF),
        ]
        + weights_scr,
        flops=6 * T * D * (2 * FF + D),
        nbytes=20 << 20,
        trans=2 * T * FF,
    )
    out_own, out_send, g_resid = res[:3]
    gmix = res[3 : 3 + G]
    packs = res[3 + G : -1]
    vec1 = res[-1]
    ghead = [gmix[0]] + [turn(gmix[d], d) for d in range(1, G)]
    (gq,) = call(
        functools.partial(attn_back_kernel, geo),
        "attend_back",
        [(meta, SM), (doc_lengths, SM), (q, VM), (k, VM), (v, VM), (lse, VM)]
        + [(m, VM) for m in mixed_all]
        + [(m, VM) for m in ghead],
        [sds((L, 3 * HL), BF)],
        scratch=[
            pltpu.VMEM((geo.NH, L, HL), BF),
            pltpu.VMEM((geo.NH, L, HL), BF),
            pltpu.VMEM((HL, L), BF),
            pltpu.VMEM((HL, L), F32),
            pltpu.VMEM((8, L), F32),
            pltpu.VMEM((L, 128), jnp.int32),
            pltpu.VMEM((8, L), jnp.int32),
            pltpu.VMEM((TK, HL), F32),
            pltpu.VMEM((TK, HL), F32),
        ],
        flops=2 * L * L * HL * 10,
        nbytes=L * HL * 20,
        trans=L * L * geo.NH // 2,
    )
    packs2_out = [sds((3, 2, 4, 64, 128), BF)] * 2 if geo.fast else [sds((D, 3 * D), BF)]
    res2 = call(
        functools.partial(qkv_back_kernel, geo),
        "qkv_back",
        [(meta, SM), (gq, VM), (h1, VM), (w_own, VM), (vec1, VM), (gain1, VM), (shift1, VM)]
        + [(p, VM) for p in pieces],
        [sds((2, BL, D), F32)] + [sds((2, BL, D), BF)] * (G - 1) + packs2_out + [sds((16, D), F32)],
        scratch=[pltpu.VMEM((D, 3 * HL), BF)],
        flops=4 * L * D * 3 * HL,
        nbytes=16 << 20,
    )
    ghs = res2[:G]
    packs2 = res2[G:-1]
    vec2 = res2[-1]
    gh_recv = [turn(ghs[G - d], d) for d in range(1, G)]
    tgrad, tgrad_send = call(
        functools.partial(last_kernel, geo),
        "norm_back",
        [(meta, SM), (gain1, VM), (g_resid, VM), (ghs[0], VM)]
        + [(r, VM) for r in gh_recv]
        + [(x0, VM), (x1, VM)],
        [sds((2, BL, D), BF), sds((BL, D), BF)],
        flops=T * D * 30,
        nbytes=8 << 20,
    )

    if geo.fast:
        def step_plane(parts, vec=None):
            a = [parts[0], plane(parts[1], 1, 0), plane(parts[2], 0, 1), plane(parts[3], 1, 1)]
            n = parts[0].shape[1]
            outs = [sds((n, 128), BF)] * 4
            if vec is not None:
                a += [vec, plane(vec, 1, 0), plane(vec, 0, 1), plane(vec, 1, 1)]
                outs += [sds(vec.shape, F32)]
            return call(
                functools.partial(plane_sum_kernel, vec is not None),
                "plane_sum",
                [(t, VM) for t in a],
                outs,
                nbytes=n * 128 * 40,
            )

        def step_line(parts, vec=None):
            a = [parts[0]] + [line(parts[d], d) for d in range(1, 4)]
            outs = [sds(parts[0].shape, BF)]
            if vec is not None:
                a += [vec] + [line(vec, d) for d in range(1, 4)]
                outs += [sds(vec.shape, F32)]
            return call(
                functools.partial(line_sum_kernel, vec is not None),
                "line_sum",
                [(t, VM) for t in a],
                outs,
                nbytes=parts[0].size * 10,
            )

        first = call(
            core_sum_kernel,
            "core_sum",
            [(packs[0], VM), (turn(packs[1], 1), VM)],
            [sds((4, 576, 128), BF)] * 4,
            nbytes=8 << 20,
        )
        first = step_plane(first)
        (first,) = step_line(first)
        first_other = plane(first, 1, 0)
        second = call(
            functools.partial(arrange_kernel, geo),
            "arrange",
            [(meta, SM), (packs2[0], VM), (turn(packs2[1], 1), VM), (vec2, VM), (turn(vec2, 1), VM)],
            [sds((4, 192, 128), BF)] * 4 + [sds(vec2.shape, F32)],
            nbytes=2 << 20,
        )
        second = step_plane(second[:4], second[4])
        second, vec = step_line(second[:4], second[4])
        second_other = plane(second, 1, 0)
        grads = call(
            finish_kernel,
            "finish",
            [(meta, SM), (first, VM), (first_other, VM), (second, VM), (second_other, VM)],
            [
                sds(qkv_weight.shape, F32),
                sds(mix_weight.shape, F32),
                sds(up_weight.shape, F32),
                sds(down_weight.shape, F32),
            ],
            nbytes=2 << 20,
        )
    else:
        def reduced(w):
            w = lax.psum_scatter(w, "col", scatter_dimension=1, tiled=True)
            w = lax.psum_scatter(w, "row", scatter_dimension=0, tiled=True)
            return lax.psum(w, "dp").astype(F32)

        grads = (reduced(packs2[0]), reduced(packs[2]), reduced(packs[0]), reduced(packs[1]))
        vec = lax.psum(vec2, ("dp", "col", "row"))

    def join(own, other):
        return lax.dynamic_update_slice(own, other[None], (1 - s, 0, 0))

    out_pair = jnp.where(s == 0, jnp.stack([out_own, swap_half(out_send)]), jnp.stack([swap_half(out_send), out_own]))
    tgrad = join(tgrad, swap_half(tgrad_send))
    return (
        out_pair,
        tgrad,
        *grads,
        vec[:8],
        vec[8 : 8 + FF // D].reshape(FF),
    )


def solution(mesh):
    return jax.shard_map(
        body,
        mesh=mesh,
        in_specs=(
            P(("dp", "row"), "col", None),
            P(("dp", "row"), None),
            P(),
            P(),
            P("row", "col"),
            P(),
            P(),
            P("row", "col"),
            P(),
            P(),
            P(),
            P("row", "col"),
            P(),
            P("row", "col"),
            P(),
            P(("dp", "row"), "col", None),
        ),
        out_specs=(
            P(("dp", "row"), "col", None),
            P(("dp", "row"), "col", None),
            P("row", "col"),
            P("row", "col"),
            P("row", "col"),
            P("row", "col"),
            P(),
            P(),
        ),
        check_vma=False,
    )
```

```python
import functools

import jax
import jax.numpy as jnp
from jax import lax
from jax.experimental import pallas as pl
from jax.experimental.pallas import tpu as pltpu
from jax.sharding import PartitionSpec as P

HEAD_DIM = 64
EPS = 1e-05
NEG = -1e30
LOG2E = 1.4426950408889634
PW = 128

BF = jnp.bfloat16
F32 = jnp.float32
VM = pl.BlockSpec(memory_space=pltpu.VMEM)
SM = pl.BlockSpec(memory_space=pltpu.SMEM)
HBM = pl.BlockSpec(memory_space=pl.ANY)
TQ = 256
TK = 256
FC = 512
RT = 256
KEEP_LB = ((0, 1, 4), (1, 4, 5))
SEND_LB = ((2, 3, 5), (0, 2, 3))


def sds(shape, dtype):
    return jax.ShapeDtypeStruct(shape, dtype)


def call(kernel, name, ins, outs, scratch=(), flops=0, nbytes=0, trans=0, **kw):
    return pl.pallas_call(
        kernel,
        name=name,
        out_shape=tuple(o for o in outs),
        in_specs=[spec for _, spec in ins],
        out_specs=tuple(VM for _ in outs),
        scratch_shapes=list(scratch),
        compiler_params=pltpu.CompilerParams(vmem_limit_bytes=60 * 1024 * 1024, **kw),
        cost_estimate=pl.CostEstimate(flops=flops, bytes_accessed=nbytes, transcendentals=trans),
    )(*[a for a, _ in ins])


def nt(a, b):
    return lax.dot_general(a, b, (((1,), (1,)), ((), ())), preferred_element_type=F32)


def nn(a, b):
    return lax.dot_general(a, b, (((1,), (0,)), ((), ())), preferred_element_type=F32)


def tn(a, b):
    return lax.dot_general(a, b, (((0,), (0,)), ((), ())), preferred_element_type=F32)


def al(value, unit):
    return pl.multiple_of(value, unit)


def normed(v):
    mean = jnp.mean(v, axis=-1, keepdims=True)
    center = v - mean
    rstd = lax.rsqrt(jnp.mean(center * center, axis=-1, keepdims=True) + EPS)
    return center * rstd, rstd


class Geo:
    def __init__(self, dp, col, row, block_len, width, hidden):
        self.dp, self.C, self.R = dp, col, row
        self.G = col // 2
        self.BL = block_len
        self.L = block_len * col
        self.T = 2 * block_len
        self.D = width
        self.FF = hidden
        self.HL = width // self.G
        self.NP = self.HL // PW
        self.TQ = min(512, block_len)
        self.fast = (
            dp == 2 and col == 4 and row == 4 and width == 512 and hidden == 2048 and block_len % 256 == 0
        )

    def where(self, meta):
        col = meta[1]
        return col // self.G, col % self.G

    def block(self, s, g, e, d):
        half = s if e == 0 else 1 - s
        return half * self.G + lax.rem(g - d + self.G, self.G)


def norm_kernel(geo, meta, doc, gain, shift, *refs):
    s, g = geo.where(meta)
    pieces, (out, segk, segq) = refs[:-3], refs[-3:]
    fill_segments(geo, doc_ends(doc, s), segk, segq)
    for e in range(2):
        for d in range(geo.G):
            src = pieces[e * geo.G + d]
            base = geo.block(s, g, e, d) * geo.BL

            def step(i, carry):
                v = src[pl.ds(al(i * 128, 128), 128), :].astype(F32)
                xhat, _ = normed(v)
                out[pl.ds(al(base + i * 128, 128), 128), :] = (xhat * gain[...] + shift[...]).astype(BF)
                return carry

            lax.fori_loop(0, geo.BL // 128, step, 0, unroll=2)


def qkv_kernel(geo, meta, h1, bias, *refs):
    s, g = geo.where(meta)
    HL, D, NP = geo.HL, geo.D, geo.NP
    outs = refs[-(4 * NP) - 2 : -2] if geo.fast else refs[-(4 * NP) :]
    if geo.fast:
        pieces, (wscr, sem) = refs[:8], refs[-2:]
        x, z = meta[0], meta[2]
        y, c = meta[1] // 2, meta[1] % 2
        copies = []
        for quad in range(4):
            yy = y if quad < 2 else 1 - y
            hh = x if quad % 2 == 0 else 1 - x
            for cc in range(2):
                cp = c if cc == 0 else 1 - c
                for d in range(4):
                    zz = lax.rem(z - d + 4, 4)
                    copies.append(
                        pltpu.make_async_copy(
                            pieces[quad * 2 + cc].at[d],
                            wscr.at[
                                pl.ds(al(zz * 128 + hh * 64, 64), 64),
                                pl.ds(al((2 * yy + cp) * 384, 128), 384),
                            ],
                            sem,
                        )
                    )
        for cpy in copies:
            cpy.start()
        for cpy in copies:
            cpy.wait()
    else:
        wscr = refs[0]

    def cols(part, p):
        return pl.ds(al(part * D + g * HL + p * PW, 128), PW)

    for p in range(NP):
        for part in range(3):
            outs[3 * NP + p][:, part * PW : (part + 1) * PW] = wscr[:, cols(part, p)]

    def step(i, carry):
        rows = pl.ds(al(i * 256, 256), 256)
        a = h1[rows, :]
        for p in range(NP):
            res = nn(a, outs[3 * NP + p][...])
            for part in range(3):
                outs[part * NP + p][rows, :] = (
                    res[:, part * PW : (part + 1) * PW] + bias[:, cols(part, p)]
                ).astype(BF)
        return carry

    lax.fori_loop(0, geo.L // 256, step, 0)


def doc_ends(doc, s):
    ends, total = [], 0
    for i in range(8):
        total = total + doc[s, i]
        ends.append(total)
    return ends


def span_start(ends, t):
    best = 0
    for e in ends:
        best = jnp.where(e <= t, e, best)
    return best


def span_end(ends, t, full):
    best = full
    for e in reversed(ends):
        best = jnp.where(e > t, e, best)
    return best


def fill_segments(geo, ends, segk, segq):
    def step(i, carry):
        rows = lax.broadcasted_iota(jnp.int32, (TK, 128), 0) + i * TK
        cols = lax.broadcasted_iota(jnp.int32, (8, TQ), 1) + i * TQ
        a = jnp.zeros((TK, 128), jnp.int32)
        b = jnp.zeros((8, TQ), jnp.int32)
        for e in ends:
            a += (rows >= e).astype(jnp.int32)
            b += (cols >= e).astype(jnp.int32)
        segk[pl.ds(al(i * TK, TK), TK), :] = a
        segq[:, pl.ds(al(i * TQ, TQ), TQ)] = b
        return carry

    lax.fori_loop(0, geo.L // TK, step, 0)


def mask_bias(segk, segq, k0, q0, tq):
    a = segk[pl.ds(k0, TK), :]
    b = segq[0:1, pl.ds(q0, tq)]
    same = jnp.concatenate([a] * (tq // 128), axis=1) == b
    return jnp.where(same, 0.0, NEG)


def head_mask(h, rows):
    lane = lax.broadcasted_iota(jnp.int32, (rows, PW), 1)
    return (lane // HEAD_DIM) == h


def ranges(first, last, one, lo, hi, tile):
    a = jnp.where(one, jnp.minimum((first + tile - 1) // tile, hi), hi)
    b = jnp.where(one, jnp.minimum(jnp.maximum(last // tile, a), hi), hi)
    return ((lo, a, True), (a, b, False), (b, hi, True))


HR = HEAD_DIM + 16


def attn_kernel(geo, dlist, meta, doc, segk, segq, *refs):
    G, NP, L, BL, TQF = geo.G, geo.NP, geo.L, geo.BL, geo.TQ
    q, k, v, refs = refs[:NP], refs[NP : 2 * NP], refs[2 * NP : 3 * NP], refs[3 * NP :]
    nd = len(dlist)
    outs, lses = refs[: nd * NP], refs[nd * NP : nd * NP + nd]
    vT, acc, sc = refs[nd * NP + nd :]
    s, g = geo.where(meta)
    ends = doc_ends(doc, s)
    heads = [(p, h) for p in range(NP) for h in range(2)]

    def flip(i, carry):
        rows = pl.ds(al(i * TK, TK), TK)
        for p in range(NP):
            t = jnp.transpose(v[p][rows, :])
            for h in range(2):
                b = (2 * p + h) * HR
                vT[b : b + HEAD_DIM, rows] = t[h * HEAD_DIM : (h + 1) * HEAD_DIM, :]
                vT[b + HEAD_DIM : b + HR, rows] = jnp.ones((16, TK), BF)
        return carry

    lax.fori_loop(0, L // TK, flip, 0)

    for di, d in enumerate(dlist):

        def q_step(i, carry):
            e = i // (BL // TQF)
            off = al(lax.rem(i, BL // TQF) * TQF, TQF)
            half = jnp.where(e == 0, s, 1 - s)
            q0 = al((half * G + lax.rem(g - d + G, G)) * BL + off, TQF)
            first, last = span_start(ends, q0), span_end(ends, q0 + TQF - 1, L)
            one = first == span_start(ends, q0 + TQF - 1)
            klo = first // TK
            khi = (last + TK - 1) // TK
            qm = []
            for p, h in heads:
                qt = q[p][pl.ds(q0, TQF), :] * jnp.asarray(HEAD_DIM ** (-0.5), BF)
                qm.append(jnp.where(head_mask(h, TQF), qt, jnp.zeros_like(qt)))
            acc[...] = jnp.zeros_like(acc)

            def scores(masked, j, ms):
                k0 = al(j * TK, TK)
                if masked:
                    bias = mask_bias(segk, segq, k0, q0, TQF)
                out = []
                for n, (p, h) in enumerate(heads):
                    st = nt(k[p][pl.ds(k0, TK), :], qm[n])
                    if masked:
                        st = st + bias
                    sc[n, pl.ds(k0, TK), :] = st
                    out.append(jnp.maximum(ms[n], jnp.max(st.reshape(TK // 8, 8, TQF), axis=0)))
                return tuple(out)

            ms = tuple(jnp.full((8, TQF), -3e38, F32) for _ in heads)
            for lo, hi, masked in ranges(first, last, one, klo, khi, TK):
                ms = lax.fori_loop(lo, hi, functools.partial(scores, masked), ms)
            ms = [jnp.max(m, axis=0, keepdims=True) for m in ms]
            ml = [m * LOG2E for m in ms]

            def values(j, c2):
                k0 = al(j * TK, TK)
                for n in range(len(heads)):
                    pr = jnp.exp2(sc[n, pl.ds(k0, TK), :] * LOG2E - ml[n])
                    hs = slice(n * HR, (n + 1) * HR)
                    acc[hs, :] += nn(vT[hs, pl.ds(k0, TK)], pr.astype(BF))
                return c2

            lax.fori_loop(klo, khi, values, 0)
            for p in range(NP):
                parts = []
                for n in (2 * p, 2 * p + 1):
                    ls = acc[n * HR + HEAD_DIM : n * HR + HEAD_DIM + 1, :]
                    parts.append(acc[n * HR : n * HR + HEAD_DIM, :] * (1.0 / ls))
                    lses[di][e, n : n + 1, pl.ds(off, TQF)] = ms[n] + jnp.log(ls)
                res = jnp.transpose(jnp.concatenate(parts, axis=0)).astype(BF)
                outs[di * NP + p][e, pl.ds(off, TQF), :] = res
            return carry

        lax.fori_loop(0, 2 * BL // TQF, q_step, 0)


def attn_back_kernel(geo, p, meta, doc, segk, segq, q, k, v, *refs):
    G, L, BL = geo.G, geo.L, geo.BL
    lses, mixed, grads = refs[:G], refs[G : 2 * G], refs[2 * G : 3 * G]
    out = refs[3 * G]
    qm, gm, kT, dqT, delta, lse, dk, dv = refs[3 * G + 1 :]
    s, g = geo.where(meta)
    ends = doc_ends(doc, s)
    scale = HEAD_DIM ** (-0.5)
    for e in range(2):
        for d in range(G):
            base = geo.block(s, g, e, d) * BL

            def load(i, carry):
                src = pl.ds(al(i * 256, 256), 256)
                dst = pl.ds(al(base + i * 256, 256), 256)
                gt = grads[d][e, src, :]
                zero = jnp.zeros_like(gt)
                prod = jnp.transpose(gt.astype(F32) * mixed[d][e, src, :].astype(F32))
                qt = q[dst, :] * jnp.asarray(scale, BF)
                for h in range(2):
                    hs = slice(h * HEAD_DIM, (h + 1) * HEAD_DIM)
                    keep = head_mask(h, 256)
                    gm[h, dst, :] = jnp.where(keep, gt, zero)
                    qm[h, dst, :] = jnp.where(keep, qt, zero)
                    delta[h : h + 1, dst] = jnp.sum(prod[hs, :], axis=0, keepdims=True)
                lse[:, dst] = lses[d][e, :, src]
                kT[:, dst] = jnp.transpose(k[dst, :])
                dqT[:, dst] = jnp.zeros((PW, 256), F32)
                return carry

            lax.fori_loop(0, BL // 256, load, 0)

    def k_step(j, carry):
        k0 = al(j * TK, TK)
        first, last = span_start(ends, k0), span_end(ends, k0 + TK - 1, L)
        one = first == span_start(ends, k0 + TK - 1)
        qlo = first // TQ
        qhi = (last + TQ - 1) // TQ
        kt = k[pl.ds(k0, TK), :]
        vt = v[pl.ds(k0, TK), :]
        dk[...] = jnp.zeros_like(dk)
        dv[...] = jnp.zeros_like(dv)

        def q_step(masked, i, c2):
            q0 = al(i * TQ, TQ)
            qs = pl.ds(q0, TQ)
            if masked:
                bias = mask_bias(segk, segq, k0, q0, TQ)
            for h in range(2):
                hs = slice(h * HEAD_DIM, (h + 1) * HEAD_DIM)
                qh, gh = qm[h, qs, :], gm[h, qs, :]
                n = 2 * p + h
                st = nt(kt, qh) - lse[n : n + 1, qs]
                if masked:
                    st = st + bias
                pr = jnp.exp(st)
                ds = (pr * (nt(vt, gh) - delta[h : h + 1, qs])).astype(BF)
                dv[...] += nn(pr.astype(BF), gh)
                dk[...] += nn(ds, qh)
                dqT[hs, qs] += nn(kT[hs, pl.ds(k0, TK)], ds)
            return c2

        for lo, hi, masked in ranges(first, last, one, qlo, qhi, TQ):
            lax.fori_loop(lo, hi, functools.partial(q_step, masked), 0)
        out[pl.ds(k0, TK), PW : 2 * PW] = dk[...].astype(BF)
        out[pl.ds(k0, TK), 2 * PW : 3 * PW] = dv[...].astype(BF)
        return carry

    lax.fori_loop(0, L // TK, k_step, 0)

    def last_step(i, carry):
        rows = pl.ds(al(i * TQ, TQ), TQ)
        out[rows, 0:PW] = (jnp.transpose(dqT[:, rows]) * scale).astype(BF)
        return carry

    lax.fori_loop(0, L // TQ, last_step, 0)


def attend_call(geo, dlist, meta, doc, segs, q, k, v):
    NP, L, BL, nd = geo.NP, geo.L, geo.BL, len(dlist)
    share = nd / geo.G
    res = call(
        functools.partial(attn_kernel, geo, dlist),
        "attend",
        [(meta, SM), (doc, SM), (segs[0], VM), (segs[1], VM)] + [(t, VM) for t in (*q, *k, *v)],
        [sds((2, BL, PW), BF)] * (nd * NP) + [sds((2, 8, BL), F32)] * nd,
        scratch=[
            pltpu.VMEM((2 * NP * HR, L), BF),
            pltpu.VMEM((2 * NP * HR, geo.TQ), F32),
            pltpu.VMEM((2 * NP, L, geo.TQ), F32),
        ],
        flops=int(2 * L * L * geo.HL * 4 * share),
        nbytes=L * geo.HL * 8,
        trans=int(L * L * NP * share),
    )
    mixed = [res[i * NP : (i + 1) * NP] for i in range(nd)]
    return mixed, res[nd * NP :]


def attend_back_call(geo, p, meta, doc, segs, q, k, v, lses, mixed, grads):
    L = geo.L
    return call(
        functools.partial(attn_back_kernel, geo, p),
        "attend_back",
        [(meta, SM), (doc, SM), (segs[0], VM), (segs[1], VM), (q, VM), (k, VM), (v, VM)]
        + [(t, VM) for t in (*lses, *mixed, *grads)],
        [sds((L, 3 * PW), BF)],
        scratch=[
            pltpu.VMEM((2, L, PW), BF),
            pltpu.VMEM((2, L, PW), BF),
            pltpu.VMEM((PW, L), BF),
            pltpu.VMEM((PW, L), F32),
            pltpu.VMEM((8, L), F32),
            pltpu.VMEM((8, L), F32),
            pltpu.VMEM((TK, PW), F32),
            pltpu.VMEM((TK, PW), F32),
        ],
        flops=2 * L * L * PW * 10,
        nbytes=L * PW * 20,
        trans=L * L,
    )[0]


def gelu_parts(u):
    phi = 0.5 + 0.5 * lax.erf(u * (2.0 ** -0.5))
    pdf = jnp.exp(-0.5 * (u * u)) * 0.3989422804014327
    return phi, pdf


def ffn_kernel(geo, meta, *refs):
    G, HL, D, FF, BL, T, NP = geo.G, geo.HL, geo.D, geo.FF, geo.BL, geo.T, geo.NP
    s, g = geo.where(meta)
    pairs = [(d, p) for d in range(G) for p in range(NP)]
    x0, x1, cot, cot1, mixb, gain, shift, upb, downb = refs[:9]
    refs = refs[9:]
    mixed, refs = refs[: G * NP], refs[G * NP :]
    nw = 8 if geo.fast else 3
    wts, refs = refs[:nw], refs[nw:]
    out_own, out_send, g_resid = refs[:3]
    refs = refs[3:]
    gmix, refs = refs[: G * NP], refs[G * NP :]
    ng = 2 if geo.fast else 3
    packs, refs = refs[:ng], refs[ng:]
    vec, refs = refs[0], refs[1:]
    resid, h2, ffn, gh2, act_s, gu_s, ga_s, mg = refs[:8]
    refs = refs[8:]
    if geo.fast:
        wo, wu, wd, wg, sems = refs
        x, z = meta[0], meta[2]
        y, c = meta[1] // 2, meta[1] % 2
        groups = [[], [], []]
        for quad in range(4):
            yy = y if quad < 2 else 1 - y
            hh = x if quad % 2 == 0 else 1 - x
            for cc in range(2):
                cl = 2 * yy + (c if cc == 0 else 1 - c)
                src = wts[quad * 2 + cc]
                for d in range(4):
                    zz = lax.rem(z - d + 4, 4)
                    groups[0].append(
                        pltpu.make_async_copy(
                            src.at[d, pl.ds(512, 64), :],
                            wo.at[pl.ds(al(zz * 128 + hh * 64, 64), 64), pl.ds(al(cl * 128, 128), 128)],
                            sems.at[0],
                        )
                    )
                    for b in range(4):
                        groups[1].append(
                            pltpu.make_async_copy(
                                src.at[d, pl.ds(b * 64, 64), :],
                                wu.at[
                                    pl.ds(al(zz * 128 + hh * 64, 64), 64),
                                    pl.ds(al(cl * 512 + b * 128, 128), 128),
                                ],
                                sems.at[1],
                            )
                        )
                    groups[2].append(
                        pltpu.make_async_copy(
                            src.at[d, pl.ds(256, 256), :],
                            wd.at[pl.ds(al(zz * 512 + hh * 256, 256), 256), pl.ds(al(cl * 128, 128), 128)],
                            sems.at[2],
                        )
                    )
        for group in groups:
            for cpy in group:
                cpy.start()
        for cpy in groups[0]:
            cpy.wait()
    else:
        wo, wu, wd = wts
        (wg,) = refs

    zrow = jnp.zeros((1, D), F32)
    vec[...] = jnp.zeros_like(vec)

    for e in range(2):
        xe = x0 if e == 0 else x1
        ce = cot if e == 0 else cot1

        def first(i, carry):
            rows = pl.ds(al(i * RT, RT), RT)
            to = pl.ds(al(e * BL + i * RT, RT), RT)
            r = xe[rows, :].astype(F32) + mixb[...]
            for n, (d, p) in enumerate(pairs):
                gp = lax.rem(g - d + G, G)
                r = r + nn(mixed[n][e, rows, :], wo[pl.ds(al(gp * HL + p * PW, 128), PW), :])
            resid[to, :] = r
            xhat, _ = normed(r)
            h2[to, :] = (xhat * gain[...] + shift[...]).astype(BF)
            ffn[to, :] = jnp.zeros((RT, D), F32)
            gh2[to, :] = jnp.zeros((RT, D), F32)
            return carry

        lax.fori_loop(0, BL // RT, first, 0)
    ga_s[0:BL, :] = cot[...]
    ga_s[BL:T, :] = cot1[...]
    if geo.fast:
        for group in groups[1:]:
            for cpy in group:
                cpy.wait()

    def chunk(f, carry):
        f0 = al(f * FC, FC)
        fs = pl.ds(f0, FC)

        def rows_step(i, hs):
            rows = pl.ds(al(i * RT, RT), RT)
            u = nn(h2[rows, :], wu[:, fs]) + upb[:, fs]
            phi, pdf = gelu_parts(u)
            act = (u * phi).astype(BF)
            gu = (nt(ga_s[rows, :], wd[fs, :]) * (phi + u * pdf)).astype(BF)
            act_s[rows, :] = act
            gu_s[rows, :] = gu
            ffn[rows, :] += nn(act, wd[fs, :])
            gh2[rows, :] += nt(gu, wu[:, fs])
            return hs + jnp.sum(gu.astype(F32), axis=0, keepdims=True)

        hsum = lax.fori_loop(0, T // RT, rows_step, jnp.zeros((1, FC), F32))
        per = D // FC
        vec[pl.ds(8 + f // per, 1), pl.ds(al(lax.rem(f, per) * FC, 128), FC)] = hsum
        dn = tn(act_s[...], ga_s[...])
        if geo.fast:
            wg[...] = dn.astype(BF)
            zr = lax.rem(f - z + 4, 4)
            for cr in range(2):
                for yr in range(2):
                    cl = 2 * (y if yr == 0 else 1 - y) + (c if cr == 0 else 1 - c)
                    for hr in range(2):
                        hh = x if hr == 0 else 1 - x
                        packs[cr][yr * 2 + hr, zr, 256:512, :] = wg[
                            pl.ds(al(hh * 256, 256), 256), pl.ds(al(cl * 128, 128), 128)
                        ]
        else:
            packs[1][fs, :] = dn.astype(BF)
        up = tn(h2[...], gu_s[...])
        if geo.fast:
            wg[...] = up.astype(BF)
            fy, fcr = f // 2, lax.rem(f, 2)
            yr = jnp.where(fy == y, 0, 1)
            for cr in range(2):
                @pl.when((fcr == c) if cr == 0 else (fcr != c))
                def _():
                    for hr in range(2):
                        hh = x if hr == 0 else 1 - x
                        for k in range(4):
                            zz = lax.rem(z + k, 4)
                            for b in range(4):
                                packs[cr][yr * 2 + hr, k, b * 64 : b * 64 + 64, :] = wg[
                                    pl.ds(al(zz * 128 + hh * 64, 64), 64), b * 128 : b * 128 + 128
                                ]
        else:
            packs[0][:, fs] = up.astype(BF)
        return carry

    lax.fori_loop(0, FF // FC, chunk, 0)

    sums = (zrow, zrow, zrow, zrow)
    for e in range(2):
        ce = cot if e == 0 else cot1
        oe = out_own if e == 0 else out_send

        def back(i, carry):
            mb, fg, fs_, db = carry
            rows = pl.ds(al(i * RT, RT), RT)
            to = pl.ds(al(e * BL + i * RT, RT), RT)
            r = resid[to, :]
            oe[rows, :] = (r + ffn[to, :] + downb[...]).astype(BF)
            xhat, rstd = normed(r)
            gh = gh2[to, :]
            ct = ce[rows, :].astype(F32)
            gx = gh * gain[...]
            gr = ct + rstd * (
                gx
                - jnp.mean(gx, axis=-1, keepdims=True)
                - xhat * jnp.mean(gx * xhat, axis=-1, keepdims=True)
            )
            g_resid[to, :] = gr
            ga = gr.astype(BF)
            gu_s[to, 0:D] = ga
            for n, (d, p) in enumerate(pairs):
                gp = lax.rem(g + d, G)
                gmix[n][e, rows, :] = nt(ga, wo[pl.ds(al(gp * HL + p * PW, 128), PW), :]).astype(BF)
            return (
                mb + jnp.sum(ga.astype(F32), axis=0, keepdims=True),
                fg + jnp.sum(gh * xhat, axis=0, keepdims=True),
                fs_ + jnp.sum(gh, axis=0, keepdims=True),
                db + jnp.sum(ct, axis=0, keepdims=True),
            )

        sums = lax.fori_loop(0, BL // RT, back, sums)
    for i in range(4):
        vec[4 + i : 5 + i, :] = sums[i]
    for n, (d, p) in enumerate(pairs):
        gp = lax.rem(g - d + G, G)
        part = tn(mixed[n][0], gu_s[0:BL, 0:D]) + tn(mixed[n][1], gu_s[BL:T, 0:D])
        mg[pl.ds(al(gp * HL + p * PW, 128), PW), :] = part.astype(BF)
    if geo.fast:
        for cr in range(2):
            for yr in range(2):
                cl = 2 * (y if yr == 0 else 1 - y) + (c if cr == 0 else 1 - c)
                for hr in range(2):
                    hh = x if hr == 0 else 1 - x
                    for k in range(4):
                        zz = lax.rem(z + k, 4)
                        packs[cr][yr * 2 + hr, k, 512:576, :] = mg[
                            pl.ds(al(zz * 128 + hh * 64, 64), 64), pl.ds(al(cl * 128, 128), 128)
                        ]
    else:
        packs[2][...] = mg[...]


def wgrad_kernel(geo, meta, h1, *refs):
    G, HL, D, NP = geo.G, geo.HL, geo.D, geo.NP
    s, g = geo.where(meta)
    gq, refs = refs[:NP], refs[NP:]
    packs, wg = refs[:-1], refs[-1]
    for p in range(NP):
        wg[:, p * 3 * PW : (p + 1) * 3 * PW] = tn(h1[...], gq[p][...]).astype(BF)
    if geo.fast:
        x, z, c = meta[0], meta[2], meta[1] % 2
        for cr, table in ((0, KEEP_LB), (1, SEND_LB)):
            for b in range(3):
                lb = [(t[b] % 2) * 3 + t[b] // 2 for t in table]
                at = jnp.where(c == 0, lb[0], lb[1])
                for hr in range(2):
                    hh = x if hr == 0 else 1 - x
                    for k in range(4):
                        zz = lax.rem(z + k, 4)
                        packs[cr][b, hr, k] = wg[
                            pl.ds(al(zz * 128 + hh * 64, 64), 64), pl.ds(al(at * 128, 128), 128)
                        ]
    else:
        packs[0][...] = jnp.zeros_like(packs[0])
        for p in range(NP):
            for part in range(3):
                packs[0][:, pl.ds(al(part * D + g * HL + p * PW, 128), PW)] = wg[
                    :, (3 * p + part) * PW : (3 * p + part + 1) * PW
                ]


def qkv_back_kernel(geo, meta, vec_in, *refs):
    G, HL, D, BL, NP = geo.G, geo.HL, geo.D, geo.BL, geo.NP
    s, g = geo.where(meta)
    gq, w, refs = refs[:NP], refs[NP : 2 * NP], refs[2 * NP :]
    pieces, refs = refs[: 2 * G], refs[2 * G :]
    ghs, vec = refs[:G], refs[G]
    vec[...] = vec_in[...]
    zrow = jnp.zeros((1, D), F32)
    zh = jnp.zeros((1, PW), F32)
    sums = (zrow, zrow) + (zh,) * (2 * NP)
    for e in range(2):
        for d in range(G):
            base = geo.block(s, g, e, d) * BL
            src = pieces[e * G + d]

            def step(i, carry):
                rows = pl.ds(al(i * RT, RT), RT)
                at = pl.ds(al(base + i * RT, RT), RT)
                xhat, _ = normed(src[rows, :].astype(F32))
                gts = [t[at, :] for t in gq]
                gh = nt(gts[0], w[0][...])
                for p in range(1, NP):
                    gh = gh + nt(gts[p], w[p][...])
                ghs[d][e, rows, :] = gh.astype(ghs[d].dtype)
                new = [
                    carry[0] + jnp.sum(gh * xhat, axis=0, keepdims=True),
                    carry[1] + jnp.sum(gh, axis=0, keepdims=True),
                ]
                for p in range(NP):
                    for n, part in enumerate((0, 2)):
                        cut = gts[p][:, part * PW : (part + 1) * PW].astype(F32)
                        new.append(carry[2 + 2 * p + n] + jnp.sum(cut, axis=0, keepdims=True))
                return tuple(new)

            sums = lax.fori_loop(0, BL // RT, step, sums)
    vec[0:1, :] = sums[0]
    vec[1:2, :] = sums[1]
    for p in range(NP):
        cols = pl.ds(al(g * HL + p * PW, 128), PW)
        vec[2:3, cols] = sums[2 + 2 * p]
        vec[3:4, cols] = sums[3 + 2 * p]


def last_kernel(geo, meta, gain, vec, vrecv, g_resid, gh, *refs):
    G, D, BL = geo.G, geo.D, geo.BL
    s, _ = geo.where(meta)
    refs, vout = refs[:-1], refs[-1]
    vout[...] = vec[...] + vrecv[...]
    recv, refs = refs[: G - 1], refs[G - 1 :]
    x0, x1, out, send = refs
    for e in range(2):
        xe = x0 if e == 0 else x1

        def step(i, carry):
            rows = pl.ds(al(i * RT, RT), RT)
            to = pl.ds(al(e * BL + i * RT, RT), RT)
            xhat, rstd = normed(xe[rows, :].astype(F32))
            total = gh[e, rows, :]
            for r in recv:
                total = total + r[e, rows, :].astype(F32)
            gx = total * gain[...]
            res = g_resid[to, :] + rstd * (
                gx
                - jnp.mean(gx, axis=-1, keepdims=True)
                - xhat * jnp.mean(gx * xhat, axis=-1, keepdims=True)
            )
            if e == 0:
                out[s, rows, :] = res.astype(BF)
            else:
                send[rows, :] = res.astype(BF)
            return carry

        lax.fori_loop(0, BL // RT, step, 0)


def core_sum_kernel(own, recv, *outs):
    for q in range(4):
        outs[q][...] = (own[q].astype(F32) + recv[q].astype(F32)).astype(BF)


def arrange_kernel(geo, meta, keep, recv, *outs):
    y, c = meta[1] // 2, meta[1] % 2
    for cs in range(2):
        mine = sorted((lb // 2) * 4 + 2 * cs + lb % 2 for lb in KEEP_LB[cs])
        theirs = sorted((lb // 2) * 4 + 2 * (1 - cs) + lb % 2 for lb in SEND_LB[1 - cs])
        for ys in range(2):
            @pl.when(jnp.logical_and(c == cs, y == ys))
            def _():
                for yr in range(2):
                    first = 3 * (2 * (ys ^ yr) + cs)
                    for o in range(3):
                        b = first + o
                        src, slot = (keep, mine.index(b)) if b in mine else (recv, theirs.index(b))
                        for hr in range(2):
                            outs[yr * 2 + hr][:, o * 64 : o * 64 + 64, :] = src[slot, hr]


def plane_sum_kernel(has_vec, a, b, c, d, *refs):
    if has_vec:
        va, vb, vc, vd = refs[:4]
        refs = refs[4:]
        refs[4][...] = (va[...] + vb[...]) + (vc[...] + vd[...])
    for k in range(4):
        refs[k][...] = (
            (a[k].astype(F32) + b[k].astype(F32)) + (c[k].astype(F32) + d[k].astype(F32))
        ).astype(BF)


def line_sum_kernel(has_vec, a, b, c, d, *refs):
    if has_vec:
        va, vb, vc, vd = refs[:4]
        refs = refs[4:]
        refs[1][...] = (va[...] + vc[...]) + (vb[...] + vd[...])
    refs[0][...] = (
        (a[...].astype(F32) + b[...].astype(F32)) + (c[...].astype(F32) + d[...].astype(F32))
    ).astype(BF)


def finish_kernel(meta, r, o, mix, up, down):
    x = meta[0]
    for src, h in ((r, x), (o, 1 - x)):
        rows = pl.ds(al(h * 64, 64), 64)
        for b in range(4):
            up[rows, b * 128 : b * 128 + 128] = src[b * 64 : b * 64 + 64, :].astype(F32)
        down[pl.ds(al(h * 256, 256), 256), :] = src[256:512, :].astype(F32)
        mix[rows, :] = src[512:576, :].astype(F32)


def finish_qkv_kernel(meta, r, o, qkv):
    x = meta[0]
    for src, h in ((r, x), (o, 1 - x)):
        for b in range(3):
            qkv[pl.ds(al(h * 64, 64), 64), b * 128 : b * 128 + 128] = src[b * 64 : b * 64 + 64, :].astype(F32)


def pack_kernel(meta, qkv, mix, up, down, first, rest):
    h = meta[0]
    rows = pl.ds(al(h * 64, 64), 64)
    first[...] = qkv[rows, :].astype(BF)
    for b in range(4):
        rest[b * 64 : b * 64 + 64, :] = up[rows, b * 128 : b * 128 + 128].astype(BF)
    rest[256:512, :] = down[pl.ds(al(h * 256, 256), 256), :].astype(BF)
    rest[512:576, :] = mix[rows, :].astype(BF)


def body(
    tokens,
    doc_lengths,
    norm_gain,
    norm_shift,
    qkv_weight,
    query_bias,
    value_bias,
    mix_weight,
    mix_bias,
    ffn_gain,
    ffn_shift,
    up_weight,
    up_bias,
    down_weight,
    down_bias,
    cotangent,
):
    DP, C, R = lax.axis_size("dp"), lax.axis_size("col"), lax.axis_size("row")
    _, BL, D = tokens.shape
    FF = up_bias.shape[0]
    geo = Geo(DP, C, R, BL, D, FF)
    G, HL, L, T = geo.G, geo.HL, geo.L, geo.T
    ix, ic, iz = lax.axis_index("dp"), lax.axis_index("col"), lax.axis_index("row")
    s = ic // G
    meta = jnp.stack([ix, ic, iz]).astype(jnp.int32)

    def swap_half(v):
        return lax.ppermute(v, "col", [(i, (i + G) % C) for i in range(C)])

    def turn(v, d):
        return lax.ppermute(v, "col", [(i, (i // G) * G + (i % G + d) % G) for i in range(C)])

    def plane(v, dx, dy):
        pairs = [
            (i * C + j, ((i + dx) % 2) * C + (j + dy * G) % C) for i in range(2) for j in range(C)
        ]
        return lax.ppermute(v, ("dp", "col"), pairs)

    def line(v, d):
        return lax.ppermute(v, "row", [(i, (i + d) % R) for i in range(R)])

    def row2(v):
        return v.reshape(1, v.shape[0])

    def pick(v, i):
        return lax.dynamic_index_in_dim(v, i, 0, keepdims=False)

    def after(v, dep):
        return lax.optimization_barrier((v, dep))[0]

    NP = geo.NP
    if geo.fast:
        half_qkv, half_rest = call(
            pack_kernel,
            "pack",
            [(meta, SM), (qkv_weight, VM), (mix_weight, VM), (up_weight, VM), (down_weight, VM)],
            [sds((64, 384), BF), sds((576, 128), BF)],
            nbytes=2 << 20,
        )

        def lines(v):
            return [v] + [line(v, d) for d in range(1, 4)]

        def quads(v):
            return [v, plane(v, 1, 0), plane(v, 0, 1), plane(v, 1, 1)]

        lines_qkv = lines(half_qkv)
        x0 = pick(tokens, s)
        x1 = swap_half(pick(after(tokens, half_qkv), 1 - s))
        lines_rest = lines(half_rest)
        quads_qkv = quads(jnp.stack(lines_qkv))
        w_qkv = [t for q in quads_qkv for t in (q, turn(q, 1))]
        quads_rest = quads(jnp.stack(after(tuple(lines_rest), w_qkv[1])))
    else:
        x0 = pick(tokens, s)
        x1 = swap_half(pick(tokens, 1 - s))

        def whole(w):
            w = lax.all_gather(w.astype(BF), "row", axis=0, tiled=True)
            return lax.all_gather(w, "col", axis=1, tiled=True)

        w_qkv = [whole(qkv_weight)]
        w_rest = [whole(mix_weight), whole(up_weight), whole(down_weight)]
    pieces = [x0] + [turn(x0, d) for d in range(1, G)]
    pieces += [x1] + [turn(x1, d) for d in range(1, G)]
    gain1, shift1 = row2(norm_gain), row2(norm_shift)
    h1, segk, segq = call(
        functools.partial(norm_kernel, geo),
        "norm_one",
        [(meta, SM), (doc_lengths, SM), (gain1, VM), (shift1, VM)] + [(p, VM) for p in pieces],
        [sds((L, D), BF), sds((L, 128), jnp.int32), sds((8, L), jnp.int32)],
        flops=L * D * 10,
        nbytes=L * D * 4,
    )
    segs = (segk, segq)
    bias = row2(jnp.concatenate([query_bias, jnp.zeros_like(query_bias), value_bias]))
    wspec = HBM if geo.fast else VM
    res = call(
        functools.partial(qkv_kernel, geo),
        "qkv",
        [(meta, SM), (h1, VM), (bias, VM)] + [(w, wspec) for w in w_qkv],
        [sds((L, PW), BF)] * (3 * NP) + [sds((D, 3 * PW), BF)] * NP,
        scratch=[pltpu.VMEM((D, 3 * D), BF), pltpu.SemaphoreType.DMA(())] if geo.fast else [],
        flops=2 * L * D * 3 * HL,
        nbytes=L * D * 2 + L * HL * 6 + D * D * 6,
    )
    q, k, v, w_own = (res[n * NP : (n + 1) * NP] for n in range(4))
    cot0 = pick(cotangent, s)
    cot1 = swap_half(pick(cotangent, 1 - s))
    far, lse_far = attend_call(geo, tuple(range(1, G)), meta, doc_lengths, segs, q, k, v)
    q_own = list(after(tuple(q), far[0][0]))
    if geo.fast:
        quads_rest = after(tuple(quads_rest), far[0][0])
        w_rest = [t for u in quads_rest for t in (u, turn(u, 1))]
    own, lse_own = attend_call(geo, (0,), meta, doc_lengths, segs, q_own, k, v)
    made = [own[0]] + list(far)
    lses = list(lse_own) + list(lse_far)
    mixed = [t for t in made[0]]
    for d in range(1, G):
        mixed += [turn(t, d) for t in made[G - d]]
    packs_out = (
        [sds((4, 4, 576, 128), BF)] * 2
        if geo.fast
        else [sds((D, FF), BF), sds((FF, D), BF), sds((D, D), BF)]
    )
    weights_scr = (
        [
            pltpu.VMEM((D, D), BF),
            pltpu.VMEM((D, FF), BF),
            pltpu.VMEM((FF, D), BF),
            pltpu.VMEM((FC, FC), BF),
            pltpu.SemaphoreType.DMA((3,)),
        ]
        if geo.fast
        else [pltpu.VMEM((8, 128), BF)]
    )
    res = call(
        functools.partial(ffn_kernel, geo),
        "ffn",
        [(meta, SM), (x0, VM), (x1, VM), (cot0, VM), (cot1, VM)]
        + [(row2(a), VM) for a in (mix_bias, ffn_gain, ffn_shift, up_bias, down_bias)]
        + [(m, VM) for m in mixed]
        + [(w, wspec) for w in w_rest],
        [sds((BL, D), BF), sds((BL, D), BF), sds((T, D), F32)]
        + [sds((2, BL, PW), BF)] * (G * NP)
        + packs_out
        + [sds((16, D), F32)],
        scratch=[
            pltpu.VMEM((T, D), F32),
            pltpu.VMEM((T, D), BF),
            pltpu.VMEM((T, D), F32),
            pltpu.VMEM((T, D), F32),
            pltpu.VMEM((T, FC), BF),
            pltpu.VMEM((T, FC), BF),
            pltpu.VMEM((T, D), BF),
            pltpu.VMEM((D, D), BF),
        ]
        + weights_scr,
        flops=6 * T * D * (2 * FF + D),
        nbytes=20 << 20,
        trans=2 * T * FF,
    )
    out_own, out_send, g_resid = res[:3]
    gmix = [res[3 + d * NP : 3 + (d + 1) * NP] for d in range(G)]
    packs = res[3 + G * NP : -1]
    vec1 = res[-1]

    def back(p, q_p):
        return attend_back_call(
            geo, p, meta, doc_lengths, segs, q_p, k[p], v[p], lses, [m[p] for m in made], ghead[p]
        )

    ghead = [[gmix[0][p]] + [turn(gmix[d][p], d) for d in range(1, G)] for p in range(NP)]

    def step_plane(parts, vec=None):
        a = [parts[0], plane(parts[1], 1, 0), plane(parts[2], 0, 1), plane(parts[3], 1, 1)]
        n = parts[0].shape[1]
        outs = [sds((n, 128), BF)] * 4
        if vec is not None:
            a += [vec, plane(vec, 1, 0), plane(vec, 0, 1), plane(vec, 1, 1)]
            outs += [sds(vec.shape, F32)]
        return a, outs

    def plane_sum(a, outs):
        return call(
            functools.partial(plane_sum_kernel, len(outs) > 4),
            "plane_sum",
            [(t, VM) for t in a],
            outs,
            nbytes=8 << 20,
        )

    def step_line(parts, vec=None):
        a = [parts[0]] + [line(parts[d], d) for d in range(1, 4)]
        outs = [sds(parts[0].shape, BF)]
        if vec is not None:
            a += [vec] + [line(vec, d) for d in range(1, 4)]
            outs += [sds(vec.shape, F32)]
        return a, outs

    def line_sum(a, outs):
        return call(
            functools.partial(line_sum_kernel, len(outs) > 1),
            "line_sum",
            [(t, VM) for t in a],
            outs,
            nbytes=2 << 20,
        )

    gq = [back(0, q[0])]
    if geo.fast:
        sums = call(
            core_sum_kernel,
            "core_sum",
            [(after(packs[0], gq[0]), VM), (turn(after(packs[1], ghead[0][1]), 1), VM)],
            [sds((4, 576, 128), BF)] * 4,
            nbytes=8 << 20,
        )
        a1, o1 = step_plane(sums)
        gq += [back(p, after(q[p], sums[0])) for p in range(1, NP)]
    else:
        gq += [back(p, q[p]) for p in range(1, NP)]
    packs2_out = [sds((3, 2, 4, 64, 128), BF)] * 2 if geo.fast else [sds((D, 3 * D), BF)]
    packs2 = call(
        functools.partial(wgrad_kernel, geo),
        "wgrad",
        [(meta, SM), (h1, VM)] + [(t, VM) for t in gq],
        packs2_out,
        scratch=[pltpu.VMEM((D, 3 * HL), BF)],
        flops=2 * L * D * 3 * HL,
        nbytes=8 << 20,
    )
    if geo.fast:
        q1 = plane_sum(list(after(tuple(a1), packs2[0])), o1)
        b1, p1 = step_line(q1)
        parts2 = call(
            functools.partial(arrange_kernel, geo),
            "arrange",
            [(meta, SM), (after(packs2[0], q1[0]), VM), (turn(packs2[1], 1), VM)],
            [sds((4, 192, 128), BF)] * 4,
            nbytes=2 << 20,
        )
        a2, o2 = step_plane(parts2)
        gq = list(after(tuple(gq), parts2[0]))
    res2 = call(
        functools.partial(qkv_back_kernel, geo),
        "qkv_back",
        [(meta, SM), (vec1, VM)] + [(t, VM) for t in (*gq, *w_own)] + [(t, VM) for t in pieces],
        [sds((2, BL, D), F32)] + [sds((2, BL, D), BF)] * (G - 1) + [sds((16, D), F32)],
        flops=2 * L * D * 3 * HL,
        nbytes=12 << 20,
    )
    ghs, vec2 = res2[:G], res2[G]
    gh_recv = [turn(ghs[G - d], d) for d in range(1, G)]
    tgrad, tgrad_send, vec3 = call(
        functools.partial(last_kernel, geo),
        "norm_back",
        [(meta, SM), (gain1, VM), (vec2, VM)]
        + [(turn(vec2, 1) if geo.fast else jnp.zeros_like(vec2), VM), (g_resid, VM), (ghs[0], VM)]
        + [(r, VM) for r in gh_recv]
        + [(x0, VM), (x1, VM)],
        [sds((2, BL, D), BF), sds((BL, D), BF), sds((16, D), F32)],
        flops=T * D * 30,
        nbytes=8 << 20,
    )
    if geo.fast:
        (r1,) = line_sum(list(after(tuple(b1), tgrad_send)), p1)
        other1 = plane(r1, 1, 0)
        va = [vec3, plane(vec3, 1, 0), plane(vec3, 0, 1), plane(vec3, 1, 1)]
        *q2, vec4 = plane_sum(a2 + va, o2 + [sds(vec3.shape, F32)])
        b2, p2 = step_line(q2, vec4)
        mix_g, up_g, down_g = call(
            finish_kernel,
            "finish",
            [(meta, SM), (after(r1, q2[0]), VM), (other1, VM)],
            [sds(w.shape, F32) for w in (mix_weight, up_weight, down_weight)],
            nbytes=2 << 20,
        )
        r2, vec = line_sum(b2, p2)
        (qkv_g,) = call(
            finish_qkv_kernel,
            "finish_qkv",
            [(meta, SM), (r2, VM), (plane(r2, 1, 0), VM)],
            [sds(qkv_weight.shape, F32)],
            nbytes=1 << 20,
        )
        grads = (qkv_g, mix_g, up_g, down_g)
    else:
        def reduced(w):
            w = lax.psum_scatter(w, "col", scatter_dimension=1, tiled=True)
            w = lax.psum_scatter(w, "row", scatter_dimension=0, tiled=True)
            return lax.psum(w, "dp").astype(F32)

        grads = (reduced(packs2[0]), reduced(packs[2]), reduced(packs[0]), reduced(packs[1]))
        vec = lax.psum(vec3, ("dp", "col", "row"))

    def join(own, other):
        return lax.dynamic_update_slice(own, other[None], (1 - s, 0, 0))

    out_pair = jnp.where(s == 0, jnp.stack([out_own, swap_half(out_send)]), jnp.stack([swap_half(out_send), out_own]))
    tgrad = join(tgrad, swap_half(tgrad_send))
    return (
        out_pair,
        tgrad,
        *grads,
        vec[:8],
        vec[8 : 8 + FF // D].reshape(FF),
    )


def solution(mesh):
    return jax.shard_map(
        body,
        mesh=mesh,
        in_specs=(
            P(("dp", "row"), "col", None),
            P(("dp", "row"), None),
            P(),
            P(),
            P("row", "col"),
            P(),
            P(),
            P("row", "col"),
            P(),
            P(),
            P(),
            P("row", "col"),
            P(),
            P("row", "col"),
            P(),
            P(("dp", "row"), "col", None),
        ),
        out_specs=(
            P(("dp", "row"), "col", None),
            P(("dp", "row"), "col", None),
            P("row", "col"),
            P("row", "col"),
            P("row", "col"),
            P("row", "col"),
            P(),
            P(),
        ),
        check_vma=False,
    )
```

```python
import functools

import jax
import jax.numpy as jnp
from jax import lax
from jax.experimental import pallas as pl
from jax.experimental.pallas import tpu as pltpu
from jax.sharding import PartitionSpec as P

HEAD_DIM = 64
EPS = 1e-05
NEG = -1e30
LOG2E = 1.4426950408889634
PW = 128

BF = jnp.bfloat16
F32 = jnp.float32
VM = pl.BlockSpec(memory_space=pltpu.VMEM)
SM = pl.BlockSpec(memory_space=pltpu.SMEM)
HBM = pl.BlockSpec(memory_space=pl.ANY)
TQ = 256
TK = 256
FC = 512
RT = 256
KEEP_LB = ((0, 1, 4), (1, 4, 5))
SEND_LB = ((2, 3, 5), (0, 2, 3))


def sds(shape, dtype):
    return jax.ShapeDtypeStruct(shape, dtype)


NEAR = ('core_sum', 'plane_sum', 'arrange', 'plane_sum_qkv', 'line_sum_qkv', 'finish', 'finish_qkv', 'norm_back')


def near(a):
    return pltpu.with_memory_space_constraint(a, pltpu.VMEM)


def call(kernel, name, ins, outs, scratch=(), flops=0, nbytes=0, trans=0, **kw):
    return pl.pallas_call(
        kernel,
        name=name,
        out_shape=tuple(o for o in outs),
        in_specs=[spec for _, spec in ins],
        out_specs=tuple(VM for _ in outs),
        scratch_shapes=list(scratch),
        compiler_params=pltpu.CompilerParams(vmem_limit_bytes=(60 if name == "ffn" else 36) * 1024 * 1024, **kw),
        cost_estimate=pl.CostEstimate(flops=flops, bytes_accessed=nbytes, transcendentals=trans),
    )(*[near(a) if spec is VM and name in NEAR and a.ndim > 1 else a for a, spec in ins])


def nt(a, b):
    return lax.dot_general(a, b, (((1,), (1,)), ((), ())), preferred_element_type=F32)


def nn(a, b):
    return lax.dot_general(a, b, (((1,), (0,)), ((), ())), preferred_element_type=F32)


def tn(a, b):
    return lax.dot_general(a, b, (((0,), (0,)), ((), ())), preferred_element_type=F32)


def al(value, unit):
    return pl.multiple_of(value, unit)


def normed(v):
    mean = jnp.mean(v, axis=-1, keepdims=True)
    center = v - mean
    rstd = lax.rsqrt(jnp.mean(center * center, axis=-1, keepdims=True) + EPS)
    return center * rstd, rstd


class Geo:
    def __init__(self, dp, col, row, block_len, width, hidden):
        self.dp, self.C, self.R = dp, col, row
        self.G = col // 2
        self.BL = block_len
        self.L = block_len * col
        self.T = 2 * block_len
        self.D = width
        self.FF = hidden
        self.HL = width // self.G
        self.NP = self.HL // PW
        self.TQ = min(512, block_len)
        self.fast = (
            dp == 2 and col == 4 and row == 4 and width == 512 and hidden == 2048 and block_len % 256 == 0
        )

    def where(self, meta):
        col = meta[1]
        return col // self.G, col % self.G

    def block(self, s, g, e, d):
        half = s if e == 0 else 1 - s
        return half * self.G + lax.rem(g - d + self.G, self.G)


def norm_kernel(geo, meta, doc, gain, shift, *refs):
    s, g = geo.where(meta)
    pieces, (out, segk, segq) = refs[:-3], refs[-3:]
    fill_segments(geo, doc_ends(doc, s), segk, segq)
    for e in range(2):
        for d in range(geo.G):
            src = pieces[e * geo.G + d]
            base = geo.block(s, g, e, d) * geo.BL

            def step(i, carry):
                v = src[pl.ds(al(i * 128, 128), 128), :].astype(F32)
                xhat, _ = normed(v)
                out[pl.ds(al(base + i * 128, 128), 128), :] = (xhat * gain[...] + shift[...]).astype(BF)
                return carry

            lax.fori_loop(0, geo.BL // 128, step, 0, unroll=2)


def qkv_kernel(geo, meta, h1, bias, *refs):
    s, g = geo.where(meta)
    HL, D, NP = geo.HL, geo.D, geo.NP
    outs = refs[-(4 * NP) - 2 : -2] if geo.fast else refs[-(4 * NP) :]
    if geo.fast:
        pieces, (wscr, sem) = refs[:4], refs[-2:]
        z = meta[2]
        y, c = meta[1] // 2, meta[1] % 2
        copies = []
        for n in range(4):
            yy = y if n < 2 else 1 - y
            cp = c if n % 2 == 0 else 1 - c
            for d in range(4):
                zz = lax.rem(z - d + 4, 4)
                copies.append(
                    pltpu.make_async_copy(
                        pieces[n].at[d],
                        wscr.at[pl.ds(al(zz * 128, 128), 128), pl.ds(al((2 * yy + cp) * 384, 128), 384)],
                        sem,
                    )
                )
        for cpy in copies:
            cpy.start()
        for cpy in copies:
            cpy.wait()
    else:
        wscr = refs[0]

    def cols(part, p):
        return pl.ds(al(part * D + g * HL + p * PW, 128), PW)

    for p in range(NP):
        for part in range(3):
            outs[3 * NP + p][:, part * PW : (part + 1) * PW] = wscr[:, cols(part, p)]

    def step(i, carry):
        rows = pl.ds(al(i * 256, 256), 256)
        a = h1[rows, :]
        for p in range(NP):
            res = nn(a, outs[3 * NP + p][...])
            for part in range(3):
                outs[part * NP + p][rows, :] = (
                    res[:, part * PW : (part + 1) * PW] + bias[:, cols(part, p)]
                ).astype(BF)
        return carry

    lax.fori_loop(0, geo.L // 256, step, 0)


def doc_ends(doc, s):
    ends, total = [], 0
    for i in range(8):
        total = total + doc[s, i]
        ends.append(total)
    return ends


def span_start(ends, t):
    best = 0
    for e in ends:
        best = jnp.where(e <= t, e, best)
    return best


def span_end(ends, t, full):
    best = full
    for e in reversed(ends):
        best = jnp.where(e > t, e, best)
    return best


def fill_segments(geo, ends, segk, segq):
    def step(i, carry):
        rows = lax.broadcasted_iota(jnp.int32, (TK, 128), 0) + i * TK
        cols = lax.broadcasted_iota(jnp.int32, (8, TQ), 1) + i * TQ
        a = jnp.zeros((TK, 128), jnp.int32)
        b = jnp.zeros((8, TQ), jnp.int32)
        for e in ends:
            a += (rows >= e).astype(jnp.int32)
            b += (cols >= e).astype(jnp.int32)
        segk[pl.ds(al(i * TK, TK), TK), :] = a
        segq[:, pl.ds(al(i * TQ, TQ), TQ)] = b
        return carry

    lax.fori_loop(0, geo.L // TK, step, 0)


def mask_bias(segk, segq, k0, q0, tq):
    a = segk[pl.ds(k0, TK), :]
    b = segq[0:1, pl.ds(q0, tq)]
    same = jnp.concatenate([a] * (tq // 128), axis=1) == b
    return jnp.where(same, 0.0, NEG)


def head_mask(h, rows):
    lane = lax.broadcasted_iota(jnp.int32, (rows, PW), 1)
    return (lane // HEAD_DIM) == h


def ranges(first, last, one, lo, hi, tile):
    a = jnp.where(one, jnp.minimum((first + tile - 1) // tile, hi), hi)
    b = jnp.where(one, jnp.minimum(jnp.maximum(last // tile, a), hi), hi)
    return ((lo, a, True), (a, b, False), (b, hi, True))


HR = HEAD_DIM + 16


def attn_kernel(geo, dlist, meta, doc, segk, segq, *refs):
    G, NP, L, BL, TQF = geo.G, geo.NP, geo.L, geo.BL, geo.TQ
    q, k, v, refs = refs[:NP], refs[NP : 2 * NP], refs[2 * NP : 3 * NP], refs[3 * NP :]
    nd = len(dlist)
    outs, lses = refs[:nd], refs[nd : 2 * nd]
    vT, acc, sc = refs[2 * nd :]
    s, g = geo.where(meta)
    ends = doc_ends(doc, s)
    heads = [(p, h) for p in range(NP) for h in range(2)]

    def flip(i, carry):
        rows = pl.ds(al(i * TK, TK), TK)
        for p in range(NP):
            t = jnp.transpose(v[p][rows, :])
            for h in range(2):
                b = (2 * p + h) * HR
                vT[b : b + HEAD_DIM, rows] = t[h * HEAD_DIM : (h + 1) * HEAD_DIM, :]
                vT[b + HEAD_DIM : b + HR, rows] = jnp.ones((16, TK), BF)
        return carry

    lax.fori_loop(0, L // TK, flip, 0)

    for di, d in enumerate(dlist):

        def q_step(i, carry):
            e = i // (BL // TQF)
            off = al(lax.rem(i, BL // TQF) * TQF, TQF)
            half = jnp.where(e == 0, s, 1 - s)
            q0 = al((half * G + lax.rem(g - d + G, G)) * BL + off, TQF)
            first, last = span_start(ends, q0), span_end(ends, q0 + TQF - 1, L)
            one = first == span_start(ends, q0 + TQF - 1)
            klo = first // TK
            khi = (last + TK - 1) // TK
            qm = []
            for p, h in heads:
                qt = q[p][pl.ds(q0, TQF), :] * jnp.asarray(HEAD_DIM ** (-0.5), BF)
                qm.append(jnp.where(head_mask(h, TQF), qt, jnp.zeros_like(qt)))
            acc[...] = jnp.zeros_like(acc)

            def scores(masked, j, ms):
                k0 = al(j * TK, TK)
                if masked:
                    bias = mask_bias(segk, segq, k0, q0, TQF)
                out = []
                for n, (p, h) in enumerate(heads):
                    st = nt(k[p][pl.ds(k0, TK), :], qm[n])
                    if masked:
                        st = st + bias
                    sc[n, pl.ds(k0, TK), :] = st
                    out.append(jnp.maximum(ms[n], jnp.max(st.reshape(TK // 8, 8, TQF), axis=0)))
                return tuple(out)

            ms = tuple(jnp.full((8, TQF), -3e38, F32) for _ in heads)
            for lo, hi, masked in ranges(first, last, one, klo, khi, TK):
                ms = lax.fori_loop(lo, hi, functools.partial(scores, masked), ms)
            ms = [jnp.max(m, axis=0, keepdims=True) for m in ms]
            ml = [m * LOG2E for m in ms]

            def values(j, c2):
                k0 = al(j * TK, TK)
                for n in range(len(heads)):
                    pr = jnp.exp2(sc[n, pl.ds(k0, TK), :] * LOG2E - ml[n])
                    hs = slice(n * HR, (n + 1) * HR)
                    acc[hs, :] += nn(vT[hs, pl.ds(k0, TK)], pr.astype(BF))
                return c2

            lax.fori_loop(klo, khi, values, 0)
            for p in range(NP):
                parts = []
                for n in (2 * p, 2 * p + 1):
                    ls = acc[n * HR + HEAD_DIM : n * HR + HEAD_DIM + 1, :]
                    parts.append(acc[n * HR : n * HR + HEAD_DIM, :] * (1.0 / ls))
                    lses[di][e, n : n + 1, pl.ds(off, TQF)] = ms[n] + jnp.log(ls)
                res = jnp.transpose(jnp.concatenate(parts, axis=0)).astype(BF)
                outs[di][p, e, pl.ds(off, TQF), :] = res
            return carry

        lax.fori_loop(0, 2 * BL // TQF, q_step, 0)


def attn_back_kernel(geo, p, meta, doc, segk, segq, q, k, v, *refs):
    G, L, BL = geo.G, geo.L, geo.BL
    lses, mixed, grads = refs[:G], refs[G : 2 * G], refs[2 * G : 3 * G]
    out = refs[3 * G]
    qm, gm, kT, dqT, delta, lse, dk, dv = refs[3 * G + 1 :]
    s, g = geo.where(meta)
    ends = doc_ends(doc, s)
    scale = HEAD_DIM ** (-0.5)
    for e in range(2):
        for d in range(G):
            base = geo.block(s, g, e, d) * BL

            def load(i, carry):
                src = pl.ds(al(i * 256, 256), 256)
                dst = pl.ds(al(base + i * 256, 256), 256)
                gt = grads[d][e, src, :]
                zero = jnp.zeros_like(gt)
                prod = jnp.transpose(gt.astype(F32) * mixed[d][p, e, src, :].astype(F32))
                qt = q[dst, :] * jnp.asarray(scale, BF)
                for h in range(2):
                    hs = slice(h * HEAD_DIM, (h + 1) * HEAD_DIM)
                    keep = head_mask(h, 256)
                    gm[h, dst, :] = jnp.where(keep, gt, zero)
                    qm[h, dst, :] = jnp.where(keep, qt, zero)
                    delta[h : h + 1, dst] = jnp.sum(prod[hs, :], axis=0, keepdims=True)
                lse[:, dst] = lses[d][e, :, src]
                kT[:, dst] = jnp.transpose(k[dst, :])
                dqT[:, dst] = jnp.zeros((PW, 256), F32)
                return carry

            lax.fori_loop(0, BL // 256, load, 0)

    def k_step(j, carry):
        k0 = al(j * TK, TK)
        first, last = span_start(ends, k0), span_end(ends, k0 + TK - 1, L)
        one = first == span_start(ends, k0 + TK - 1)
        qlo = first // TQ
        qhi = (last + TQ - 1) // TQ
        kt = k[pl.ds(k0, TK), :]
        vt = v[pl.ds(k0, TK), :]
        dk[...] = jnp.zeros_like(dk)
        dv[...] = jnp.zeros_like(dv)

        def q_step(masked, i, c2):
            q0 = al(i * TQ, TQ)
            qs = pl.ds(q0, TQ)
            if masked:
                bias = mask_bias(segk, segq, k0, q0, TQ)
            for h in range(2):
                hs = slice(h * HEAD_DIM, (h + 1) * HEAD_DIM)
                qh, gh = qm[h, qs, :], gm[h, qs, :]
                n = 2 * p + h
                st = nt(kt, qh) - lse[n : n + 1, qs]
                if masked:
                    st = st + bias
                pr = jnp.exp(st)
                ds = (pr * (nt(vt, gh) - delta[h : h + 1, qs])).astype(BF)
                dv[...] += nn(pr.astype(BF), gh)
                dk[...] += nn(ds, qh)
                dqT[hs, qs] += nn(kT[hs, pl.ds(k0, TK)], ds)
            return c2

        for lo, hi, masked in ranges(first, last, one, qlo, qhi, TQ):
            lax.fori_loop(lo, hi, functools.partial(q_step, masked), 0)
        out[pl.ds(k0, TK), PW : 2 * PW] = dk[...].astype(BF)
        out[pl.ds(k0, TK), 2 * PW : 3 * PW] = dv[...].astype(BF)
        return carry

    lax.fori_loop(0, L // TK, k_step, 0)

    def last_step(i, carry):
        rows = pl.ds(al(i * TQ, TQ), TQ)
        out[rows, 0:PW] = (jnp.transpose(dqT[:, rows]) * scale).astype(BF)
        return carry

    lax.fori_loop(0, L // TQ, last_step, 0)


def attend_call(geo, dlist, meta, doc, segs, q, k, v):
    NP, L, BL, nd = geo.NP, geo.L, geo.BL, len(dlist)
    share = nd / geo.G
    res = call(
        functools.partial(attn_kernel, geo, dlist),
        "attend",
        [(meta, SM), (doc, SM), (segs[0], VM), (segs[1], VM)] + [(t, VM) for t in (*q, *k, *v)],
        [sds((NP, 2, BL, PW), BF)] * nd + [sds((2, 8, BL), F32)] * nd,
        scratch=[
            pltpu.VMEM((2 * NP * HR, L), BF),
            pltpu.VMEM((2 * NP * HR, geo.TQ), F32),
            pltpu.VMEM((2 * NP, L, geo.TQ), F32),
        ],
        flops=int(2 * L * L * geo.HL * 4 * share),
        nbytes=L * geo.HL * 8,
        trans=int(L * L * NP * share),
    )
    return res[:nd], res[nd:]


def attend_back_call(geo, p, meta, doc, segs, q, k, v, lses, mixed, grads):
    L = geo.L
    return call(
        functools.partial(attn_back_kernel, geo, p),
        "attend_back",
        [(meta, SM), (doc, SM), (segs[0], VM), (segs[1], VM), (q, VM), (k, VM), (v, VM)]
        + [(t, VM) for t in (*lses, *mixed, *grads)],
        [sds((L, 3 * PW), BF)],
        scratch=[
            pltpu.VMEM((2, L, PW), BF),
            pltpu.VMEM((2, L, PW), BF),
            pltpu.VMEM((PW, L), BF),
            pltpu.VMEM((PW, L), F32),
            pltpu.VMEM((8, L), F32),
            pltpu.VMEM((8, L), F32),
            pltpu.VMEM((TK, PW), F32),
            pltpu.VMEM((TK, PW), F32),
        ],
        flops=2 * L * L * PW * 10,
        nbytes=L * PW * 20,
        trans=L * L,
    )[0]


def gelu_parts(u):
    phi = 0.5 + 0.5 * lax.erf(u * (2.0 ** -0.5))
    pdf = jnp.exp(-0.5 * (u * u)) * 0.3989422804014327
    return phi, pdf


def ffn_kernel(geo, meta, *refs):
    G, HL, D, FF, BL, T, NP = geo.G, geo.HL, geo.D, geo.FF, geo.BL, geo.T, geo.NP
    s, g = geo.where(meta)
    pairs = [(d, p) for d in range(G) for p in range(NP)]
    x0, x1, cot, cot1, mixb, gain, shift, upb, downb = refs[:9]
    refs = refs[9:]
    mixed, refs = refs[:G], refs[G:]
    nw = 8 if geo.fast else 3
    wts, refs = refs[:nw], refs[nw:]
    out_own, out_send, g_resid = refs[:3]
    refs = refs[3:]
    gmix, refs = refs[: G * NP], refs[G * NP :]
    ng = 2 if geo.fast else 3
    packs, refs = refs[:ng], refs[ng:]
    vec, refs = refs[0], refs[1:]
    resid, h2, ffn, gh2, act_s, gu_s, ga_s, mg = refs[:8]
    refs = refs[8:]
    if geo.fast:
        wo, wu, wd, wg, sems = refs
        x, z = meta[0], meta[2]
        y, c = meta[1] // 2, meta[1] % 2
        groups = [[], [], []]
        for quad in range(4):
            yy = y if quad < 2 else 1 - y
            hh = x if quad % 2 == 0 else 1 - x
            for cc in range(2):
                cl = 2 * yy + (c if cc == 0 else 1 - c)
                src = wts[quad * 2 + cc]
                for d in range(4):
                    zz = lax.rem(z - d + 4, 4)
                    groups[0].append(
                        pltpu.make_async_copy(
                            src.at[d, pl.ds(512, 64), :],
                            wo.at[pl.ds(al(zz * 128 + hh * 64, 64), 64), pl.ds(al(cl * 128, 128), 128)],
                            sems.at[0],
                        )
                    )
                    for b in range(4):
                        groups[1].append(
                            pltpu.make_async_copy(
                                src.at[d, pl.ds(b * 64, 64), :],
                                wu.at[
                                    pl.ds(al(zz * 128 + hh * 64, 64), 64),
                                    pl.ds(al(cl * 512 + b * 128, 128), 128),
                                ],
                                sems.at[1],
                            )
                        )
                    groups[2].append(
                        pltpu.make_async_copy(
                            src.at[d, pl.ds(256, 256), :],
                            wd.at[pl.ds(al(zz * 512 + hh * 256, 256), 256), pl.ds(al(cl * 128, 128), 128)],
                            sems.at[2],
                        )
                    )
        for group in groups:
            for cpy in group:
                cpy.start()
        for cpy in groups[0]:
            cpy.wait()
    else:
        wo, wu, wd = wts
        (wg,) = refs

    zrow = jnp.zeros((1, D), F32)
    vec[...] = jnp.zeros_like(vec)

    for e in range(2):
        xe = x0 if e == 0 else x1
        ce = cot if e == 0 else cot1

        def first(i, carry):
            rows = pl.ds(al(i * RT, RT), RT)
            to = pl.ds(al(e * BL + i * RT, RT), RT)
            r = xe[rows, :].astype(F32) + mixb[...]
            for d, p in pairs:
                gp = lax.rem(g - d + G, G)
                r = r + nn(mixed[d][p, e, rows, :], wo[pl.ds(al(gp * HL + p * PW, 128), PW), :])
            resid[to, :] = r
            xhat, _ = normed(r)
            h2[to, :] = (xhat * gain[...] + shift[...]).astype(BF)
            ffn[to, :] = jnp.zeros((RT, D), F32)
            gh2[to, :] = jnp.zeros((RT, D), F32)
            return carry

        lax.fori_loop(0, BL // RT, first, 0)
    ga_s[0:BL, :] = cot[...]
    ga_s[BL:T, :] = cot1[...]
    if geo.fast:
        for group in groups[1:]:
            for cpy in group:
                cpy.wait()

    def chunk(f, carry):
        f0 = al(f * FC, FC)
        fs = pl.ds(f0, FC)

        def rows_step(i, hs):
            rows = pl.ds(al(i * RT, RT), RT)
            u = nn(h2[rows, :], wu[:, fs]) + upb[:, fs]
            phi, pdf = gelu_parts(u)
            act = (u * phi).astype(BF)
            gu = (nt(ga_s[rows, :], wd[fs, :]) * (phi + u * pdf)).astype(BF)
            act_s[rows, :] = act
            gu_s[rows, :] = gu
            ffn[rows, :] += nn(act, wd[fs, :])
            gh2[rows, :] += nt(gu, wu[:, fs])
            return hs + jnp.sum(gu.astype(F32), axis=0, keepdims=True)

        hsum = lax.fori_loop(0, T // RT, rows_step, jnp.zeros((1, FC), F32))
        per = D // FC
        vec[pl.ds(8 + f // per, 1), pl.ds(al(lax.rem(f, per) * FC, 128), FC)] = hsum
        dn = tn(act_s[...], ga_s[...])
        if geo.fast:
            wg[...] = dn.astype(BF)
            zr = lax.rem(f - z + 4, 4)
            for cr in range(2):
                for yr in range(2):
                    cl = 2 * (y if yr == 0 else 1 - y) + (c if cr == 0 else 1 - c)
                    for hr in range(2):
                        hh = x if hr == 0 else 1 - x
                        packs[cr][yr * 2 + hr, zr, 256:512, :] = wg[
                            pl.ds(al(hh * 256, 256), 256), pl.ds(al(cl * 128, 128), 128)
                        ]
        else:
            packs[1][fs, :] = dn.astype(BF)
        up = tn(h2[...], gu_s[...])
        if geo.fast:
            wg[...] = up.astype(BF)
            fy, fcr = f // 2, lax.rem(f, 2)
            yr = jnp.where(fy == y, 0, 1)
            for cr in range(2):
                @pl.when((fcr == c) if cr == 0 else (fcr != c))
                def _():
                    for hr in range(2):
                        hh = x if hr == 0 else 1 - x
                        for k in range(4):
                            zz = lax.rem(z + k, 4)
                            for b in range(4):
                                packs[cr][yr * 2 + hr, k, b * 64 : b * 64 + 64, :] = wg[
                                    pl.ds(al(zz * 128 + hh * 64, 64), 64), b * 128 : b * 128 + 128
                                ]
        else:
            packs[0][:, fs] = up.astype(BF)
        return carry

    lax.fori_loop(0, FF // FC, chunk, 0)

    sums = (zrow, zrow, zrow, zrow)
    for e in range(2):
        ce = cot if e == 0 else cot1
        oe = out_own if e == 0 else out_send

        def back(i, carry):
            mb, fg, fs_, db = carry
            rows = pl.ds(al(i * RT, RT), RT)
            to = pl.ds(al(e * BL + i * RT, RT), RT)
            r = resid[to, :]
            oe[rows, :] = (r + ffn[to, :] + downb[...]).astype(BF)
            xhat, rstd = normed(r)
            gh = gh2[to, :]
            ct = ce[rows, :].astype(F32)
            gx = gh * gain[...]
            gr = ct + rstd * (
                gx
                - jnp.mean(gx, axis=-1, keepdims=True)
                - xhat * jnp.mean(gx * xhat, axis=-1, keepdims=True)
            )
            g_resid[to, :] = gr
            ga = gr.astype(BF)
            gu_s[to, 0:D] = ga
            for n, (d, p) in enumerate(pairs):
                gp = lax.rem(g + d, G)
                gmix[n][e, rows, :] = nt(ga, wo[pl.ds(al(gp * HL + p * PW, 128), PW), :]).astype(BF)
            return (
                mb + jnp.sum(ga.astype(F32), axis=0, keepdims=True),
                fg + jnp.sum(gh * xhat, axis=0, keepdims=True),
                fs_ + jnp.sum(gh, axis=0, keepdims=True),
                db + jnp.sum(ct, axis=0, keepdims=True),
            )

        sums = lax.fori_loop(0, BL // RT, back, sums)
    for i in range(4):
        vec[4 + i : 5 + i, :] = sums[i]
    for d, p in pairs:
        gp = lax.rem(g - d + G, G)
        part = tn(mixed[d][p, 0], gu_s[0:BL, 0:D]) + tn(mixed[d][p, 1], gu_s[BL:T, 0:D])
        mg[pl.ds(al(gp * HL + p * PW, 128), PW), :] = part.astype(BF)
    if geo.fast:
        for cr in range(2):
            for yr in range(2):
                cl = 2 * (y if yr == 0 else 1 - y) + (c if cr == 0 else 1 - c)
                for hr in range(2):
                    hh = x if hr == 0 else 1 - x
                    for k in range(4):
                        zz = lax.rem(z + k, 4)
                        packs[cr][yr * 2 + hr, k, 512:576, :] = mg[
                            pl.ds(al(zz * 128 + hh * 64, 64), 64), pl.ds(al(cl * 128, 128), 128)
                        ]
    else:
        packs[2][...] = mg[...]


def put_vec(ref, base, v):
    hi = v.astype(BF)
    lo = (v - hi.astype(F32)).astype(BF)
    for n, t in enumerate((hi, lo)):
        for b in range(4):
            at = base + (n * 4 + b) * 16
            ref[at : at + 16, :] = t[:, b * 128 : b * 128 + 128]


def get_vec(ref, base):
    def term(n):
        at = base + n * 64
        return jnp.concatenate([ref[at + b * 16 : at + b * 16 + 16, :] for b in range(4)], axis=1).astype(F32)

    return term(0) + term(1)


def wgrad_kernel(geo, meta, vec_in, gain, shift, h1, *refs):
    G, HL, D, NP = geo.G, geo.HL, geo.D, geo.NP
    s, g = geo.where(meta)
    gq, w, refs = refs[:NP], refs[NP : 2 * NP], refs[2 * NP :]
    if geo.fast:
        a, b, c, d, *refs = refs
        refs[2][...] = add4(a[...], b[...], c[...], d[...]).astype(BF)
        refs = refs[:2] + refs[3:]
    packs, (wg, vec, acc) = refs[:-3], refs[-3:]
    vec[...] = vec_in[...]
    ones = jnp.ones((16, geo.L), BF)
    back = jnp.zeros((16, D), F32)
    for p in range(NP):
        part = tn(h1[...], gq[p][...])
        wg[:, p * 3 * PW : (p + 1) * 3 * PW] = part.astype(BF)
        prod = part * w[p][...].astype(F32)
        prod = prod[:, 0:PW] + prod[:, PW : 2 * PW] + prod[:, 2 * PW : 3 * PW]
        if p == 0:
            acc[...] = prod
        else:
            acc[...] += prod
        total = nn(ones, gq[p][...])
        hi = total.astype(BF)
        lo = (total - hi.astype(F32)).astype(BF)
        back = back + nt(hi, w[p][...]) + nt(lo, w[p][...])
        cols = pl.ds(al(g * HL + p * PW, 128), PW)
        vec[2:3, cols] = total[0:1, 0:PW]
        vec[3:4, cols] = total[0:1, 2 * PW : 3 * PW]
    first = jnp.sum(jnp.transpose(acc[...]), axis=0, keepdims=True)
    vec[0:1, :] = (first - shift[...] * back[0:1, :]) / gain[...]
    vec[1:2, :] = back[0:1, :]
    if geo.fast:
        x, z, c = meta[0], meta[2], meta[1] % 2
        for cr, table in ((0, KEEP_LB), (1, SEND_LB)):
            for b in range(3):
                lb = [(t[b] % 2) * 3 + t[b] // 2 for t in table]
                at = jnp.where(c == 0, lb[0], lb[1])
                for hr in range(2):
                    hh = x if hr == 0 else 1 - x
                    for k in range(4):
                        zz = lax.rem(z + k, 4)
                        to = ((b * 2 + hr) * 4 + k) * 64
                        packs[cr][to : to + 64, :] = wg[
                            pl.ds(al(zz * 128 + hh * 64, 64), 64), pl.ds(al(at * 128, 128), 128)
                        ]
            put_vec(packs[cr], 1536, vec[...])
    else:
        packs[1][...] = vec[...]
        packs[0][...] = jnp.zeros_like(packs[0])
        for p in range(NP):
            for part in range(3):
                packs[0][:, pl.ds(al(part * D + g * HL + p * PW, 128), PW)] = wg[
                    :, (3 * p + part) * PW : (3 * p + part + 1) * PW
                ]


def qkv_back_kernel(geo, meta, *refs):
    G, BL, NP = geo.G, geo.BL, geo.NP
    s, g = geo.where(meta)
    gq, w, ghs = refs[:NP], refs[NP : 2 * NP], refs[2 * NP :]
    for e in range(2):
        for d in range(G):
            base = geo.block(s, g, e, d) * BL

            def step(i, carry):
                rows = pl.ds(al(i * RT, RT), RT)
                at = pl.ds(al(base + i * RT, RT), RT)
                gh = nt(gq[0][at, :], w[0][...])
                for p in range(1, NP):
                    gh = gh + nt(gq[p][at, :], w[p][...])
                ghs[d][e, rows, :] = gh.astype(ghs[d].dtype)
                return carry

            lax.fori_loop(0, BL // RT, step, 0)


def last_kernel(geo, meta, gain, g_resid, gh, *refs):
    G, D, BL = geo.G, geo.D, geo.BL
    s, _ = geo.where(meta)
    recv, (x0, x1, out, send) = refs[: G - 1], refs[G - 1 :]
    for e in range(2):
        xe = x0 if e == 0 else x1

        def step(i, carry):
            rows = pl.ds(al(i * RT, RT), RT)
            to = pl.ds(al(e * BL + i * RT, RT), RT)
            xhat, rstd = normed(xe[rows, :].astype(F32))
            total = gh[e, rows, :]
            for r in recv:
                total = total + r[e, rows, :].astype(F32)
            gx = total * gain[...]
            res = g_resid[to, :] + rstd * (
                gx
                - jnp.mean(gx, axis=-1, keepdims=True)
                - xhat * jnp.mean(gx * xhat, axis=-1, keepdims=True)
            )
            if e == 0:
                out[s, rows, :] = res.astype(BF)
            else:
                send[rows, :] = res.astype(BF)
            return carry

        lax.fori_loop(0, BL // RT, step, 0)


def core_sum_kernel(own, recv, *outs):
    for q in range(4):
        outs[q][...] = (own[q].astype(F32) + recv[q].astype(F32)).astype(BF)


def arrange_kernel(geo, meta, keep, recv, *outs):
    y, c = meta[1] // 2, meta[1] % 2
    total = get_vec(keep, 1536) + get_vec(recv, 1536)
    for out in outs:
        put_vec(out, 768, total)
    for cs in range(2):
        mine = sorted((lb // 2) * 4 + 2 * cs + lb % 2 for lb in KEEP_LB[cs])
        theirs = sorted((lb // 2) * 4 + 2 * (1 - cs) + lb % 2 for lb in SEND_LB[1 - cs])
        for ys in range(2):
            @pl.when(jnp.logical_and(c == cs, y == ys))
            def _():
                for yr in range(2):
                    first = 3 * (2 * (ys ^ yr) + cs)
                    for o in range(3):
                        b = first + o
                        src, slot = (keep, mine.index(b)) if b in mine else (recv, theirs.index(b))
                        for hr in range(2):
                            for k in range(4):
                                at = ((slot * 2 + hr) * 4 + k) * 64
                                to = k * 192 + o * 64
                                outs[yr * 2 + hr][to : to + 64, :] = src[at : at + 64, :]


def add4(a, b, c, d):
    return (a.astype(F32) + b.astype(F32)) + (c.astype(F32) + d.astype(F32))


def plane_sum_kernel(a, b, c, d, *outs):
    for k in range(4):
        outs[k][...] = add4(a[k], b[k], c[k], d[k]).astype(BF)


def plane_sum_qkv_kernel(a, b, c, d, *outs):
    va, vb, vc, vd = (get_vec(t, 768) for t in (a, b, c, d))
    total = (va + vb) + (vc + vd)
    for k in range(4):
        at = slice(k * 192, k * 192 + 192)
        outs[k][0:192, :] = add4(a[at, :], b[at, :], c[at, :], d[at, :]).astype(BF)
        put_vec(outs[k], 192, total)


def line_sum_qkv_kernel(a, b, c, d, out, vec):
    va, vb, vc, vd = (get_vec(t, 192) for t in (a, b, c, d))
    vec[...] = (va + vc) + (vb + vd)
    out[...] = add4(a[0:192, :], b[0:192, :], c[0:192, :], d[0:192, :]).astype(BF)


def finish_kernel(meta, r, o, mix, up, down):
    x = meta[0]
    for src, h in ((r, x), (o, 1 - x)):
        rows = pl.ds(al(h * 64, 64), 64)
        for b in range(4):
            up[rows, b * 128 : b * 128 + 128] = src[b * 64 : b * 64 + 64, :].astype(F32)
        down[pl.ds(al(h * 256, 256), 256), :] = src[256:512, :].astype(F32)
        mix[rows, :] = src[512:576, :].astype(F32)


def finish_qkv_kernel(meta, r, o, qkv):
    x = meta[0]
    for src, h in ((r, x), (o, 1 - x)):
        for b in range(3):
            qkv[pl.ds(al(h * 64, 64), 64), b * 128 : b * 128 + 128] = src[b * 64 : b * 64 + 64, :].astype(F32)


def pack_kernel(meta, mix, up, down, rest):
    h = meta[0]
    rows = pl.ds(al(h * 64, 64), 64)
    for b in range(4):
        rest[b * 64 : b * 64 + 64, :] = up[rows, b * 128 : b * 128 + 128].astype(BF)
    rest[256:512, :] = down[pl.ds(al(h * 256, 256), 256), :].astype(BF)
    rest[512:576, :] = mix[rows, :].astype(BF)


def body(
    tokens,
    doc_lengths,
    norm_gain,
    norm_shift,
    qkv_weight,
    query_bias,
    value_bias,
    mix_weight,
    mix_bias,
    ffn_gain,
    ffn_shift,
    up_weight,
    up_bias,
    down_weight,
    down_bias,
    cotangent,
):
    DP, C, R = lax.axis_size("dp"), lax.axis_size("col"), lax.axis_size("row")
    _, BL, D = tokens.shape
    FF = up_bias.shape[0]
    geo = Geo(DP, C, R, BL, D, FF)
    G, HL, L, T = geo.G, geo.HL, geo.L, geo.T
    ix, ic, iz = lax.axis_index("dp"), lax.axis_index("col"), lax.axis_index("row")
    s = ic // G
    meta = jnp.stack([ix, ic, iz]).astype(jnp.int32)

    def swap_half(v):
        return lax.ppermute(v, "col", [(i, (i + G) % C) for i in range(C)])

    def turn(v, d):
        return lax.ppermute(v, "col", [(i, (i // G) * G + (i % G + d) % G) for i in range(C)])

    def plane(v, dx, dy):
        pairs = [
            (i * C + j, ((i + dx) % 2) * C + (j + dy * G) % C) for i in range(2) for j in range(C)
        ]
        return lax.ppermute(v, ("dp", "col"), pairs)

    def line(v, d):
        return lax.ppermute(v, "row", [(i, (i + d) % R) for i in range(R)])

    def row2(v):
        return v.reshape(1, v.shape[0])

    def pick(v, i):
        return lax.dynamic_index_in_dim(v, i, 0, keepdims=False)

    def after(v, dep):
        return lax.optimization_barrier((v, dep))[0]

    NP = geo.NP
    if geo.fast:
        def lines(v):
            return [v] + [line(v, d) for d in range(1, 4)]

        wq = qkv_weight.astype(BF)
        lines_qkv = lines(wq)
        x0 = pick(after(tokens, wq), s)
        x1 = swap_half(pick(after(tokens, wq), 1 - s))
        (half_rest,) = call(
            pack_kernel,
            "pack",
            [(after(meta, wq), SM), (mix_weight, VM), (up_weight, VM), (down_weight, VM)],
            [sds((576, 128), BF)],
            nbytes=2 << 20,
        )
        turn0 = turn(x0, 1)
        own_qkv = jnp.stack(after(tuple(lines_qkv), half_rest))
        across = swap_half(after(own_qkv, turn0))
        lines_rest = lines(after(half_rest, own_qkv))
    else:
        x0 = pick(tokens, s)
        x1 = swap_half(pick(tokens, 1 - s))

        def whole(w):
            w = lax.all_gather(w.astype(BF), "row", axis=0, tiled=True)
            return lax.all_gather(w, "col", axis=1, tiled=True)

        w_qkv = [whole(qkv_weight)]
        w_rest = [whole(mix_weight), whole(up_weight), whole(down_weight)]
    pieces = [x0] + ([turn0] if geo.fast else [turn(x0, d) for d in range(1, G)])
    pieces += [x1] + [turn(x1, d) for d in range(1, G)]
    gain1, shift1 = row2(norm_gain), row2(norm_shift)
    h1, segk, segq = call(
        functools.partial(norm_kernel, geo),
        "norm_one",
        [(meta, SM), (doc_lengths, SM), (gain1, VM), (shift1, VM)] + [(p, VM) for p in pieces],
        [sds((L, D), BF), sds((L, 128), jnp.int32), sds((8, L), jnp.int32)],
        flops=L * D * 10,
        nbytes=L * D * 4,
    )
    segs = (segk, segq)
    if geo.fast:
        w_qkv = [own_qkv, turn(own_qkv, 1), across, turn(after(across, h1), 1)]
    bias = row2(jnp.concatenate([query_bias, jnp.zeros_like(query_bias), value_bias]))
    wspec = HBM if geo.fast else VM
    res = call(
        functools.partial(qkv_kernel, geo),
        "qkv",
        [(meta, SM), (h1, VM), (bias, VM)] + [(w, wspec) for w in w_qkv],
        [sds((L, PW), BF)] * (3 * NP) + [sds((D, 3 * PW), BF)] * NP,
        scratch=[pltpu.VMEM((D, 3 * D), BF), pltpu.SemaphoreType.DMA(())] if geo.fast else [],
        flops=2 * L * D * 3 * HL,
        nbytes=L * D * 2 + L * HL * 6 + D * D * 6,
    )
    q, k, v, w_own = (res[n * NP : (n + 1) * NP] for n in range(4))
    cot0 = pick(cotangent, s)
    cot1 = swap_half(pick(after(cotangent, x1) if geo.fast else cotangent, 1 - s))
    if geo.fast:
        rest = jnp.stack(after(tuple(lines_rest), (q[0], cot1)))
        quads_rest = [plane(rest, 1, 0), plane(rest, 0, 1), plane(rest, 1, 1)]
    far, lse_far = attend_call(geo, tuple(range(1, G)), meta, doc_lengths, segs, q, k, v)
    if geo.fast:
        w_rest = [rest, turn(rest, 1)]
        w_rest += [t for u in after(tuple(quads_rest[:2]), (far[0], w_rest[1])) for t in (u, turn(u, 1))]
        q_own = list(after(tuple(q), (far[0], w_rest[2], w_rest[4])))
    else:
        q_own = list(after(tuple(q), far[0]))
    own, lse_own = attend_call(geo, (0,), meta, doc_lengths, segs, q_own, k, v)
    if geo.fast:
        diag = after(quads_rest[2], own[0])
        w_rest += [diag, turn(diag, 1)]
    made = [own[0]] + list(far)
    lses = list(lse_own) + list(lse_far)
    mixed = [made[0]] + [turn(made[G - d], d) for d in range(1, G)]
    packs_out = (
        [sds((4, 4, 576, 128), BF)] * 2
        if geo.fast
        else [sds((D, FF), BF), sds((FF, D), BF), sds((D, D), BF)]
    )
    weights_scr = (
        [
            pltpu.VMEM((D, D), BF),
            pltpu.VMEM((D, FF), BF),
            pltpu.VMEM((FF, D), BF),
            pltpu.VMEM((FC, FC), BF),
            pltpu.SemaphoreType.DMA((3,)),
        ]
        if geo.fast
        else [pltpu.VMEM((8, 128), BF)]
    )
    res = call(
        functools.partial(ffn_kernel, geo),
        "ffn",
        [(meta, SM), (x0, VM), (x1, VM), (cot0, VM), (cot1, VM)]
        + [(row2(a), VM) for a in (mix_bias, ffn_gain, ffn_shift, up_bias, down_bias)]
        + [(m, VM) for m in mixed]
        + [(w, wspec) for w in w_rest],
        [sds((BL, D), BF), sds((BL, D), BF), sds((T, D), F32)]
        + [sds((2, BL, PW), BF)] * (G * NP)
        + packs_out
        + [sds((16, D), F32)],
        scratch=[
            pltpu.VMEM((T, D), F32),
            pltpu.VMEM((T, D), BF),
            pltpu.VMEM((T, D), F32),
            pltpu.VMEM((T, D), F32),
            pltpu.VMEM((T, FC), BF),
            pltpu.VMEM((T, FC), BF),
            pltpu.VMEM((T, D), BF),
            pltpu.VMEM((D, D), BF),
        ]
        + weights_scr,
        flops=6 * T * D * (2 * FF + D),
        nbytes=20 << 20,
        trans=2 * T * FF,
    )
    out_own, out_send, g_resid = res[:3]
    gmix = [res[3 + d * NP : 3 + (d + 1) * NP] for d in range(G)]
    packs = res[3 + G * NP : -1]
    vec1 = res[-1]

    def back(p, q_p):
        return attend_back_call(
            geo, p, meta, doc_lengths, segs, q_p, k[p], v[p], lses, made, ghead[p]
        )

    def turned(p, dep):
        return [gmix[0][p]] + [turn(after(gmix[d][p], dep), d) for d in range(1, G)]

    def step_plane(parts):
        return (parts[0], plane(parts[1], 1, 0), plane(parts[2], 0, 1), plane(parts[3], 1, 1))

    def step_line(parts):
        return (parts[0],) + tuple(line(parts[d], d) for d in range(1, 4))

    def add(kernel, name, arrays, outs):
        return call(kernel, name, [(t, VM) for t in arrays], outs, nbytes=4 << 20)

    if geo.fast:
        sums = add(core_sum_kernel, "core_sum", (packs[0], turn(packs[1], 1)), [sds((4, 576, 128), BF)] * 4)
        a1 = step_plane(sums)
        ghead = [turned(0, sums[0])]
        gq = [back(0, after(q[0], sums[0]))]
        q1 = add(plane_sum_kernel, "plane_sum", after(a1, gq[0]), [sds((576, 128), BF)] * 4)
        b1 = step_line(q1)
        out_recv = swap_half(after(out_send, q1[0]))
        ghead.append(turned(1, q1[0]))
        gq += [back(1, after(q[1], q1[0]))]
        packs2_out = [sds((1664, 128), BF)] * 2 + [sds((576, 128), BF)]
    else:
        b1 = ()
        ghead = [turned(p, q[p]) for p in range(NP)]
        gq = [back(p, q[p]) for p in range(NP)]
        out_recv = swap_half(out_send)
        packs2_out = [sds((D, 3 * D), BF), sds((16, D), F32)]
    packs2 = call(
        functools.partial(wgrad_kernel, geo),
        "wgrad",
        [(meta, SM), (vec1, VM), (gain1, VM), (shift1, VM), (after(h1, out_recv), VM)]
        + [(t, VM) for t in (*gq, *w_own, *b1)],
        packs2_out,
        scratch=[pltpu.VMEM((D, 3 * HL), BF), pltpu.VMEM((16, D), F32), pltpu.VMEM((D, PW), F32)],
        flops=2 * L * D * 3 * HL,
        nbytes=8 << 20,
    )
    if geo.fast:
        recv2, r1 = turn(packs2[1], 1), packs2[2]
        gq = list(after(tuple(gq), r1))
    ghs = call(
        functools.partial(qkv_back_kernel, geo),
        "qkv_back",
        [(meta, SM)] + [(t, VM) for t in (*gq, *w_own)],
        [sds((2, BL, D), F32)] + [sds((2, BL, D), BF)] * (G - 1),
        flops=2 * L * D * 3 * HL,
        nbytes=12 << 20,
    )
    gh_recv = [turn(ghs[G - d], d) for d in range(1, G)]
    if geo.fast:
        own2, recv2 = after((packs2[0], recv2), ghs[0])
        parts2 = call(
            functools.partial(arrange_kernel, geo),
            "arrange",
            [(meta, SM), (own2, VM), (recv2, VM)],
            [sds((896, 128), BF)] * 4,
            nbytes=2 << 20,
        )
        a2 = step_plane(parts2)
        other1 = plane(after(r1, parts2[0]), 1, 0)

    tgrad, tgrad_send = call(
        functools.partial(last_kernel, geo),
        "norm_back",
        [(meta, SM), (gain1, VM), (g_resid, VM), (after(ghs[0], parts2[0]) if geo.fast else ghs[0], VM)]
        + [(r, VM) for r in gh_recv]
        + [(x0, VM), (x1, VM)],
        [sds((2, BL, D), BF), sds((BL, D), BF)],
        flops=T * D * 30,
        nbytes=8 << 20,
    )
    tgrad_recv = swap_half(tgrad_send)
    if geo.fast:
        q2 = add(plane_sum_qkv_kernel, "plane_sum_qkv", after(a2, tgrad_send), [sds((320, 128), BF)] * 4)
        b2 = step_line(q2)
        mix_g, up_g, down_g = call(
            finish_kernel,
            "finish",
            [(meta, SM), (after(r1, q2[0]), VM), (other1, VM)],
            [sds(w.shape, F32) for w in (mix_weight, up_weight, down_weight)],
            nbytes=2 << 20,
        )
        r2, vec = add(
            line_sum_qkv_kernel, "line_sum_qkv", after(b2, mix_g), [sds((192, 128), BF), sds((16, D), F32)]
        )
        (qkv_g,) = call(
            finish_qkv_kernel,
            "finish_qkv",
            [(meta, SM), (r2, VM), (plane(r2, 1, 0), VM)],
            [sds(qkv_weight.shape, F32)],
            nbytes=1 << 20,
        )
        grads = (qkv_g, mix_g, up_g, down_g)
    else:
        def reduced(w):
            w = lax.psum_scatter(w, "col", scatter_dimension=1, tiled=True)
            w = lax.psum_scatter(w, "row", scatter_dimension=0, tiled=True)
            return lax.psum(w, "dp").astype(F32)

        grads = (reduced(packs2[0]), reduced(packs[2]), reduced(packs[0]), reduced(packs[1]))
        vec = lax.psum(packs2[1], ("dp", "col", "row"))

    def join(own, other):
        return lax.dynamic_update_slice(own, other[None], (1 - s, 0, 0))

    out_pair = jnp.where(s == 0, jnp.stack([out_own, out_recv]), jnp.stack([out_recv, out_own]))
    tgrad = join(tgrad, tgrad_recv)
    return (
        out_pair,
        tgrad,
        *grads,
        vec[:8],
        vec[8 : 8 + FF // D].reshape(FF),
    )


def solution(mesh):
    return jax.shard_map(
        body,
        mesh=mesh,
        in_specs=(
            P(("dp", "row"), "col", None),
            P(("dp", "row"), None),
            P(),
            P(),
            P("row", "col"),
            P(),
            P(),
            P("row", "col"),
            P(),
            P(),
            P(),
            P("row", "col"),
            P(),
            P("row", "col"),
            P(),
            P(("dp", "row"), "col", None),
        ),
        out_specs=(
            P(("dp", "row"), "col", None),
            P(("dp", "row"), "col", None),
            P("row", "col"),
            P("row", "col"),
            P("row", "col"),
            P("row", "col"),
            P(),
            P(),
        ),
        check_vma=False,
    )
```

```python
import functools

import jax
import jax.numpy as jnp
from jax import lax
from jax.experimental import pallas as pl
from jax.experimental.pallas import tpu as pltpu
from jax.sharding import PartitionSpec as P

HEAD_DIM = 64
EPS = 1e-05
NEG = -1e30
LOG2E = 1.4426950408889634
PW = 128

BF = jnp.bfloat16
F32 = jnp.float32
VM = pl.BlockSpec(memory_space=pltpu.VMEM)
SM = pl.BlockSpec(memory_space=pltpu.SMEM)
HBM = pl.BlockSpec(memory_space=pl.ANY)
TQ = 256
TK = 256
FC = 512
RT = 256
KEEP_LB = ((0, 1, 4), (1, 4, 5))
SEND_LB = ((2, 3, 5), (0, 2, 3))


def sds(shape, dtype):
    return jax.ShapeDtypeStruct(shape, dtype)


NEAR = ('core_sum', 'plane_sum', 'arrange', 'plane_sum_qkv', 'line_sum_qkv', 'finish', 'finish_qkv', 'norm_back')


def near(a):
    return pltpu.with_memory_space_constraint(a, pltpu.VMEM)


def call(kernel, name, ins, outs, scratch=(), flops=0, nbytes=0, trans=0, **kw):
    return pl.pallas_call(
        kernel,
        name=name,
        out_shape=tuple(o for o in outs),
        in_specs=[spec for _, spec in ins],
        out_specs=tuple(VM for _ in outs),
        scratch_shapes=list(scratch),
        compiler_params=pltpu.CompilerParams(vmem_limit_bytes=36 * 1024 * 1024, **kw),
        cost_estimate=pl.CostEstimate(flops=flops, bytes_accessed=nbytes, transcendentals=trans),
    )(*[near(a) if spec is VM and name in NEAR and a.ndim > 1 else a for a, spec in ins])


def nt(a, b):
    return lax.dot_general(a, b, (((1,), (1,)), ((), ())), preferred_element_type=F32)


def nn(a, b):
    return lax.dot_general(a, b, (((1,), (0,)), ((), ())), preferred_element_type=F32)


def tn(a, b):
    return lax.dot_general(a, b, (((0,), (0,)), ((), ())), preferred_element_type=F32)


def al(value, unit):
    return pl.multiple_of(value, unit)


def normed(v):
    mean = jnp.mean(v, axis=-1, keepdims=True)
    center = v - mean
    rstd = lax.rsqrt(jnp.mean(center * center, axis=-1, keepdims=True) + EPS)
    return center * rstd, rstd


class Geo:
    def __init__(self, dp, col, row, block_len, width, hidden):
        self.dp, self.C, self.R = dp, col, row
        self.G = col // 2
        self.BL = block_len
        self.L = block_len * col
        self.T = 2 * block_len
        self.D = width
        self.FF = hidden
        self.HL = width // self.G
        self.NP = self.HL // PW
        self.TQ = min(512, block_len)
        self.fast = (
            dp == 2 and col == 4 and row == 4 and width == 512 and hidden == 2048 and block_len % 256 == 0
        )

    def where(self, meta):
        col = meta[1]
        return col // self.G, col % self.G

    def block(self, s, g, e, d):
        half = s if e == 0 else 1 - s
        return half * self.G + lax.rem(g - d + self.G, self.G)


def norm_kernel(geo, meta, doc, gain, shift, *refs):
    s, g = geo.where(meta)
    pieces, (out, segk, segq) = refs[:-3], refs[-3:]
    fill_segments(geo, doc_ends(doc, s), segk, segq)
    for e in range(2):
        for d in range(geo.G):
            src = pieces[e * geo.G + d]
            base = geo.block(s, g, e, d) * geo.BL

            def step(i, carry):
                v = src[pl.ds(al(i * 128, 128), 128), :].astype(F32)
                xhat, _ = normed(v)
                out[pl.ds(al(base + i * 128, 128), 128), :] = (xhat * gain[...] + shift[...]).astype(BF)
                return carry

            lax.fori_loop(0, geo.BL // 128, step, 0, unroll=2)


def qkv_kernel(geo, meta, h1, bias, *refs):
    s, g = geo.where(meta)
    HL, D, NP = geo.HL, geo.D, geo.NP
    outs = refs[-(4 * NP) - 2 : -2] if geo.fast else refs[-(4 * NP) :]
    if geo.fast:
        pieces, (wscr, sem) = refs[:4], refs[-2:]
        z = meta[2]
        y, c = meta[1] // 2, meta[1] % 2
        copies = []
        for n in range(4):
            yy = y if n < 2 else 1 - y
            cp = c if n % 2 == 0 else 1 - c
            for d in range(4):
                zz = lax.rem(z - d + 4, 4)
                copies.append(
                    pltpu.make_async_copy(
                        pieces[n].at[d],
                        wscr.at[pl.ds(al(zz * 128, 128), 128), pl.ds(al((2 * yy + cp) * 384, 128), 384)],
                        sem,
                    )
                )
        for cpy in copies:
            cpy.start()
        for cpy in copies:
            cpy.wait()
    else:
        wscr = refs[0]

    def cols(part, p):
        return pl.ds(al(part * D + g * HL + p * PW, 128), PW)

    for p in range(NP):
        for part in range(3):
            outs[3 * NP + p][:, part * PW : (part + 1) * PW] = wscr[:, cols(part, p)]

    def step(i, carry):
        rows = pl.ds(al(i * 256, 256), 256)
        a = h1[rows, :]
        for p in range(NP):
            res = nn(a, outs[3 * NP + p][...])
            for part in range(3):
                outs[part * NP + p][rows, :] = (
                    res[:, part * PW : (part + 1) * PW] + bias[:, cols(part, p)]
                ).astype(BF)
        return carry

    lax.fori_loop(0, geo.L // 256, step, 0)


def doc_ends(doc, s):
    ends, total = [], 0
    for i in range(8):
        total = total + doc[s, i]
        ends.append(total)
    return ends


def span_start(ends, t):
    best = 0
    for e in ends:
        best = jnp.where(e <= t, e, best)
    return best


def span_end(ends, t, full):
    best = full
    for e in reversed(ends):
        best = jnp.where(e > t, e, best)
    return best


def fill_segments(geo, ends, segk, segq):
    def step(i, carry):
        rows = lax.broadcasted_iota(jnp.int32, (TK, 128), 0) + i * TK
        cols = lax.broadcasted_iota(jnp.int32, (8, TQ), 1) + i * TQ
        a = jnp.zeros((TK, 128), jnp.int32)
        b = jnp.zeros((8, TQ), jnp.int32)
        for e in ends:
            a += (rows >= e).astype(jnp.int32)
            b += (cols >= e).astype(jnp.int32)
        segk[pl.ds(al(i * TK, TK), TK), :] = a
        segq[:, pl.ds(al(i * TQ, TQ), TQ)] = b
        return carry

    lax.fori_loop(0, geo.L // TK, step, 0)


def mask_bias(segk, segq, k0, q0, tq):
    a = segk[pl.ds(k0, TK), :]
    b = segq[0:1, pl.ds(q0, tq)]
    same = jnp.concatenate([a] * (tq // 128), axis=1) == b
    return jnp.where(same, 0.0, NEG)


def head_mask(h, rows):
    lane = lax.broadcasted_iota(jnp.int32, (rows, PW), 1)
    return (lane // HEAD_DIM) == h


def ranges(first, last, one, lo, hi, tile):
    a = jnp.where(one, jnp.minimum((first + tile - 1) // tile, hi), hi)
    b = jnp.where(one, jnp.minimum(jnp.maximum(last // tile, a), hi), hi)
    return ((lo, a, True), (a, b, False), (b, hi, True))


HR = HEAD_DIM + 16


def attn_kernel(geo, dlist, meta, doc, segk, segq, *refs):
    G, NP, L, BL, TQF = geo.G, geo.NP, geo.L, geo.BL, geo.TQ
    q, k, v, refs = refs[:NP], refs[NP : 2 * NP], refs[2 * NP : 3 * NP], refs[3 * NP :]
    nd = len(dlist)
    outs, lses = refs[:nd], refs[nd : 2 * nd]
    vT, acc, sc = refs[2 * nd :]
    s, g = geo.where(meta)
    ends = doc_ends(doc, s)
    heads = [(p, h) for p in range(NP) for h in range(2)]

    def flip(i, carry):
        rows = pl.ds(al(i * TK, TK), TK)
        for p in range(NP):
            t = jnp.transpose(v[p][rows, :])
            for h in range(2):
                b = (2 * p + h) * HR
                vT[b : b + HEAD_DIM, rows] = t[h * HEAD_DIM : (h + 1) * HEAD_DIM, :]
                vT[b + HEAD_DIM : b + HR, rows] = jnp.ones((16, TK), BF)
        return carry

    lax.fori_loop(0, L // TK, flip, 0)

    for di, d in enumerate(dlist):

        def q_step(i, carry):
            e = i // (BL // TQF)
            off = al(lax.rem(i, BL // TQF) * TQF, TQF)
            half = jnp.where(e == 0, s, 1 - s)
            q0 = al((half * G + lax.rem(g - d + G, G)) * BL + off, TQF)
            first, last = span_start(ends, q0), span_end(ends, q0 + TQF - 1, L)
            one = first == span_start(ends, q0 + TQF - 1)
            klo = first // TK
            khi = (last + TK - 1) // TK
            qm = []
            for p, h in heads:
                qt = q[p][pl.ds(q0, TQF), :] * jnp.asarray(HEAD_DIM ** (-0.5), BF)
                qm.append(jnp.where(head_mask(h, TQF), qt, jnp.zeros_like(qt)))
            acc[...] = jnp.zeros_like(acc)

            def scores(masked, j, ms):
                k0 = al(j * TK, TK)
                if masked:
                    bias = mask_bias(segk, segq, k0, q0, TQF)
                out = []
                for n, (p, h) in enumerate(heads):
                    st = nt(k[p][pl.ds(k0, TK), :], qm[n])
                    if masked:
                        st = st + bias
                    sc[n, pl.ds(k0, TK), :] = st
                    out.append(jnp.maximum(ms[n], jnp.max(st.reshape(TK // 8, 8, TQF), axis=0)))
                return tuple(out)

            ms = tuple(jnp.full((8, TQF), -3e38, F32) for _ in heads)
            for lo, hi, masked in ranges(first, last, one, klo, khi, TK):
                ms = lax.fori_loop(lo, hi, functools.partial(scores, masked), ms)
            ms = [jnp.max(m, axis=0, keepdims=True) for m in ms]
            ml = [m * LOG2E for m in ms]

            def values(j, c2):
                k0 = al(j * TK, TK)
                for n in range(len(heads)):
                    pr = jnp.exp2(sc[n, pl.ds(k0, TK), :] * LOG2E - ml[n])
                    hs = slice(n * HR, (n + 1) * HR)
                    acc[hs, :] += nn(vT[hs, pl.ds(k0, TK)], pr.astype(BF))
                return c2

            lax.fori_loop(klo, khi, values, 0)
            for p in range(NP):
                parts = []
                for n in (2 * p, 2 * p + 1):
                    ls = acc[n * HR + HEAD_DIM : n * HR + HEAD_DIM + 1, :]
                    parts.append(acc[n * HR : n * HR + HEAD_DIM, :] * (1.0 / ls))
                    lses[di][e, n : n + 1, pl.ds(off, TQF)] = ms[n] + jnp.log(ls)
                res = jnp.transpose(jnp.concatenate(parts, axis=0)).astype(BF)
                outs[di][p, e, pl.ds(off, TQF), :] = res
            return carry

        lax.fori_loop(0, 2 * BL // TQF, q_step, 0)


def attn_back_kernel(geo, p, meta, doc, segk, segq, q, k, v, *refs):
    G, L, BL = geo.G, geo.L, geo.BL
    lses, mixed, grads = refs[:G], refs[G : 2 * G], refs[2 * G : 3 * G]
    out = refs[3 * G]
    qm, gm, kT, dqT, delta, lse, dk, dv = refs[3 * G + 1 :]
    s, g = geo.where(meta)
    ends = doc_ends(doc, s)
    scale = HEAD_DIM ** (-0.5)
    for e in range(2):
        for d in range(G):
            base = geo.block(s, g, e, d) * BL

            def load(i, carry):
                src = pl.ds(al(i * 256, 256), 256)
                dst = pl.ds(al(base + i * 256, 256), 256)
                gt = grads[d][e, src, :]
                zero = jnp.zeros_like(gt)
                prod = jnp.transpose(gt.astype(F32) * mixed[d][p, e, src, :].astype(F32))
                qt = q[dst, :] * jnp.asarray(scale, BF)
                for h in range(2):
                    hs = slice(h * HEAD_DIM, (h + 1) * HEAD_DIM)
                    keep = head_mask(h, 256)
                    gm[h, dst, :] = jnp.where(keep, gt, zero)
                    qm[h, dst, :] = jnp.where(keep, qt, zero)
                    delta[h : h + 1, dst] = jnp.sum(prod[hs, :], axis=0, keepdims=True)
                lse[:, dst] = lses[d][e, :, src]
                kT[:, dst] = jnp.transpose(k[dst, :])
                dqT[:, dst] = jnp.zeros((PW, 256), F32)
                return carry

            lax.fori_loop(0, BL // 256, load, 0)

    def k_step(j, carry):
        k0 = al(j * TK, TK)
        first, last = span_start(ends, k0), span_end(ends, k0 + TK - 1, L)
        one = first == span_start(ends, k0 + TK - 1)
        qlo = first // TQ
        qhi = (last + TQ - 1) // TQ
        kt = k[pl.ds(k0, TK), :]
        vt = v[pl.ds(k0, TK), :]
        dk[...] = jnp.zeros_like(dk)
        dv[...] = jnp.zeros_like(dv)

        def q_step(masked, i, c2):
            q0 = al(i * TQ, TQ)
            qs = pl.ds(q0, TQ)
            if masked:
                bias = mask_bias(segk, segq, k0, q0, TQ)
            for h in range(2):
                hs = slice(h * HEAD_DIM, (h + 1) * HEAD_DIM)
                qh, gh = qm[h, qs, :], gm[h, qs, :]
                n = 2 * p + h
                st = nt(kt, qh) - lse[n : n + 1, qs]
                if masked:
                    st = st + bias
                pr = jnp.exp(st)
                ds = (pr * (nt(vt, gh) - delta[h : h + 1, qs])).astype(BF)
                dv[...] += nn(pr.astype(BF), gh)
                dk[...] += nn(ds, qh)
                dqT[hs, qs] += nn(kT[hs, pl.ds(k0, TK)], ds)
            return c2

        for lo, hi, masked in ranges(first, last, one, qlo, qhi, TQ):
            lax.fori_loop(lo, hi, functools.partial(q_step, masked), 0)
        out[pl.ds(k0, TK), PW : 2 * PW] = dk[...].astype(BF)
        out[pl.ds(k0, TK), 2 * PW : 3 * PW] = dv[...].astype(BF)
        return carry

    lax.fori_loop(0, L // TK, k_step, 0)

    def last_step(i, carry):
        rows = pl.ds(al(i * TQ, TQ), TQ)
        out[rows, 0:PW] = (jnp.transpose(dqT[:, rows]) * scale).astype(BF)
        return carry

    lax.fori_loop(0, L // TQ, last_step, 0)


def attend_call(geo, dlist, meta, doc, segs, q, k, v):
    NP, L, BL, nd = geo.NP, geo.L, geo.BL, len(dlist)
    share = nd / geo.G
    res = call(
        functools.partial(attn_kernel, geo, dlist),
        "attend",
        [(meta, SM), (doc, SM), (segs[0], VM), (segs[1], VM)] + [(t, VM) for t in (*q, *k, *v)],
        [sds((NP, 2, BL, PW), BF)] * nd + [sds((2, 8, BL), F32)] * nd,
        scratch=[
            pltpu.VMEM((2 * NP * HR, L), BF),
            pltpu.VMEM((2 * NP * HR, geo.TQ), F32),
            pltpu.VMEM((2 * NP, L, geo.TQ), F32),
        ],
        flops=int(2 * L * L * geo.HL * 4 * share),
        nbytes=L * geo.HL * 8,
        trans=int(L * L * NP * share),
    )
    return res[:nd], res[nd:]


def attend_back_call(geo, p, meta, doc, segs, q, k, v, lses, mixed, grads):
    L = geo.L
    return call(
        functools.partial(attn_back_kernel, geo, p),
        "attend_back",
        [(meta, SM), (doc, SM), (segs[0], VM), (segs[1], VM), (q, VM), (k, VM), (v, VM)]
        + [(t, VM) for t in (*lses, *mixed, *grads)],
        [sds((L, 3 * PW), BF)],
        scratch=[
            pltpu.VMEM((2, L, PW), BF),
            pltpu.VMEM((2, L, PW), BF),
            pltpu.VMEM((PW, L), BF),
            pltpu.VMEM((PW, L), F32),
            pltpu.VMEM((8, L), F32),
            pltpu.VMEM((8, L), F32),
            pltpu.VMEM((TK, PW), F32),
            pltpu.VMEM((TK, PW), F32),
        ],
        flops=2 * L * L * PW * 10,
        nbytes=L * PW * 20,
        trans=L * L,
    )[0]


def gelu_parts(u):
    phi = 0.5 + 0.5 * lax.erf(u * (2.0 ** -0.5))
    pdf = jnp.exp(-0.5 * (u * u)) * 0.3989422804014327
    return phi, pdf


def ffn_kernel(geo, meta, *refs):
    G, HL, D, FF, BL, T, NP = geo.G, geo.HL, geo.D, geo.FF, geo.BL, geo.T, geo.NP
    s, g = geo.where(meta)
    pairs = [(d, p) for d in range(G) for p in range(NP)]
    x0, x1, cot, cot1, mixb, gain, shift, upb, downb = refs[:9]
    refs = refs[9:]
    mixed, refs = refs[:G], refs[G:]
    nw = 8 if geo.fast else 3
    wts, refs = refs[:nw], refs[nw:]
    out_own, out_send, g_resid = refs[:3]
    refs = refs[3:]
    gmix, refs = refs[: G * NP], refs[G * NP :]
    ng = 2 if geo.fast else 3
    packs, refs = refs[:ng], refs[ng:]
    vec, refs = refs[0], refs[1:]
    resid, h2, ffn, gh2, act_s, gu_s, ga_s, mg = refs[:8]
    refs = refs[8:]
    if geo.fast:
        wo, wu, wd, wg, sems = refs
        x, z = meta[0], meta[2]
        y, c = meta[1] // 2, meta[1] % 2
        groups = [[], [], []]
        for quad in range(4):
            yy = y if quad < 2 else 1 - y
            hh = x if quad % 2 == 0 else 1 - x
            for cc in range(2):
                cl = 2 * yy + (c if cc == 0 else 1 - c)
                src = wts[quad * 2 + cc]
                for d in range(4):
                    zz = lax.rem(z - d + 4, 4)
                    groups[0].append(
                        pltpu.make_async_copy(
                            src.at[d, pl.ds(512, 64), :],
                            wo.at[pl.ds(al(zz * 128 + hh * 64, 64), 64), pl.ds(al(cl * 128, 128), 128)],
                            sems.at[0],
                        )
                    )
                    for b in range(4):
                        groups[1].append(
                            pltpu.make_async_copy(
                                src.at[d, pl.ds(b * 64, 64), :],
                                wu.at[
                                    pl.ds(al(zz * 128 + hh * 64, 64), 64),
                                    pl.ds(al(cl * 512 + b * 128, 128), 128),
                                ],
                                sems.at[1],
                            )
                        )
                    groups[2].append(
                        pltpu.make_async_copy(
                            src.at[d, pl.ds(256, 256), :],
                            wd.at[pl.ds(al(zz * 512 + hh * 256, 256), 256), pl.ds(al(cl * 128, 128), 128)],
                            sems.at[2],
                        )
                    )
        for group in groups:
            for cpy in group:
                cpy.start()
        for cpy in groups[0]:
            cpy.wait()
    else:
        wo, wu, wd = wts
        (wg,) = refs

    zrow = jnp.zeros((1, D), F32)
    vec[...] = jnp.zeros_like(vec)

    for e in range(2):
        xe = x0 if e == 0 else x1
        ce = cot if e == 0 else cot1

        def first(i, carry):
            rows = pl.ds(al(i * RT, RT), RT)
            to = pl.ds(al(e * BL + i * RT, RT), RT)
            r = xe[rows, :].astype(F32) + mixb[...]
            for d, p in pairs:
                gp = lax.rem(g - d + G, G)
                r = r + nn(mixed[d][p, e, rows, :], wo[pl.ds(al(gp * HL + p * PW, 128), PW), :])
            resid[to, :] = r
            xhat, _ = normed(r)
            h2[to, :] = (xhat * gain[...] + shift[...]).astype(BF)
            ffn[to, :] = jnp.zeros((RT, D), F32)
            gh2[to, :] = jnp.zeros((RT, D), F32)
            return carry

        lax.fori_loop(0, BL // RT, first, 0)
    ga_s[0:BL, :] = cot[...]
    ga_s[BL:T, :] = cot1[...]
    if geo.fast:
        for group in groups[1:]:
            for cpy in group:
                cpy.wait()

    def chunk(f, carry):
        f0 = al(f * FC, FC)
        fs = pl.ds(f0, FC)

        def rows_step(i, hs):
            rows = pl.ds(al(i * RT, RT), RT)
            u = nn(h2[rows, :], wu[:, fs]) + upb[:, fs]
            phi, pdf = gelu_parts(u)
            act = (u * phi).astype(BF)
            gu = (nt(ga_s[rows, :], wd[fs, :]) * (phi + u * pdf)).astype(BF)
            act_s[rows, :] = act
            gu_s[rows, :] = gu
            ffn[rows, :] += nn(act, wd[fs, :])
            gh2[rows, :] += nt(gu, wu[:, fs])
            return hs + jnp.sum(gu.astype(F32), axis=0, keepdims=True)

        hsum = lax.fori_loop(0, T // RT, rows_step, jnp.zeros((1, FC), F32))
        per = D // FC
        vec[pl.ds(8 + f // per, 1), pl.ds(al(lax.rem(f, per) * FC, 128), FC)] = hsum
        dn = tn(act_s[...], ga_s[...])
        if geo.fast:
            wg[...] = dn.astype(BF)
            zr = lax.rem(f - z + 4, 4)
            for cr in range(2):
                for yr in range(2):
                    cl = 2 * (y if yr == 0 else 1 - y) + (c if cr == 0 else 1 - c)
                    for hr in range(2):
                        hh = x if hr == 0 else 1 - x
                        packs[cr][yr * 2 + hr, zr, 256:512, :] = wg[
                            pl.ds(al(hh * 256, 256), 256), pl.ds(al(cl * 128, 128), 128)
                        ]
        else:
            packs[1][fs, :] = dn.astype(BF)
        up = tn(h2[...], gu_s[...])
        if geo.fast:
            wg[...] = up.astype(BF)
            fy, fcr = f // 2, lax.rem(f, 2)
            yr = jnp.where(fy == y, 0, 1)
            for cr in range(2):
                @pl.when((fcr == c) if cr == 0 else (fcr != c))
                def _():
                    for hr in range(2):
                        hh = x if hr == 0 else 1 - x
                        for k in range(4):
                            zz = lax.rem(z + k, 4)
                            for b in range(4):
                                packs[cr][yr * 2 + hr, k, b * 64 : b * 64 + 64, :] = wg[
                                    pl.ds(al(zz * 128 + hh * 64, 64), 64), b * 128 : b * 128 + 128
                                ]
        else:
            packs[0][:, fs] = up.astype(BF)
        return carry

    lax.fori_loop(0, FF // FC, chunk, 0)

    sums = (zrow, zrow, zrow, zrow)
    for e in range(2):
        ce = cot if e == 0 else cot1
        oe = out_own if e == 0 else out_send

        def back(i, carry):
            mb, fg, fs_, db = carry
            rows = pl.ds(al(i * RT, RT), RT)
            to = pl.ds(al(e * BL + i * RT, RT), RT)
            r = resid[to, :]
            oe[rows, :] = (r + ffn[to, :] + downb[...]).astype(BF)
            xhat, rstd = normed(r)
            gh = gh2[to, :]
            ct = ce[rows, :].astype(F32)
            gx = gh * gain[...]
            gr = ct + rstd * (
                gx
                - jnp.mean(gx, axis=-1, keepdims=True)
                - xhat * jnp.mean(gx * xhat, axis=-1, keepdims=True)
            )
            g_resid[to, :] = gr
            ga = gr.astype(BF)
            gu_s[to, 0:D] = ga
            for n, (d, p) in enumerate(pairs):
                gp = lax.rem(g + d, G)
                gmix[n][e, rows, :] = nt(ga, wo[pl.ds(al(gp * HL + p * PW, 128), PW), :]).astype(BF)
            return (
                mb + jnp.sum(ga.astype(F32), axis=0, keepdims=True),
                fg + jnp.sum(gh * xhat, axis=0, keepdims=True),
                fs_ + jnp.sum(gh, axis=0, keepdims=True),
                db + jnp.sum(ct, axis=0, keepdims=True),
            )

        sums = lax.fori_loop(0, BL // RT, back, sums)
    for i in range(4):
        vec[4 + i : 5 + i, :] = sums[i]
    for d, p in pairs:
        gp = lax.rem(g - d + G, G)
        part = tn(mixed[d][p, 0], gu_s[0:BL, 0:D]) + tn(mixed[d][p, 1], gu_s[BL:T, 0:D])
        mg[pl.ds(al(gp * HL + p * PW, 128), PW), :] = part.astype(BF)
    if geo.fast:
        for cr in range(2):
            for yr in range(2):
                cl = 2 * (y if yr == 0 else 1 - y) + (c if cr == 0 else 1 - c)
                for hr in range(2):
                    hh = x if hr == 0 else 1 - x
                    for k in range(4):
                        zz = lax.rem(z + k, 4)
                        packs[cr][yr * 2 + hr, k, 512:576, :] = mg[
                            pl.ds(al(zz * 128 + hh * 64, 64), 64), pl.ds(al(cl * 128, 128), 128)
                        ]
    else:
        packs[2][...] = mg[...]


def put_vec(ref, base, v):
    hi = v.astype(BF)
    lo = (v - hi.astype(F32)).astype(BF)
    for n, t in enumerate((hi, lo)):
        for b in range(4):
            at = base + (n * 4 + b) * 16
            ref[at : at + 16, :] = t[:, b * 128 : b * 128 + 128]


def get_vec(ref, base):
    def term(n):
        at = base + n * 64
        return jnp.concatenate([ref[at + b * 16 : at + b * 16 + 16, :] for b in range(4)], axis=1).astype(F32)

    return term(0) + term(1)


def wgrad_kernel(geo, meta, vec_in, gain, shift, h1, *refs):
    G, HL, D, NP = geo.G, geo.HL, geo.D, geo.NP
    s, g = geo.where(meta)
    gq, w, refs = refs[:NP], refs[NP : 2 * NP], refs[2 * NP :]
    if geo.fast:
        a, b, c, d, *refs = refs
        refs[2][...] = add4(a[...], b[...], c[...], d[...]).astype(BF)
        refs = refs[:2] + refs[3:]
    packs, (wg, vec, acc) = refs[:-3], refs[-3:]
    vec[...] = vec_in[...]
    ones = jnp.ones((16, geo.L), BF)
    back = jnp.zeros((16, D), F32)
    for p in range(NP):
        part = tn(h1[...], gq[p][...])
        wg[:, p * 3 * PW : (p + 1) * 3 * PW] = part.astype(BF)
        prod = part * w[p][...].astype(F32)
        prod = prod[:, 0:PW] + prod[:, PW : 2 * PW] + prod[:, 2 * PW : 3 * PW]
        if p == 0:
            acc[...] = prod
        else:
            acc[...] += prod
        total = nn(ones, gq[p][...])
        hi = total.astype(BF)
        lo = (total - hi.astype(F32)).astype(BF)
        back = back + nt(hi, w[p][...]) + nt(lo, w[p][...])
        cols = pl.ds(al(g * HL + p * PW, 128), PW)
        vec[2:3, cols] = total[0:1, 0:PW]
        vec[3:4, cols] = total[0:1, 2 * PW : 3 * PW]
    first = jnp.sum(jnp.transpose(acc[...]), axis=0, keepdims=True)
    vec[0:1, :] = (first - shift[...] * back[0:1, :]) / gain[...]
    vec[1:2, :] = back[0:1, :]
    if geo.fast:
        x, z, c = meta[0], meta[2], meta[1] % 2
        for cr, table in ((0, KEEP_LB), (1, SEND_LB)):
            for b in range(3):
                lb = [(t[b] % 2) * 3 + t[b] // 2 for t in table]
                at = jnp.where(c == 0, lb[0], lb[1])
                for hr in range(2):
                    hh = x if hr == 0 else 1 - x
                    for k in range(4):
                        zz = lax.rem(z + k, 4)
                        to = ((b * 2 + hr) * 4 + k) * 64
                        packs[cr][to : to + 64, :] = wg[
                            pl.ds(al(zz * 128 + hh * 64, 64), 64), pl.ds(al(at * 128, 128), 128)
                        ]
            put_vec(packs[cr], 1536, vec[...])
    else:
        packs[1][...] = vec[...]
        packs[0][...] = jnp.zeros_like(packs[0])
        for p in range(NP):
            for part in range(3):
                packs[0][:, pl.ds(al(part * D + g * HL + p * PW, 128), PW)] = wg[
                    :, (3 * p + part) * PW : (3 * p + part + 1) * PW
                ]


def qkv_back_kernel(geo, meta, *refs):
    G, BL, NP = geo.G, geo.BL, geo.NP
    s, g = geo.where(meta)
    gq, w, ghs = refs[:NP], refs[NP : 2 * NP], refs[2 * NP :]
    for e in range(2):
        for d in range(G):
            base = geo.block(s, g, e, d) * BL

            def step(i, carry):
                rows = pl.ds(al(i * RT, RT), RT)
                at = pl.ds(al(base + i * RT, RT), RT)
                gh = nt(gq[0][at, :], w[0][...])
                for p in range(1, NP):
                    gh = gh + nt(gq[p][at, :], w[p][...])
                ghs[d][e, rows, :] = gh.astype(ghs[d].dtype)
                return carry

            lax.fori_loop(0, BL // RT, step, 0)


def last_kernel(geo, meta, gain, g_resid, gh, *refs):
    G, D, BL = geo.G, geo.D, geo.BL
    s, _ = geo.where(meta)
    recv, (x0, x1, out, send) = refs[: G - 1], refs[G - 1 :]
    for e in range(2):
        xe = x0 if e == 0 else x1

        def step(i, carry):
            rows = pl.ds(al(i * RT, RT), RT)
            to = pl.ds(al(e * BL + i * RT, RT), RT)
            xhat, rstd = normed(xe[rows, :].astype(F32))
            total = gh[e, rows, :]
            for r in recv:
                total = total + r[e, rows, :].astype(F32)
            gx = total * gain[...]
            res = g_resid[to, :] + rstd * (
                gx
                - jnp.mean(gx, axis=-1, keepdims=True)
                - xhat * jnp.mean(gx * xhat, axis=-1, keepdims=True)
            )
            if e == 0:
                out[s, rows, :] = res.astype(BF)
            else:
                send[rows, :] = res.astype(BF)
            return carry

        lax.fori_loop(0, BL // RT, step, 0)


def core_sum_kernel(own, recv, *outs):
    for q in range(4):
        outs[q][...] = (own[q].astype(F32) + recv[q].astype(F32)).astype(BF)


def arrange_kernel(geo, meta, keep, recv, *outs):
    y, c = meta[1] // 2, meta[1] % 2
    total = get_vec(keep, 1536) + get_vec(recv, 1536)
    for out in outs:
        put_vec(out, 768, total)
    for cs in range(2):
        mine = sorted((lb // 2) * 4 + 2 * cs + lb % 2 for lb in KEEP_LB[cs])
        theirs = sorted((lb // 2) * 4 + 2 * (1 - cs) + lb % 2 for lb in SEND_LB[1 - cs])
        for ys in range(2):
            @pl.when(jnp.logical_and(c == cs, y == ys))
            def _():
                for yr in range(2):
                    first = 3 * (2 * (ys ^ yr) + cs)
                    for o in range(3):
                        b = first + o
                        src, slot = (keep, mine.index(b)) if b in mine else (recv, theirs.index(b))
                        for hr in range(2):
                            for k in range(4):
                                at = ((slot * 2 + hr) * 4 + k) * 64
                                to = k * 192 + o * 64
                                outs[yr * 2 + hr][to : to + 64, :] = src[at : at + 64, :]


def add4(a, b, c, d):
    return (a.astype(F32) + b.astype(F32)) + (c.astype(F32) + d.astype(F32))


def plane_sum_kernel(a, b, c, d, *outs):
    for k in range(4):
        outs[k][...] = add4(a[k], b[k], c[k], d[k]).astype(BF)


def plane_sum_qkv_kernel(a, b, c, d, *outs):
    va, vb, vc, vd = (get_vec(t, 768) for t in (a, b, c, d))
    total = (va + vb) + (vc + vd)
    for k in range(4):
        at = slice(k * 192, k * 192 + 192)
        outs[k][0:192, :] = add4(a[at, :], b[at, :], c[at, :], d[at, :]).astype(BF)
        put_vec(outs[k], 192, total)


def line_sum_qkv_kernel(a, b, c, d, out, vec):
    va, vb, vc, vd = (get_vec(t, 192) for t in (a, b, c, d))
    vec[...] = (va + vc) + (vb + vd)
    out[...] = add4(a[0:192, :], b[0:192, :], c[0:192, :], d[0:192, :]).astype(BF)


def finish_kernel(meta, r, o, mix, up, down):
    x = meta[0]
    for src, h in ((r, x), (o, 1 - x)):
        rows = pl.ds(al(h * 64, 64), 64)
        for b in range(4):
            up[rows, b * 128 : b * 128 + 128] = src[b * 64 : b * 64 + 64, :].astype(F32)
        down[pl.ds(al(h * 256, 256), 256), :] = src[256:512, :].astype(F32)
        mix[rows, :] = src[512:576, :].astype(F32)


def finish_qkv_kernel(meta, r, o, qkv):
    x = meta[0]
    for src, h in ((r, x), (o, 1 - x)):
        for b in range(3):
            qkv[pl.ds(al(h * 64, 64), 64), b * 128 : b * 128 + 128] = src[b * 64 : b * 64 + 64, :].astype(F32)


def pack_kernel(meta, mix, up, down, rest):
    h = meta[0]
    rows = pl.ds(al(h * 64, 64), 64)
    for b in range(4):
        rest[b * 64 : b * 64 + 64, :] = up[rows, b * 128 : b * 128 + 128].astype(BF)
    rest[256:512, :] = down[pl.ds(al(h * 256, 256), 256), :].astype(BF)
    rest[512:576, :] = mix[rows, :].astype(BF)


def body(
    tokens,
    doc_lengths,
    norm_gain,
    norm_shift,
    qkv_weight,
    query_bias,
    value_bias,
    mix_weight,
    mix_bias,
    ffn_gain,
    ffn_shift,
    up_weight,
    up_bias,
    down_weight,
    down_bias,
    cotangent,
):
    DP, C, R = lax.axis_size("dp"), lax.axis_size("col"), lax.axis_size("row")
    _, BL, D = tokens.shape
    FF = up_bias.shape[0]
    geo = Geo(DP, C, R, BL, D, FF)
    G, HL, L, T = geo.G, geo.HL, geo.L, geo.T
    ix, ic, iz = lax.axis_index("dp"), lax.axis_index("col"), lax.axis_index("row")
    s = ic // G
    meta = jnp.stack([ix, ic, iz]).astype(jnp.int32)

    def swap_half(v):
        return lax.ppermute(v, "col", [(i, (i + G) % C) for i in range(C)])

    def turn(v, d):
        return lax.ppermute(v, "col", [(i, (i // G) * G + (i % G + d) % G) for i in range(C)])

    def plane(v, dx, dy):
        pairs = [
            (i * C + j, ((i + dx) % 2) * C + (j + dy * G) % C) for i in range(2) for j in range(C)
        ]
        return lax.ppermute(v, ("dp", "col"), pairs)

    def line(v, d):
        return lax.ppermute(v, "row", [(i, (i + d) % R) for i in range(R)])

    def row2(v):
        return v.reshape(1, v.shape[0])

    def pick(v, i):
        return lax.dynamic_index_in_dim(v, i, 0, keepdims=False)

    def after(v, dep):
        return lax.optimization_barrier((v, dep))[0]

    NP = geo.NP
    if geo.fast:
        def lines(v):
            return [v] + [line(v, d) for d in range(1, 4)]

        wq = qkv_weight.astype(BF)
        lines_qkv = lines(wq)
        x0 = pick(after(tokens, wq), s)
        x1 = swap_half(pick(after(tokens, wq), 1 - s))
        (half_rest,) = call(
            pack_kernel,
            "pack",
            [(after(meta, wq), SM), (mix_weight, VM), (up_weight, VM), (down_weight, VM)],
            [sds((576, 128), BF)],
            nbytes=2 << 20,
        )
        cot1 = swap_half(pick(after(cotangent, wq), 1 - s))
        own_qkv = jnp.stack(after(tuple(lines_qkv), half_rest))
        turns = [turn(after(t, own_qkv), 1) for t in (x0, x1)]
        across = swap_half(own_qkv)
        lines_rest = lines(after(half_rest, (own_qkv, *turns)))
    else:
        x0 = pick(tokens, s)
        x1 = swap_half(pick(tokens, 1 - s))

        def whole(w):
            w = lax.all_gather(w.astype(BF), "row", axis=0, tiled=True)
            return lax.all_gather(w, "col", axis=1, tiled=True)

        w_qkv = [whole(qkv_weight)]
        w_rest = [whole(mix_weight), whole(up_weight), whole(down_weight)]
    if geo.fast:
        pieces = [x0, turns[0], x1, turns[1]]
    else:
        pieces = [x0] + [turn(x0, d) for d in range(1, G)] + [x1] + [turn(x1, d) for d in range(1, G)]
    gain1, shift1 = row2(norm_gain), row2(norm_shift)
    h1, segk, segq = call(
        functools.partial(norm_kernel, geo),
        "norm_one",
        [(meta, SM), (doc_lengths, SM), (gain1, VM), (shift1, VM)] + [(p, VM) for p in pieces],
        [sds((L, D), BF), sds((L, 128), jnp.int32), sds((8, L), jnp.int32)],
        flops=L * D * 10,
        nbytes=L * D * 4,
    )
    segs = (segk, segq)
    if geo.fast:
        own_turned = turn(after(own_qkv, h1), 1)
        w_qkv = [own_qkv, own_turned, across, turn(after(across, (h1, *lines_rest)), 1)]
    bias = row2(jnp.concatenate([query_bias, jnp.zeros_like(query_bias), value_bias]))
    wspec = HBM if geo.fast else VM
    res = call(
        functools.partial(qkv_kernel, geo),
        "qkv",
        [(meta, SM), (h1, VM), (bias, VM)] + [(w, wspec) for w in w_qkv],
        [sds((L, PW), BF)] * (3 * NP) + [sds((D, 3 * PW), BF)] * NP,
        scratch=[pltpu.VMEM((D, 3 * D), BF), pltpu.SemaphoreType.DMA(())] if geo.fast else [],
        flops=0,
        nbytes=0,
    )
    q, k, v, w_own = (res[n * NP : (n + 1) * NP] for n in range(4))
    cot0 = pick(cotangent, s)
    if not geo.fast:
        cot1 = swap_half(pick(cotangent, 1 - s))
    if geo.fast:
        rest = jnp.stack(after(tuple(lines_rest), (q[0], cot1)))
        quads_rest = [plane(rest, 1, 0), plane(rest, 0, 1), plane(rest, 1, 1)]
    far, lse_far = attend_call(geo, tuple(range(1, G)), meta, doc_lengths, segs, q, k, v)
    if geo.fast:
        w_rest = [rest, turn(rest, 1)]
        w_rest += [t for u in after(tuple(quads_rest[:2]), (far[0], w_rest[1])) for t in (u, turn(u, 1))]
        q_own = list(after(tuple(q), (far[0], w_rest[2], w_rest[4])))
    else:
        q_own = list(after(tuple(q), far[0]))
    own, lse_own = attend_call(geo, (0,), meta, doc_lengths, segs, q_own, k, v)
    if geo.fast:
        diag = after(quads_rest[2], own[0])
        w_rest += [diag, turn(diag, 1)]
    made = [own[0]] + list(far)
    lses = list(lse_own) + list(lse_far)
    mixed = [made[0]] + [turn(made[G - d], d) for d in range(1, G)]
    packs_out = (
        [sds((4, 4, 576, 128), BF)] * 2
        if geo.fast
        else [sds((D, FF), BF), sds((FF, D), BF), sds((D, D), BF)]
    )
    weights_scr = (
        [
            pltpu.VMEM((D, D), BF),
            pltpu.VMEM((D, FF), BF),
            pltpu.VMEM((FF, D), BF),
            pltpu.VMEM((FC, FC), BF),
            pltpu.SemaphoreType.DMA((3,)),
        ]
        if geo.fast
        else [pltpu.VMEM((8, 128), BF)]
    )
    res = call(
        functools.partial(ffn_kernel, geo),
        "ffn",
        [(meta, SM), (x0, VM), (x1, VM), (cot0, VM), (cot1, VM)]
        + [(row2(a), VM) for a in (mix_bias, ffn_gain, ffn_shift, up_bias, down_bias)]
        + [(m, VM) for m in mixed]
        + [(w, wspec) for w in w_rest],
        [sds((BL, D), BF), sds((BL, D), BF), sds((T, D), F32)]
        + [sds((2, BL, PW), BF)] * (G * NP)
        + packs_out
        + [sds((16, D), F32)],
        scratch=[
            pltpu.VMEM((T, D), F32),
            pltpu.VMEM((T, D), BF),
            pltpu.VMEM((T, D), F32),
            pltpu.VMEM((T, D), F32),
            pltpu.VMEM((T, FC), BF),
            pltpu.VMEM((T, FC), BF),
            pltpu.VMEM((T, D), BF),
            pltpu.VMEM((D, D), BF),
        ]
        + weights_scr,
        flops=6 * T * D * (2 * FF + D),
        nbytes=20 << 20,
        trans=2 * T * FF,
    )
    out_own, out_send, g_resid = res[:3]
    gmix = [res[3 + d * NP : 3 + (d + 1) * NP] for d in range(G)]
    packs = res[3 + G * NP : -1]
    vec1 = res[-1]

    def back(p, q_p):
        return attend_back_call(
            geo, p, meta, doc_lengths, segs, q_p, k[p], v[p], lses, made, ghead[p]
        )

    def turned(p, dep):
        return [gmix[0][p]] + [turn(after(gmix[d][p], dep), d) for d in range(1, G)]

    def step_plane(parts):
        return (parts[0], plane(parts[1], 1, 0), plane(parts[2], 0, 1), plane(parts[3], 1, 1))

    def step_line(parts):
        return (parts[0],) + tuple(line(parts[d], d) for d in range(1, 4))

    def add(kernel, name, arrays, outs):
        return call(kernel, name, [(t, VM) for t in arrays], outs, nbytes=4 << 20)

    if geo.fast:
        sums = add(core_sum_kernel, "core_sum", (packs[0], turn(packs[1], 1)), [sds((4, 576, 128), BF)] * 4)
        a1 = step_plane(sums)
        ghead = [turned(0, sums[0])]
        gq = [back(0, after(q[0], sums[0]))]
        q1 = add(plane_sum_kernel, "plane_sum", after(a1, gq[0]), [sds((576, 128), BF)] * 4)
        b1 = step_line(q1)
        out_recv = swap_half(after(out_send, q1[0]))
        ghead.append(turned(1, q1[0]))
        gq += [back(1, after(q[1], q1[0]))]
        packs2_out = [sds((1664, 128), BF)] * 2 + [sds((576, 128), BF)]
    else:
        b1 = ()
        ghead = [turned(p, q[p]) for p in range(NP)]
        gq = [back(p, q[p]) for p in range(NP)]
        out_recv = swap_half(out_send)
        packs2_out = [sds((D, 3 * D), BF), sds((16, D), F32)]
    packs2 = call(
        functools.partial(wgrad_kernel, geo),
        "wgrad",
        [(meta, SM), (vec1, VM), (gain1, VM), (shift1, VM), (after(h1, out_recv), VM)]
        + [(t, VM) for t in (*gq, *w_own, *b1)],
        packs2_out,
        scratch=[pltpu.VMEM((D, 3 * HL), BF), pltpu.VMEM((16, D), F32), pltpu.VMEM((D, PW), F32)],
        flops=2 * L * D * 3 * HL,
        nbytes=8 << 20,
    )
    if geo.fast:
        recv2, r1 = turn(packs2[1], 1), packs2[2]
        gq = list(after(tuple(gq), r1))
    ghs = call(
        functools.partial(qkv_back_kernel, geo),
        "qkv_back",
        [(meta, SM)] + [(t, VM) for t in (*gq, *w_own)],
        [sds((2, BL, D), F32)] + [sds((2, BL, D), BF)] * (G - 1),
        flops=2 * L * D * 3 * HL,
        nbytes=12 << 20,
    )
    gh_recv = [turn(ghs[G - d], d) for d in range(1, G)]
    if geo.fast:
        own2, recv2 = after((packs2[0], recv2), ghs[0])
        parts2 = call(
            functools.partial(arrange_kernel, geo),
            "arrange",
            [(meta, SM), (own2, VM), (recv2, VM)],
            [sds((896, 128), BF)] * 4,
            nbytes=2 << 20,
        )
        a2 = step_plane(parts2)
        other1 = plane(after(r1, parts2[0]), 1, 0)

    tgrad, tgrad_send = call(
        functools.partial(last_kernel, geo),
        "norm_back",
        [(meta, SM), (gain1, VM), (g_resid, VM), (after(ghs[0], parts2[0]) if geo.fast else ghs[0], VM)]
        + [(r, VM) for r in gh_recv]
        + [(x0, VM), (x1, VM)],
        [sds((2, BL, D), BF), sds((BL, D), BF)],
        flops=T * D * 30,
        nbytes=8 << 20,
    )
    tgrad_recv = swap_half(tgrad_send)
    if geo.fast:
        q2 = add(plane_sum_qkv_kernel, "plane_sum_qkv", after(a2, tgrad_send), [sds((320, 128), BF)] * 4)
        b2 = step_line(q2)
        mix_g, up_g, down_g = call(
            finish_kernel,
            "finish",
            [(meta, SM), (after(r1, q2[0]), VM), (other1, VM)],
            [sds(w.shape, F32) for w in (mix_weight, up_weight, down_weight)],
            nbytes=2 << 20,
        )
        r2, vec = add(
            line_sum_qkv_kernel, "line_sum_qkv", after(b2, mix_g), [sds((192, 128), BF), sds((16, D), F32)]
        )
        (qkv_g,) = call(
            finish_qkv_kernel,
            "finish_qkv",
            [(meta, SM), (r2, VM), (plane(r2, 1, 0), VM)],
            [sds(qkv_weight.shape, F32)],
            nbytes=1 << 20,
        )
        grads = (qkv_g, mix_g, up_g, down_g)
    else:
        def reduced(w):
            w = lax.psum_scatter(w, "col", scatter_dimension=1, tiled=True)
            w = lax.psum_scatter(w, "row", scatter_dimension=0, tiled=True)
            return lax.psum(w, "dp").astype(F32)

        grads = (reduced(packs2[0]), reduced(packs[2]), reduced(packs[0]), reduced(packs[1]))
        vec = lax.psum(packs2[1], ("dp", "col", "row"))

    def join(own, other):
        return lax.dynamic_update_slice(own, other[None], (1 - s, 0, 0))

    out_pair = jnp.where(s == 0, jnp.stack([out_own, out_recv]), jnp.stack([out_recv, out_own]))
    tgrad = join(tgrad, tgrad_recv)
    return (
        out_pair,
        tgrad,
        *grads,
        vec[:8],
        vec[8 : 8 + FF // D].reshape(FF),
    )


def solution(mesh):
    return jax.shard_map(
        body,
        mesh=mesh,
        in_specs=(
            P(("dp", "row"), "col", None),
            P(("dp", "row"), None),
            P(),
            P(),
            P("row", "col"),
            P(),
            P(),
            P("row", "col"),
            P(),
            P(),
            P(),
            P("row", "col"),
            P(),
            P("row", "col"),
            P(),
            P(("dp", "row"), "col", None),
        ),
        out_specs=(
            P(("dp", "row"), "col", None),
            P(("dp", "row"), "col", None),
            P("row", "col"),
            P("row", "col"),
            P("row", "col"),
            P("row", "col"),
            P(),
            P(),
        ),
        check_vma=False,
    )
```

```python
import functools

import jax
import jax.numpy as jnp
from jax import lax
from jax.experimental import pallas as pl
from jax.experimental.pallas import tpu as pltpu
from jax.sharding import PartitionSpec as P

HEAD_DIM = 64
EPS = 1e-05
NEG = -1e30
LOG2E = 1.4426950408889634
PW = 128

BF = jnp.bfloat16
F32 = jnp.float32
VM = pl.BlockSpec(memory_space=pltpu.VMEM)
SM = pl.BlockSpec(memory_space=pltpu.SMEM)
HBM = pl.BlockSpec(memory_space=pl.ANY)
TQ = 256
TK = 256
FC = 512
RT = 256
KEEP_LB = ((0, 1, 4), (1, 4, 5))
SEND_LB = ((2, 3, 5), (0, 2, 3))


def sds(shape, dtype):
    return jax.ShapeDtypeStruct(shape, dtype)


NEAR = ('core_sum', 'plane_sum', 'arrange', 'plane_sum_qkv', 'line_sum_qkv', 'finish', 'finish_qkv', 'token_back')


def near(a):
    return pltpu.with_memory_space_constraint(a, pltpu.VMEM)


def call(kernel, name, ins, outs, scratch=(), flops=0, nbytes=0, trans=0, **kw):
    return pl.pallas_call(
        kernel,
        name=name,
        out_shape=tuple(o for o in outs),
        in_specs=[spec for _, spec in ins],
        out_specs=tuple(VM for _ in outs),
        scratch_shapes=list(scratch),
        compiler_params=pltpu.CompilerParams(vmem_limit_bytes=36 * 1024 * 1024, **kw),
        cost_estimate=pl.CostEstimate(flops=flops, bytes_accessed=nbytes, transcendentals=trans),
    )(*[near(a) if spec is VM and name in NEAR and a.ndim > 1 else a for a, spec in ins])


def nt(a, b):
    return lax.dot_general(a, b, (((1,), (1,)), ((), ())), preferred_element_type=F32)


def nn(a, b):
    return lax.dot_general(a, b, (((1,), (0,)), ((), ())), preferred_element_type=F32)


def tn(a, b):
    return lax.dot_general(a, b, (((0,), (0,)), ((), ())), preferred_element_type=F32)


def al(value, unit):
    return pl.multiple_of(value, unit)


def normed(v):
    mean = jnp.mean(v, axis=-1, keepdims=True)
    center = v - mean
    rstd = lax.rsqrt(jnp.mean(center * center, axis=-1, keepdims=True) + EPS)
    return center * rstd, rstd


class Geo:
    def __init__(self, dp, col, row, block_len, width, hidden):
        self.dp, self.C, self.R = dp, col, row
        self.G = col // 2
        self.BL = block_len
        self.L = block_len * col
        self.T = 2 * block_len
        self.D = width
        self.FF = hidden
        self.HL = width // self.G
        self.NP = self.HL // PW
        self.TQ = min(512, block_len)
        self.fast = (
            dp == 2 and col == 4 and row == 4 and width == 512 and hidden == 2048 and block_len % 256 == 0
        )

    def where(self, meta):
        col = meta[1]
        return col // self.G, col % self.G

    def block(self, s, g, e, d):
        half = s if e == 0 else 1 - s
        return half * self.G + lax.rem(g - d + self.G, self.G)


def norm_kernel(geo, meta, doc, gain, shift, *refs):
    s, g = geo.where(meta)
    pieces, (out, segk, segq) = refs[:-3], refs[-3:]
    fill_segments(geo, doc_ends(doc, s), segk, segq)
    for e in range(2):
        for d in range(geo.G):
            src = pieces[e * geo.G + d]
            base = geo.block(s, g, e, d) * geo.BL

            def step(i, carry):
                v = src[pl.ds(al(i * 128, 128), 128), :].astype(F32)
                xhat, _ = normed(v)
                out[pl.ds(al(base + i * 128, 128), 128), :] = (xhat * gain[...] + shift[...]).astype(BF)
                return carry

            lax.fori_loop(0, geo.BL // 128, step, 0, unroll=2)


def qkv_kernel(geo, meta, h1, bias, *refs):
    s, g = geo.where(meta)
    HL, D, NP = geo.HL, geo.D, geo.NP
    no = (3 + geo.G) * NP
    outs = refs[-no - 2 : -2] if geo.fast else refs[-no:]
    if geo.fast:
        pieces, (wscr, sem) = refs[:4], refs[-2:]
        z = meta[2]
        y, c = meta[1] // 2, meta[1] % 2
        copies = []
        for n in range(4):
            yy = y if n < 2 else 1 - y
            cp = c if n % 2 == 0 else 1 - c
            for d in range(4):
                zz = lax.rem(z - d + 4, 4)
                copies.append(
                    pltpu.make_async_copy(
                        pieces[n].at[d],
                        wscr.at[pl.ds(al(zz * 128, 128), 128), pl.ds(al((2 * yy + cp) * 384, 128), 384)],
                        sem,
                    )
                )
        for cpy in copies:
            cpy.start()
        for cpy in copies:
            cpy.wait()
    else:
        wscr = refs[0]

    def cols(part, p):
        return pl.ds(al(part * D + g * HL + p * PW, 128), PW)

    for d in range(geo.G):
        gd = lax.rem(g - d + geo.G, geo.G)
        for p in range(NP):
            for part in range(3):
                at = pl.ds(al(part * D + gd * HL + p * PW, 128), PW)
                outs[(3 + d) * NP + p][:, part * PW : (part + 1) * PW] = wscr[:, at]

    def step(i, carry):
        rows = pl.ds(al(i * 256, 256), 256)
        a = h1[rows, :]
        for p in range(NP):
            res = nn(a, outs[3 * NP + p][...])
            for part in range(3):
                outs[part * NP + p][rows, :] = (
                    res[:, part * PW : (part + 1) * PW] + bias[:, cols(part, p)]
                ).astype(BF)
        return carry

    lax.fori_loop(0, geo.L // 256, step, 0)


def doc_ends(doc, s):
    ends, total = [], 0
    for i in range(8):
        total = total + doc[s, i]
        ends.append(total)
    return ends


def span_start(ends, t):
    best = 0
    for e in ends:
        best = jnp.where(e <= t, e, best)
    return best


def span_end(ends, t, full):
    best = full
    for e in reversed(ends):
        best = jnp.where(e > t, e, best)
    return best


def fill_segments(geo, ends, segk, segq):
    def step(i, carry):
        rows = lax.broadcasted_iota(jnp.int32, (TK, 128), 0) + i * TK
        cols = lax.broadcasted_iota(jnp.int32, (8, TQ), 1) + i * TQ
        a = jnp.zeros((TK, 128), jnp.int32)
        b = jnp.zeros((8, TQ), jnp.int32)
        for e in ends:
            a += (rows >= e).astype(jnp.int32)
            b += (cols >= e).astype(jnp.int32)
        segk[pl.ds(al(i * TK, TK), TK), :] = a
        segq[:, pl.ds(al(i * TQ, TQ), TQ)] = b
        return carry

    lax.fori_loop(0, geo.L // TK, step, 0)


def mask_bias(segk, segq, k0, q0, tq):
    a = segk[pl.ds(k0, TK), :]
    b = segq[0:1, pl.ds(q0, tq)]
    same = jnp.concatenate([a] * (tq // 128), axis=1) == b
    return jnp.where(same, 0.0, NEG)


def head_mask(h, rows):
    lane = lax.broadcasted_iota(jnp.int32, (rows, PW), 1)
    return (lane // HEAD_DIM) == h


def ranges(first, last, one, lo, hi, tile):
    a = jnp.where(one, jnp.minimum((first + tile - 1) // tile, hi), hi)
    b = jnp.where(one, jnp.minimum(jnp.maximum(last // tile, a), hi), hi)
    return ((lo, a, True), (a, b, False), (b, hi, True))


HR = HEAD_DIM + 16


def attn_kernel(geo, dlist, meta, doc, segk, segq, *refs):
    G, NP, L, BL, TQF = geo.G, geo.NP, geo.L, geo.BL, geo.TQ
    q, k, v, refs = refs[:NP], refs[NP : 2 * NP], refs[2 * NP : 3 * NP], refs[3 * NP :]
    nd = len(dlist)
    outs, lses = refs[:nd], refs[nd : 2 * nd]
    vT, acc, sc = refs[2 * nd :]
    s, g = geo.where(meta)
    ends = doc_ends(doc, s)
    heads = [(p, h) for p in range(NP) for h in range(2)]

    def flip(i, carry):
        rows = pl.ds(al(i * TK, TK), TK)
        for p in range(NP):
            t = jnp.transpose(v[p][rows, :])
            for h in range(2):
                b = (2 * p + h) * HR
                vT[b : b + HEAD_DIM, rows] = t[h * HEAD_DIM : (h + 1) * HEAD_DIM, :]
                vT[b + HEAD_DIM : b + HR, rows] = jnp.ones((16, TK), BF)
        return carry

    lax.fori_loop(0, L // TK, flip, 0)

    for di, d in enumerate(dlist):

        def q_step(i, carry):
            e = i // (BL // TQF)
            off = al(lax.rem(i, BL // TQF) * TQF, TQF)
            half = jnp.where(e == 0, s, 1 - s)
            q0 = al((half * G + lax.rem(g - d + G, G)) * BL + off, TQF)
            first, last = span_start(ends, q0), span_end(ends, q0 + TQF - 1, L)
            one = first == span_start(ends, q0 + TQF - 1)
            klo = first // TK
            khi = (last + TK - 1) // TK
            qm = []
            for p, h in heads:
                qt = q[p][pl.ds(q0, TQF), :] * jnp.asarray(HEAD_DIM ** (-0.5), BF)
                qm.append(jnp.where(head_mask(h, TQF), qt, jnp.zeros_like(qt)))
            acc[...] = jnp.zeros_like(acc)

            def scores(masked, j, ms):
                k0 = al(j * TK, TK)
                if masked:
                    bias = mask_bias(segk, segq, k0, q0, TQF)
                out = []
                for n, (p, h) in enumerate(heads):
                    st = nt(k[p][pl.ds(k0, TK), :], qm[n])
                    if masked:
                        st = st + bias
                    sc[n, pl.ds(k0, TK), :] = st
                    out.append(jnp.maximum(ms[n], jnp.max(st.reshape(TK // 8, 8, TQF), axis=0)))
                return tuple(out)

            ms = tuple(jnp.full((8, TQF), -3e38, F32) for _ in heads)
            for lo, hi, masked in ranges(first, last, one, klo, khi, TK):
                ms = lax.fori_loop(lo, hi, functools.partial(scores, masked), ms)
            ms = [jnp.max(m, axis=0, keepdims=True) for m in ms]
            ml = [m * LOG2E for m in ms]

            def values(j, c2):
                k0 = al(j * TK, TK)
                for n in range(len(heads)):
                    pr = jnp.exp2(sc[n, pl.ds(k0, TK), :] * LOG2E - ml[n])
                    hs = slice(n * HR, (n + 1) * HR)
                    acc[hs, :] += nn(vT[hs, pl.ds(k0, TK)], pr.astype(BF))
                return c2

            lax.fori_loop(klo, khi, values, 0)
            for p in range(NP):
                parts = []
                for n in (2 * p, 2 * p + 1):
                    ls = acc[n * HR + HEAD_DIM : n * HR + HEAD_DIM + 1, :]
                    parts.append(acc[n * HR : n * HR + HEAD_DIM, :] * (1.0 / ls))
                    lses[di][e, n : n + 1, pl.ds(off, TQF)] = ms[n] + jnp.log(ls)
                res = jnp.transpose(jnp.concatenate(parts, axis=0)).astype(BF)
                outs[di][p, e, pl.ds(off, TQF), :] = res
            return carry

        lax.fori_loop(0, 2 * BL // TQF, q_step, 0)


def attn_back_kernel(geo, p, meta, doc, segk, segq, q, k, v, *refs):
    G, L, BL = geo.G, geo.L, geo.BL
    lses, mixed, grads = refs[:G], refs[G : 2 * G], refs[2 * G : 3 * G]
    out, sends = refs[3 * G], refs[3 * G + 1 : 4 * G]
    qm, gm, kT, dqT, delta, lse, dk, dv = refs[4 * G :]
    s, g = geo.where(meta)
    ends = doc_ends(doc, s)
    scale = HEAD_DIM ** (-0.5)
    for e in range(2):
        for d in range(G):
            base = geo.block(s, g, e, d) * BL

            def load(i, carry):
                src = pl.ds(al(i * 256, 256), 256)
                dst = pl.ds(al(base + i * 256, 256), 256)
                gt = grads[d][e, src, :]
                zero = jnp.zeros_like(gt)
                prod = jnp.transpose(gt.astype(F32) * mixed[d][p, e, src, :].astype(F32))
                qt = q[dst, :] * jnp.asarray(scale, BF)
                for h in range(2):
                    hs = slice(h * HEAD_DIM, (h + 1) * HEAD_DIM)
                    keep = head_mask(h, 256)
                    gm[h, dst, :] = jnp.where(keep, gt, zero)
                    qm[h, dst, :] = jnp.where(keep, qt, zero)
                    delta[h : h + 1, dst] = jnp.sum(prod[hs, :], axis=0, keepdims=True)
                lse[:, dst] = lses[d][e, :, src]
                kT[:, dst] = jnp.transpose(k[dst, :])
                dqT[:, dst] = jnp.zeros((PW, 256), F32)
                return carry

            lax.fori_loop(0, BL // 256, load, 0)

    def k_step(j, carry):
        k0 = al(j * TK, TK)
        first, last = span_start(ends, k0), span_end(ends, k0 + TK - 1, L)
        one = first == span_start(ends, k0 + TK - 1)
        qlo = first // TQ
        qhi = (last + TQ - 1) // TQ
        kt = k[pl.ds(k0, TK), :]
        vt = v[pl.ds(k0, TK), :]
        dk[...] = jnp.zeros_like(dk)
        dv[...] = jnp.zeros_like(dv)

        def q_step(masked, i, c2):
            q0 = al(i * TQ, TQ)
            qs = pl.ds(q0, TQ)
            if masked:
                bias = mask_bias(segk, segq, k0, q0, TQ)
            for h in range(2):
                hs = slice(h * HEAD_DIM, (h + 1) * HEAD_DIM)
                qh, gh = qm[h, qs, :], gm[h, qs, :]
                n = 2 * p + h
                st = nt(kt, qh) - lse[n : n + 1, qs]
                if masked:
                    st = st + bias
                pr = jnp.exp(st)
                ds = (pr * (nt(vt, gh) - delta[h : h + 1, qs])).astype(BF)
                dv[...] += nn(pr.astype(BF), gh)
                dk[...] += nn(ds, qh)
                dqT[hs, qs] += nn(kT[hs, pl.ds(k0, TK)], ds)
            return c2

        for lo, hi, masked in ranges(first, last, one, qlo, qhi, TQ):
            lax.fori_loop(lo, hi, functools.partial(q_step, masked), 0)
        out[pl.ds(k0, TK), PW : 2 * PW] = dk[...].astype(BF)
        out[pl.ds(k0, TK), 2 * PW : 3 * PW] = dv[...].astype(BF)
        return carry

    lax.fori_loop(0, L // TK, k_step, 0)

    def last_step(i, carry):
        rows = pl.ds(al(i * TQ, TQ), TQ)
        out[rows, 0:PW] = (jnp.transpose(dqT[:, rows]) * scale).astype(BF)
        return carry

    lax.fori_loop(0, L // TQ, last_step, 0)
    for d in range(1, G):
        for e in range(2):
            sends[d - 1][e] = out[pl.ds(al(geo.block(s, g, e, d) * BL, 256), BL), :]


def attend_call(geo, dlist, meta, doc, segs, q, k, v):
    NP, L, BL, nd = geo.NP, geo.L, geo.BL, len(dlist)
    share = nd / geo.G
    res = call(
        functools.partial(attn_kernel, geo, dlist),
        "attend",
        [(meta, SM), (doc, SM), (segs[0], VM), (segs[1], VM)] + [(t, VM) for t in (*q, *k, *v)],
        [sds((NP, 2, BL, PW), BF)] * nd + [sds((2, 8, BL), F32)] * nd,
        scratch=[
            pltpu.VMEM((2 * NP * HR, L), BF),
            pltpu.VMEM((2 * NP * HR, geo.TQ), F32),
            pltpu.VMEM((2 * NP, L, geo.TQ), F32),
        ],
        flops=int(2 * L * L * geo.HL * 4 * share),
        nbytes=L * geo.HL * 8,
        trans=int(L * L * NP * share),
    )
    return res[:nd], res[nd:]


def attend_back_call(geo, p, meta, doc, segs, q, k, v, lses, mixed, grads):
    L = geo.L
    return call(
        functools.partial(attn_back_kernel, geo, p),
        "attend_back",
        [(meta, SM), (doc, SM), (segs[0], VM), (segs[1], VM), (q, VM), (k, VM), (v, VM)]
        + [(t, VM) for t in (*lses, *mixed, *grads)],
        [sds((L, 3 * PW), BF)] + [sds((2, geo.BL, 3 * PW), BF)] * (geo.G - 1),
        scratch=[
            pltpu.VMEM((2, L, PW), BF),
            pltpu.VMEM((2, L, PW), BF),
            pltpu.VMEM((PW, L), BF),
            pltpu.VMEM((PW, L), F32),
            pltpu.VMEM((8, L), F32),
            pltpu.VMEM((8, L), F32),
            pltpu.VMEM((TK, PW), F32),
            pltpu.VMEM((TK, PW), F32),
        ],
        flops=2 * L * L * PW * 10,
        nbytes=L * PW * 20,
        trans=L * L,
    )


def gelu_parts(u):
    phi = 0.5 + 0.5 * lax.erf(u * (2.0 ** -0.5))
    pdf = jnp.exp(-0.5 * (u * u)) * 0.3989422804014327
    return phi, pdf


def ffn_kernel(geo, meta, *refs):
    G, HL, D, FF, BL, T, NP = geo.G, geo.HL, geo.D, geo.FF, geo.BL, geo.T, geo.NP
    s, g = geo.where(meta)
    pairs = [(d, p) for d in range(G) for p in range(NP)]
    x0, x1, cot, cot1, mixb, gain, shift, upb, downb = refs[:9]
    refs = refs[9:]
    mixed, refs = refs[:G], refs[G:]
    nw = 8 if geo.fast else 3
    wts, refs = refs[:nw], refs[nw:]
    out_own, out_send, g_resid = refs[:3]
    refs = refs[3:]
    gmix, refs = refs[: G * NP], refs[G * NP :]
    ng = 2 if geo.fast else 3
    packs, refs = refs[:ng], refs[ng:]
    vec, refs = refs[0], refs[1:]
    resid, h2, ffn, gh2, act_s, gu_s, ga_s, mg = refs[:8]
    refs = refs[8:]
    if geo.fast:
        wo, wu, wd, wg, sems = refs
        x, z = meta[0], meta[2]
        y, c = meta[1] // 2, meta[1] % 2
        groups = [[], [], []]
        for quad in range(4):
            yy = y if quad < 2 else 1 - y
            hh = x if quad % 2 == 0 else 1 - x
            for cc in range(2):
                cl = 2 * yy + (c if cc == 0 else 1 - c)
                src = wts[quad * 2 + cc]
                for d in range(4):
                    zz = lax.rem(z - d + 4, 4)
                    groups[0].append(
                        pltpu.make_async_copy(
                            src.at[d, pl.ds(512, 64), :],
                            wo.at[pl.ds(al(zz * 128 + hh * 64, 64), 64), pl.ds(al(cl * 128, 128), 128)],
                            sems.at[0],
                        )
                    )
                    for b in range(4):
                        groups[1].append(
                            pltpu.make_async_copy(
                                src.at[d, pl.ds(b * 64, 64), :],
                                wu.at[
                                    pl.ds(al(zz * 128 + hh * 64, 64), 64),
                                    pl.ds(al(cl * 512 + b * 128, 128), 128),
                                ],
                                sems.at[1],
                            )
                        )
                    groups[2].append(
                        pltpu.make_async_copy(
                            src.at[d, pl.ds(256, 256), :],
                            wd.at[pl.ds(al(zz * 512 + hh * 256, 256), 256), pl.ds(al(cl * 128, 128), 128)],
                            sems.at[2],
                        )
                    )
        for group in groups:
            for cpy in group:
                cpy.start()
        for cpy in groups[0]:
            cpy.wait()
    else:
        wo, wu, wd = wts
        (wg,) = refs

    zrow = jnp.zeros((1, D), F32)
    vec[...] = jnp.zeros_like(vec)

    for e in range(2):
        xe = x0 if e == 0 else x1
        ce = cot if e == 0 else cot1

        def first(i, carry):
            rows = pl.ds(al(i * RT, RT), RT)
            to = pl.ds(al(e * BL + i * RT, RT), RT)
            r = xe[rows, :].astype(F32) + mixb[...]
            for d, p in pairs:
                gp = lax.rem(g - d + G, G)
                r = r + nn(mixed[d][p, e, rows, :], wo[pl.ds(al(gp * HL + p * PW, 128), PW), :])
            resid[to, :] = r
            xhat, _ = normed(r)
            h2[to, :] = (xhat * gain[...] + shift[...]).astype(BF)
            ffn[to, :] = jnp.zeros((RT, D), F32)
            gh2[to, :] = jnp.zeros((RT, D), F32)
            return carry

        lax.fori_loop(0, BL // RT, first, 0)
    ga_s[0:BL, :] = cot[...]
    ga_s[BL:T, :] = cot1[...]
    if geo.fast:
        for group in groups[1:]:
            for cpy in group:
                cpy.wait()

    def chunk(f, carry):
        f0 = al(f * FC, FC)
        fs = pl.ds(f0, FC)

        def rows_step(i, hs):
            rows = pl.ds(al(i * RT, RT), RT)
            u = nn(h2[rows, :], wu[:, fs]) + upb[:, fs]
            phi, pdf = gelu_parts(u)
            act = (u * phi).astype(BF)
            gu = (nt(ga_s[rows, :], wd[fs, :]) * (phi + u * pdf)).astype(BF)
            act_s[rows, :] = act
            gu_s[rows, :] = gu
            ffn[rows, :] += nn(act, wd[fs, :])
            gh2[rows, :] += nt(gu, wu[:, fs])
            return hs + jnp.sum(gu.astype(F32), axis=0, keepdims=True)

        hsum = lax.fori_loop(0, T // RT, rows_step, jnp.zeros((1, FC), F32))
        per = D // FC
        vec[pl.ds(8 + f // per, 1), pl.ds(al(lax.rem(f, per) * FC, 128), FC)] = hsum
        dn = tn(act_s[...], ga_s[...])
        if geo.fast:
            wg[...] = dn.astype(BF)
            zr = lax.rem(f - z + 4, 4)
            for cr in range(2):
                for yr in range(2):
                    cl = 2 * (y if yr == 0 else 1 - y) + (c if cr == 0 else 1 - c)
                    for hr in range(2):
                        hh = x if hr == 0 else 1 - x
                        packs[cr][yr * 2 + hr, zr, 256:512, :] = wg[
                            pl.ds(al(hh * 256, 256), 256), pl.ds(al(cl * 128, 128), 128)
                        ]
        else:
            packs[1][fs, :] = dn.astype(BF)
        up = tn(h2[...], gu_s[...])
        if geo.fast:
            wg[...] = up.astype(BF)
            fy, fcr = f // 2, lax.rem(f, 2)
            yr = jnp.where(fy == y, 0, 1)
            for cr in range(2):
                @pl.when((fcr == c) if cr == 0 else (fcr != c))
                def _():
                    for hr in range(2):
                        hh = x if hr == 0 else 1 - x
                        for k in range(4):
                            zz = lax.rem(z + k, 4)
                            for b in range(4):
                                packs[cr][yr * 2 + hr, k, b * 64 : b * 64 + 64, :] = wg[
                                    pl.ds(al(zz * 128 + hh * 64, 64), 64), b * 128 : b * 128 + 128
                                ]
        else:
            packs[0][:, fs] = up.astype(BF)
        return carry

    lax.fori_loop(0, FF // FC, chunk, 0)

    sums = (zrow, zrow, zrow, zrow)
    for e in range(2):
        ce = cot if e == 0 else cot1
        oe = out_own if e == 0 else out_send

        def back(i, carry):
            mb, fg, fs_, db = carry
            rows = pl.ds(al(i * RT, RT), RT)
            to = pl.ds(al(e * BL + i * RT, RT), RT)
            r = resid[to, :]
            oe[rows, :] = (r + ffn[to, :] + downb[...]).astype(BF)
            xhat, rstd = normed(r)
            gh = gh2[to, :]
            ct = ce[rows, :].astype(F32)
            gx = gh * gain[...]
            gr = ct + rstd * (
                gx
                - jnp.mean(gx, axis=-1, keepdims=True)
                - xhat * jnp.mean(gx * xhat, axis=-1, keepdims=True)
            )
            g_resid[to, :] = gr
            ga = gr.astype(BF)
            gu_s[to, 0:D] = ga
            for n, (d, p) in enumerate(pairs):
                gp = lax.rem(g + d, G)
                gmix[n][e, rows, :] = nt(ga, wo[pl.ds(al(gp * HL + p * PW, 128), PW), :]).astype(BF)
            return (
                mb + jnp.sum(ga.astype(F32), axis=0, keepdims=True),
                fg + jnp.sum(gh * xhat, axis=0, keepdims=True),
                fs_ + jnp.sum(gh, axis=0, keepdims=True),
                db + jnp.sum(ct, axis=0, keepdims=True),
            )

        sums = lax.fori_loop(0, BL // RT, back, sums)
    for i in range(4):
        vec[4 + i : 5 + i, :] = sums[i]
    for d, p in pairs:
        gp = lax.rem(g - d + G, G)
        part = tn(mixed[d][p, 0], gu_s[0:BL, 0:D]) + tn(mixed[d][p, 1], gu_s[BL:T, 0:D])
        mg[pl.ds(al(gp * HL + p * PW, 128), PW), :] = part.astype(BF)
    if geo.fast:
        for cr in range(2):
            for yr in range(2):
                cl = 2 * (y if yr == 0 else 1 - y) + (c if cr == 0 else 1 - c)
                for hr in range(2):
                    hh = x if hr == 0 else 1 - x
                    for k in range(4):
                        zz = lax.rem(z + k, 4)
                        packs[cr][yr * 2 + hr, k, 512:576, :] = mg[
                            pl.ds(al(zz * 128 + hh * 64, 64), 64), pl.ds(al(cl * 128, 128), 128)
                        ]
    else:
        packs[2][...] = mg[...]


def put_vec(ref, base, v):
    hi = v.astype(BF)
    lo = (v - hi.astype(F32)).astype(BF)
    for n, t in enumerate((hi, lo)):
        for b in range(4):
            at = base + (n * 4 + b) * 16
            ref[at : at + 16, :] = t[:, b * 128 : b * 128 + 128]


def get_vec(ref, base):
    def term(n):
        at = base + n * 64
        return jnp.concatenate([ref[at + b * 16 : at + b * 16 + 16, :] for b in range(4)], axis=1).astype(F32)

    return term(0) + term(1)


def wgrad_kernel(geo, meta, vec_in, gain, shift, h1, *refs):
    G, HL, D, NP = geo.G, geo.HL, geo.D, geo.NP
    s, g = geo.where(meta)
    gq, w, refs = refs[:NP], refs[NP : 2 * NP], refs[2 * NP :]
    if geo.fast:
        a, b, c, d, *refs = refs
        refs[2][...] = add4(a[...], b[...], c[...], d[...]).astype(BF)
        refs = refs[:2] + refs[3:]
    packs, (wg, vec, acc) = refs[:-3], refs[-3:]
    vec[...] = vec_in[...]
    ones = jnp.ones((16, geo.L), BF)
    back = jnp.zeros((16, D), F32)
    for p in range(NP):
        part = tn(h1[...], gq[p][...])
        wg[:, p * 3 * PW : (p + 1) * 3 * PW] = part.astype(BF)
        prod = part * w[p][...].astype(F32)
        prod = prod[:, 0:PW] + prod[:, PW : 2 * PW] + prod[:, 2 * PW : 3 * PW]
        if p == 0:
            acc[...] = prod
        else:
            acc[...] += prod
        total = nn(ones, gq[p][...])
        hi = total.astype(BF)
        lo = (total - hi.astype(F32)).astype(BF)
        back = back + nt(hi, w[p][...]) + nt(lo, w[p][...])
        cols = pl.ds(al(g * HL + p * PW, 128), PW)
        vec[2:3, cols] = total[0:1, 0:PW]
        vec[3:4, cols] = total[0:1, 2 * PW : 3 * PW]
    first = jnp.sum(jnp.transpose(acc[...]), axis=0, keepdims=True)
    vec[0:1, :] = (first - shift[...] * back[0:1, :]) / gain[...]
    vec[1:2, :] = back[0:1, :]
    if geo.fast:
        x, z, c = meta[0], meta[2], meta[1] % 2
        for cr, table in ((0, KEEP_LB), (1, SEND_LB)):
            for b in range(3):
                lb = [(t[b] % 2) * 3 + t[b] // 2 for t in table]
                at = jnp.where(c == 0, lb[0], lb[1])
                for hr in range(2):
                    hh = x if hr == 0 else 1 - x
                    for k in range(4):
                        zz = lax.rem(z + k, 4)
                        to = ((b * 2 + hr) * 4 + k) * 64
                        packs[cr][to : to + 64, :] = wg[
                            pl.ds(al(zz * 128 + hh * 64, 64), 64), pl.ds(al(at * 128, 128), 128)
                        ]
            put_vec(packs[cr], 1536, vec[...])
    else:
        packs[1][...] = vec[...]
        packs[0][...] = jnp.zeros_like(packs[0])
        for p in range(NP):
            for part in range(3):
                packs[0][:, pl.ds(al(part * D + g * HL + p * PW, 128), PW)] = wg[
                    :, (3 * p + part) * PW : (3 * p + part + 1) * PW
                ]


def token_back_kernel(geo, meta, gain, g_resid, x0, x1, *refs):
    G, BL, NP = geo.G, geo.BL, geo.NP
    s, g = geo.where(meta)
    gq, recv, w = refs[:NP], refs[NP : G * NP], refs[G * NP : 2 * G * NP]
    out, send = refs[2 * G * NP :]
    for e in range(2):
        xe = x0 if e == 0 else x1
        base = geo.block(s, g, e, 0) * BL

        def step(i, carry):
            rows = pl.ds(al(i * RT, RT), RT)
            to = pl.ds(al(e * BL + i * RT, RT), RT)
            at = pl.ds(al(base + i * RT, RT), RT)
            total = nt(gq[0][at, :], w[0][...])
            for p in range(1, NP):
                total = total + nt(gq[p][at, :], w[p][...])
            for n, r in enumerate(recv):
                total = total + nt(r[e, rows, :], w[NP + n][...])
            xhat, rstd = normed(xe[rows, :].astype(F32))
            gx = total * gain[...]
            res = g_resid[to, :] + rstd * (
                gx
                - jnp.mean(gx, axis=-1, keepdims=True)
                - xhat * jnp.mean(gx * xhat, axis=-1, keepdims=True)
            )
            if e == 0:
                out[s, rows, :] = res.astype(BF)
            else:
                send[rows, :] = res.astype(BF)
            return carry

        lax.fori_loop(0, BL // RT, step, 0)


def core_sum_kernel(own, recv, *outs):
    for q in range(4):
        outs[q][...] = (own[q].astype(F32) + recv[q].astype(F32)).astype(BF)


def arrange_kernel(geo, meta, keep, recv, *outs):
    y, c = meta[1] // 2, meta[1] % 2
    total = get_vec(keep, 1536) + get_vec(recv, 1536)
    for out in outs:
        put_vec(out, 768, total)
    for cs in range(2):
        mine = sorted((lb // 2) * 4 + 2 * cs + lb % 2 for lb in KEEP_LB[cs])
        theirs = sorted((lb // 2) * 4 + 2 * (1 - cs) + lb % 2 for lb in SEND_LB[1 - cs])
        for ys in range(2):
            @pl.when(jnp.logical_and(c == cs, y == ys))
            def _():
                for yr in range(2):
                    first = 3 * (2 * (ys ^ yr) + cs)
                    for o in range(3):
                        b = first + o
                        src, slot = (keep, mine.index(b)) if b in mine else (recv, theirs.index(b))
                        for hr in range(2):
                            for k in range(4):
                                at = ((slot * 2 + hr) * 4 + k) * 64
                                to = k * 192 + o * 64
                                outs[yr * 2 + hr][to : to + 64, :] = src[at : at + 64, :]


def add4(a, b, c, d):
    return (a.astype(F32) + b.astype(F32)) + (c.astype(F32) + d.astype(F32))


def plane_sum_kernel(a, b, c, d, *outs):
    for k in range(4):
        outs[k][...] = add4(a[k], b[k], c[k], d[k]).astype(BF)


def plane_sum_qkv_kernel(a, b, c, d, *outs):
    va, vb, vc, vd = (get_vec(t, 768) for t in (a, b, c, d))
    total = (va + vb) + (vc + vd)
    for k in range(4):
        at = slice(k * 192, k * 192 + 192)
        outs[k][0:192, :] = add4(a[at, :], b[at, :], c[at, :], d[at, :]).astype(BF)
        put_vec(outs[k], 192, total)


def line_sum_qkv_kernel(a, b, c, d, out, vec):
    va, vb, vc, vd = (get_vec(t, 192) for t in (a, b, c, d))
    vec[...] = (va + vc) + (vb + vd)
    out[...] = add4(a[0:192, :], b[0:192, :], c[0:192, :], d[0:192, :]).astype(BF)


def finish_kernel(meta, r, o, mix, up, down):
    x = meta[0]
    for src, h in ((r, x), (o, 1 - x)):
        rows = pl.ds(al(h * 64, 64), 64)
        for b in range(4):
            up[rows, b * 128 : b * 128 + 128] = src[b * 64 : b * 64 + 64, :].astype(F32)
        down[pl.ds(al(h * 256, 256), 256), :] = src[256:512, :].astype(F32)
        mix[rows, :] = src[512:576, :].astype(F32)


def finish_qkv_kernel(meta, r, o, qkv):
    x = meta[0]
    for src, h in ((r, x), (o, 1 - x)):
        for b in range(3):
            qkv[pl.ds(al(h * 64, 64), 64), b * 128 : b * 128 + 128] = src[b * 64 : b * 64 + 64, :].astype(F32)


def pack_kernel(meta, mix, up, down, rest):
    h = meta[0]
    rows = pl.ds(al(h * 64, 64), 64)
    for b in range(4):
        rest[b * 64 : b * 64 + 64, :] = up[rows, b * 128 : b * 128 + 128].astype(BF)
    rest[256:512, :] = down[pl.ds(al(h * 256, 256), 256), :].astype(BF)
    rest[512:576, :] = mix[rows, :].astype(BF)


def body(
    tokens,
    doc_lengths,
    norm_gain,
    norm_shift,
    qkv_weight,
    query_bias,
    value_bias,
    mix_weight,
    mix_bias,
    ffn_gain,
    ffn_shift,
    up_weight,
    up_bias,
    down_weight,
    down_bias,
    cotangent,
):
    DP, C, R = lax.axis_size("dp"), lax.axis_size("col"), lax.axis_size("row")
    _, BL, D = tokens.shape
    FF = up_bias.shape[0]
    geo = Geo(DP, C, R, BL, D, FF)
    G, HL, L, T = geo.G, geo.HL, geo.L, geo.T
    ix, ic, iz = lax.axis_index("dp"), lax.axis_index("col"), lax.axis_index("row")
    s = ic // G
    meta = jnp.stack([ix, ic, iz]).astype(jnp.int32)

    def swap_half(v):
        return lax.ppermute(v, "col", [(i, (i + G) % C) for i in range(C)])

    def turn(v, d):
        return lax.ppermute(v, "col", [(i, (i // G) * G + (i % G + d) % G) for i in range(C)])

    def plane(v, dx, dy):
        pairs = [
            (i * C + j, ((i + dx) % 2) * C + (j + dy * G) % C) for i in range(2) for j in range(C)
        ]
        return lax.ppermute(v, ("dp", "col"), pairs)

    def line(v, d):
        return lax.ppermute(v, "row", [(i, (i + d) % R) for i in range(R)])

    def row2(v):
        return v.reshape(1, v.shape[0])

    def pick(v, i):
        return lax.dynamic_index_in_dim(v, i, 0, keepdims=False)

    def after(v, dep):
        return lax.optimization_barrier((v, dep))[0]

    NP = geo.NP
    if geo.fast:
        def lines(v):
            return [v] + [line(v, d) for d in range(1, 4)]

        wq = qkv_weight.astype(BF)
        lines_qkv = lines(wq)
        x0 = pick(after(tokens, wq), s)
        x1 = swap_half(pick(after(tokens, wq), 1 - s))
        (half_rest,) = call(
            pack_kernel,
            "pack",
            [(after(meta, wq), SM), (mix_weight, VM), (up_weight, VM), (down_weight, VM)],
            [sds((576, 128), BF)],
            nbytes=2 << 20,
        )
        cot1 = swap_half(pick(after(cotangent, wq), 1 - s))
        own_qkv = jnp.stack(after(tuple(lines_qkv), half_rest))
        turns = [turn(after(t, own_qkv), 1) for t in (x0, x1)]
        across = swap_half(own_qkv)
        lines_rest = lines(after(half_rest, (own_qkv, *turns)))
    else:
        x0 = pick(tokens, s)
        x1 = swap_half(pick(tokens, 1 - s))

        def whole(w):
            w = lax.all_gather(w.astype(BF), "row", axis=0, tiled=True)
            return lax.all_gather(w, "col", axis=1, tiled=True)

        w_qkv = [whole(qkv_weight)]
        w_rest = [whole(mix_weight), whole(up_weight), whole(down_weight)]
    if geo.fast:
        pieces = [x0, turns[0], x1, turns[1]]
    else:
        pieces = [x0] + [turn(x0, d) for d in range(1, G)] + [x1] + [turn(x1, d) for d in range(1, G)]
    gain1, shift1 = row2(norm_gain), row2(norm_shift)
    h1, segk, segq = call(
        functools.partial(norm_kernel, geo),
        "norm_one",
        [(meta, SM), (doc_lengths, SM), (gain1, VM), (shift1, VM)] + [(p, VM) for p in pieces],
        [sds((L, D), BF), sds((L, 128), jnp.int32), sds((8, L), jnp.int32)],
        flops=L * D * 10,
        nbytes=L * D * 4,
    )
    segs = (segk, segq)
    if geo.fast:
        own_turned = turn(after(own_qkv, h1), 1)
        w_qkv = [own_qkv, own_turned, across, turn(after(across, (h1, *lines_rest)), 1)]
    bias = row2(jnp.concatenate([query_bias, jnp.zeros_like(query_bias), value_bias]))
    wspec = HBM if geo.fast else VM
    res = call(
        functools.partial(qkv_kernel, geo),
        "qkv",
        [(meta, SM), (h1, VM), (bias, VM)] + [(w, wspec) for w in w_qkv],
        [sds((L, PW), BF)] * (3 * NP) + [sds((D, 3 * PW), BF)] * (G * NP),
        scratch=[pltpu.VMEM((D, 3 * D), BF), pltpu.SemaphoreType.DMA(())] if geo.fast else [],
        flops=0,
        nbytes=0,
    )
    q, k, v, w_own = (res[n * NP : (n + 1) * NP] for n in range(4))
    w_all = res[3 * NP :]
    cot0 = pick(cotangent, s)
    if not geo.fast:
        cot1 = swap_half(pick(cotangent, 1 - s))
    if geo.fast:
        rest = jnp.stack(after(tuple(lines_rest), (q[0], cot1)))
        quads_rest = [plane(rest, 1, 0), plane(rest, 0, 1), plane(rest, 1, 1)]
    far, lse_far = attend_call(geo, tuple(range(1, G)), meta, doc_lengths, segs, q, k, v)
    if geo.fast:
        w_rest = [rest, turn(rest, 1)]
        w_rest += [t for u in after(tuple(quads_rest[:2]), (far[0], w_rest[1])) for t in (u, turn(u, 1))]
        q_own = list(after(tuple(q), (far[0], w_rest[2], w_rest[4])))
    else:
        q_own = list(after(tuple(q), far[0]))
    own, lse_own = attend_call(geo, (0,), meta, doc_lengths, segs, q_own, k, v)
    if geo.fast:
        diag = after(quads_rest[2], own[0])
        w_rest += [diag, turn(diag, 1)]
    made = [own[0]] + list(far)
    lses = list(lse_own) + list(lse_far)
    mixed = [made[0]] + [turn(made[G - d], d) for d in range(1, G)]
    packs_out = (
        [sds((4, 4, 576, 128), BF)] * 2
        if geo.fast
        else [sds((D, FF), BF), sds((FF, D), BF), sds((D, D), BF)]
    )
    weights_scr = (
        [
            pltpu.VMEM((D, D), BF),
            pltpu.VMEM((D, FF), BF),
            pltpu.VMEM((FF, D), BF),
            pltpu.VMEM((FC, FC), BF),
            pltpu.SemaphoreType.DMA((3,)),
        ]
        if geo.fast
        else [pltpu.VMEM((8, 128), BF)]
    )
    res = call(
        functools.partial(ffn_kernel, geo),
        "ffn",
        [(meta, SM), (x0, VM), (x1, VM), (cot0, VM), (cot1, VM)]
        + [(row2(a), VM) for a in (mix_bias, ffn_gain, ffn_shift, up_bias, down_bias)]
        + [(m, VM) for m in mixed]
        + [(w, wspec) for w in w_rest],
        [sds((BL, D), BF), sds((BL, D), BF), sds((T, D), F32)]
        + [sds((2, BL, PW), BF)] * (G * NP)
        + packs_out
        + [sds((16, D), F32)],
        scratch=[
            pltpu.VMEM((T, D), F32),
            pltpu.VMEM((T, D), BF),
            pltpu.VMEM((T, D), F32),
            pltpu.VMEM((T, D), F32),
            pltpu.VMEM((T, FC), BF),
            pltpu.VMEM((T, FC), BF),
            pltpu.VMEM((T, D), BF),
            pltpu.VMEM((D, D), BF),
        ]
        + weights_scr,
        flops=6 * T * D * (2 * FF + D),
        nbytes=20 << 20,
        trans=2 * T * FF,
    )
    out_own, out_send, g_resid = res[:3]
    gmix = [res[3 + d * NP : 3 + (d + 1) * NP] for d in range(G)]
    packs = res[3 + G * NP : -1]
    vec1 = res[-1]

    def back(p, q_p):
        return attend_back_call(
            geo, p, meta, doc_lengths, segs, q_p, k[p], v[p], lses, made, ghead[p]
        )

    def turned(p, dep):
        return [gmix[0][p]] + [turn(after(gmix[d][p], dep), d) for d in range(1, G)]

    def exchanged(p, dep):
        return [turn(after(made_back[p][G - d], dep), d) for d in range(1, G)]

    def step_plane(parts):
        return (parts[0], plane(parts[1], 1, 0), plane(parts[2], 0, 1), plane(parts[3], 1, 1))

    def step_line(parts):
        return (parts[0],) + tuple(line(parts[d], d) for d in range(1, 4))

    def add(kernel, name, arrays, outs):
        return call(kernel, name, [(t, VM) for t in arrays], outs, nbytes=4 << 20)

    if geo.fast:
        sums = add(core_sum_kernel, "core_sum", (packs[0], turn(packs[1], 1)), [sds((4, 576, 128), BF)] * 4)
        a1 = step_plane(sums)
        ghead = [turned(0, sums[0])]
        made_back = [back(0, after(q[0], sums[0]))]
        q1 = add(plane_sum_kernel, "plane_sum", after(a1, made_back[0][0]), [sds((576, 128), BF)] * 4)
        b1 = step_line(q1)
        out_recv = swap_half(after(out_send, q1[0]))
        ghead.append(turned(1, q1[0]))
        made_back += [back(1, after(q[1], q1[0]))]
        packs2_out = [sds((1664, 128), BF)] * 2 + [sds((576, 128), BF)]
    else:
        b1 = ()
        ghead = [turned(p, q[p]) for p in range(NP)]
        made_back = [back(p, q[p]) for p in range(NP)]
        gq_recv = [turn(made_back[p][G - d], d) for d in range(1, G) for p in range(NP)]
        out_recv = swap_half(out_send)
        packs2_out = [sds((D, 3 * D), BF), sds((16, D), F32)]
    gq = [t[0] for t in made_back]
    packs2 = call(
        functools.partial(wgrad_kernel, geo),
        "wgrad",
        [(meta, SM), (vec1, VM), (gain1, VM), (shift1, VM), (after(h1, out_recv), VM)]
        + [(t, VM) for t in (*gq, *w_own, *b1)],
        packs2_out,
        scratch=[pltpu.VMEM((D, 3 * HL), BF), pltpu.VMEM((16, D), F32), pltpu.VMEM((D, PW), F32)],
        flops=2 * L * D * 3 * HL,
        nbytes=8 << 20,
    )
    if geo.fast:
        recv2, r1 = turn(packs2[1], 1), packs2[2]
        gq_recv = exchanged(0, recv2) + exchanged(1, recv2)
        own2 = packs2[0]
        parts2 = call(
            functools.partial(arrange_kernel, geo),
            "arrange",
            [(meta, SM), (own2, VM), (recv2, VM)],
            [sds((896, 128), BF)] * 4,
            nbytes=2 << 20,
        )
        a2 = step_plane(parts2)
        other1 = plane(after(r1, parts2[0]), 1, 0)

        gq = list(after(tuple(gq), parts2[0]))
    tgrad, tgrad_send = call(
        functools.partial(token_back_kernel, geo),
        "token_back",
        [(meta, SM), (gain1, VM), (g_resid, VM), (x0, VM), (x1, VM)]
        + [(t, VM) for t in (*gq, *gq_recv, *w_all)],
        [sds((2, BL, D), BF), sds((BL, D), BF)],
        flops=2 * T * D * 3 * D,
        nbytes=8 << 20,
    )
    tgrad = lax.dynamic_update_slice(tgrad, swap_half(tgrad_send)[None], (1 - s, 0, 0))
    if geo.fast:
        q2 = add(plane_sum_qkv_kernel, "plane_sum_qkv", after(a2, tgrad_send), [sds((320, 128), BF)] * 4)
        b2 = step_line(q2)
        mix_g, up_g, down_g = call(
            finish_kernel,
            "finish",
            [(meta, SM), (after(r1, q2[0]), VM), (other1, VM)],
            [sds(w.shape, F32) for w in (mix_weight, up_weight, down_weight)],
            nbytes=2 << 20,
        )
        r2, vec = add(
            line_sum_qkv_kernel, "line_sum_qkv", after(b2, mix_g), [sds((192, 128), BF), sds((16, D), F32)]
        )
        (qkv_g,) = call(
            finish_qkv_kernel,
            "finish_qkv",
            [(meta, SM), (r2, VM), (after(plane(r2, 1, 0), tgrad), VM)],
            [sds(qkv_weight.shape, F32)],
            nbytes=1 << 20,
        )
        grads = (qkv_g, mix_g, up_g, down_g)
    else:
        def reduced(w):
            w = lax.psum_scatter(w, "col", scatter_dimension=1, tiled=True)
            w = lax.psum_scatter(w, "row", scatter_dimension=0, tiled=True)
            return lax.psum(w, "dp").astype(F32)

        grads = (reduced(packs2[0]), reduced(packs[2]), reduced(packs[0]), reduced(packs[1]))
        vec = lax.psum(packs2[1], ("dp", "col", "row"))

    out_pair = jnp.where(s == 0, jnp.stack([out_own, out_recv]), jnp.stack([out_recv, out_own]))
    return (
        out_pair,
        tgrad,
        *grads,
        vec[:8],
        vec[8 : 8 + FF // D].reshape(FF),
    )


def solution(mesh):
    return jax.shard_map(
        body,
        mesh=mesh,
        in_specs=(
            P(("dp", "row"), "col", None),
            P(("dp", "row"), None),
            P(),
            P(),
            P("row", "col"),
            P(),
            P(),
            P("row", "col"),
            P(),
            P(),
            P(),
            P("row", "col"),
            P(),
            P("row", "col"),
            P(),
            P(("dp", "row"), "col", None),
        ),
        out_specs=(
            P(("dp", "row"), "col", None),
            P(("dp", "row"), "col", None),
            P("row", "col"),
            P("row", "col"),
            P("row", "col"),
            P("row", "col"),
            P(),
            P(),
        ),
        check_vma=False,
    )
```

```python
import functools

import jax
import jax.numpy as jnp
from jax import lax
from jax.experimental import pallas as pl
from jax.experimental.pallas import tpu as pltpu
from jax.sharding import PartitionSpec as P

HEAD_DIM = 64
EPS = 1e-05
NEG = -1e30
LOG2E = 1.4426950408889634
PW = 128

BF = jnp.bfloat16
F32 = jnp.float32
VM = pl.BlockSpec(memory_space=pltpu.VMEM)
SM = pl.BlockSpec(memory_space=pltpu.SMEM)
HBM = pl.BlockSpec(memory_space=pl.ANY)
TQ = 256
TK = 256
FC = 512
FT = 1024
RT = 256
KEEP_LB = ((0, 1, 4), (1, 4, 5))
SEND_LB = ((2, 3, 5), (0, 2, 3))


def sds(shape, dtype):
    return jax.ShapeDtypeStruct(shape, dtype)


NEAR = ('core_sum', 'plane_sum', 'arrange', 'plane_sum_qkv', 'line_sum_qkv', 'finish', 'finish_qkv', 'token_back')


def near(a):
    return pltpu.with_memory_space_constraint(a, pltpu.VMEM)


def call(kernel, name, ins, outs, scratch=(), flops=0, nbytes=0, trans=0, **kw):
    return pl.pallas_call(
        kernel,
        name=name,
        out_shape=tuple(o for o in outs),
        in_specs=[spec for _, spec in ins],
        out_specs=tuple(VM for _ in outs),
        scratch_shapes=list(scratch),
        compiler_params=pltpu.CompilerParams(vmem_limit_bytes=36 * 1024 * 1024, **kw),
        cost_estimate=pl.CostEstimate(flops=flops, bytes_accessed=nbytes, transcendentals=trans),
    )(*[near(a) if spec is VM and name in NEAR and a.ndim > 1 else a for a, spec in ins])


def nt(a, b):
    return lax.dot_general(a, b, (((1,), (1,)), ((), ())), preferred_element_type=F32)


def nn(a, b):
    return lax.dot_general(a, b, (((1,), (0,)), ((), ())), preferred_element_type=F32)


def tn(a, b):
    return lax.dot_general(a, b, (((0,), (0,)), ((), ())), preferred_element_type=F32)


def al(value, unit):
    return pl.multiple_of(value, unit)


def normed(v):
    mean = jnp.mean(v, axis=-1, keepdims=True)
    center = v - mean
    rstd = lax.rsqrt(jnp.mean(center * center, axis=-1, keepdims=True) + EPS)
    return center * rstd, rstd


class Geo:
    def __init__(self, dp, col, row, block_len, width, hidden):
        self.dp, self.C, self.R = dp, col, row
        self.G = col // 2
        self.BL = block_len
        self.L = block_len * col
        self.T = 2 * block_len
        self.D = width
        self.FF = hidden
        self.HL = width // self.G
        self.NP = self.HL // PW
        self.TQ = min(512, block_len)
        self.fast = (
            dp == 2 and col == 4 and row == 4 and width == 512 and hidden == 2048 and block_len % 256 == 0
        )

    def where(self, meta):
        col = meta[1]
        return col // self.G, col % self.G

    def block(self, s, g, e, d):
        half = s if e == 0 else 1 - s
        return half * self.G + lax.rem(g - d + self.G, self.G)


def norm_kernel(geo, meta, doc, gain, shift, *refs):
    s, g = geo.where(meta)
    pieces, (out, segk, segq) = refs[:-3], refs[-3:]
    fill_segments(geo, doc_ends(doc, s), segk, segq)
    for e in range(2):
        for d in range(geo.G):
            src = pieces[e * geo.G + d]
            base = geo.block(s, g, e, d) * geo.BL

            def step(i, carry):
                v = src[pl.ds(al(i * 128, 128), 128), :].astype(F32)
                xhat, _ = normed(v)
                out[pl.ds(al(base + i * 128, 128), 128), :] = (xhat * gain[...] + shift[...]).astype(BF)
                return carry

            lax.fori_loop(0, geo.BL // 128, step, 0, unroll=2)


def qkv_kernel(geo, meta, h1, bias, *refs):
    s, g = geo.where(meta)
    HL, D, NP = geo.HL, geo.D, geo.NP
    no = (3 + geo.G) * NP
    outs = refs[-no - 2 : -2] if geo.fast else refs[-no:]
    if geo.fast:
        pieces, (wscr, sem) = refs[:4], refs[-2:]
        z = meta[2]
        y, c = meta[1] // 2, meta[1] % 2
        copies = []
        for n in range(4):
            yy = y if n < 2 else 1 - y
            cp = c if n % 2 == 0 else 1 - c
            for d in range(4):
                zz = lax.rem(z - d + 4, 4)
                copies.append(
                    pltpu.make_async_copy(
                        pieces[n].at[d],
                        wscr.at[pl.ds(al(zz * 128, 128), 128), pl.ds(al((2 * yy + cp) * 384, 128), 384)],
                        sem,
                    )
                )
        for cpy in copies:
            cpy.start()
        for cpy in copies:
            cpy.wait()
    else:
        wscr = refs[0]

    def cols(part, p):
        return pl.ds(al(part * D + g * HL + p * PW, 128), PW)

    for d in range(geo.G):
        gd = lax.rem(g - d + geo.G, geo.G)
        for p in range(NP):
            for part in range(3):
                at = pl.ds(al(part * D + gd * HL + p * PW, 128), PW)
                outs[(3 + d) * NP + p][:, part * PW : (part + 1) * PW] = wscr[:, at]

    def step(i, carry):
        rows = pl.ds(al(i * 256, 256), 256)
        a = h1[rows, :]
        for p in range(NP):
            res = nn(a, outs[3 * NP + p][...])
            for part in range(3):
                outs[part * NP + p][rows, :] = (
                    res[:, part * PW : (part + 1) * PW] + bias[:, cols(part, p)]
                ).astype(BF)
        return carry

    lax.fori_loop(0, geo.L // 256, step, 0)


def doc_ends(doc, s):
    ends, total = [], 0
    for i in range(8):
        total = total + doc[s, i]
        ends.append(total)
    return ends


def span_start(ends, t):
    best = 0
    for e in ends:
        best = jnp.where(e <= t, e, best)
    return best


def span_end(ends, t, full):
    best = full
    for e in reversed(ends):
        best = jnp.where(e > t, e, best)
    return best


def fill_segments(geo, ends, segk, segq):
    def step(i, carry):
        rows = lax.broadcasted_iota(jnp.int32, (TK, 128), 0) + i * TK
        cols = lax.broadcasted_iota(jnp.int32, (8, TQ), 1) + i * TQ
        a = jnp.zeros((TK, 128), jnp.int32)
        b = jnp.zeros((8, TQ), jnp.int32)
        for e in ends:
            a += (rows >= e).astype(jnp.int32)
            b += (cols >= e).astype(jnp.int32)
        segk[pl.ds(al(i * TK, TK), TK), :] = a
        segq[:, pl.ds(al(i * TQ, TQ), TQ)] = b
        return carry

    lax.fori_loop(0, geo.L // TK, step, 0)


def mask_bias(segk, segq, k0, q0, tq):
    a = segk[pl.ds(k0, TK), :]
    b = segq[0:1, pl.ds(q0, tq)]
    same = jnp.concatenate([a] * (tq // 128), axis=1) == b
    return jnp.where(same, 0.0, NEG)


def head_mask(h, rows):
    lane = lax.broadcasted_iota(jnp.int32, (rows, PW), 1)
    return (lane // HEAD_DIM) == h


def ranges(first, last, one, lo, hi, tile):
    a = jnp.where(one, jnp.minimum((first + tile - 1) // tile, hi), hi)
    b = jnp.where(one, jnp.minimum(jnp.maximum(last // tile, a), hi), hi)
    return ((lo, a, True), (a, b, False), (b, hi, True))


HR = HEAD_DIM + 16


def attn_kernel(geo, dlist, meta, doc, segk, segq, *refs):
    G, NP, L, BL, TQF = geo.G, geo.NP, geo.L, geo.BL, geo.TQ
    q, k, v, refs = refs[:NP], refs[NP : 2 * NP], refs[2 * NP : 3 * NP], refs[3 * NP :]
    nd = len(dlist)
    outs, lses = refs[:nd], refs[nd : 2 * nd]
    vT, acc, sc = refs[2 * nd :]
    s, g = geo.where(meta)
    ends = doc_ends(doc, s)
    heads = [(p, h) for p in range(NP) for h in range(2)]

    def flip(i, carry):
        rows = pl.ds(al(i * TK, TK), TK)
        for p in range(NP):
            t = jnp.transpose(v[p][rows, :])
            for h in range(2):
                b = (2 * p + h) * HR
                vT[b : b + HEAD_DIM, rows] = t[h * HEAD_DIM : (h + 1) * HEAD_DIM, :]
                vT[b + HEAD_DIM : b + HR, rows] = jnp.ones((16, TK), BF)
        return carry

    lax.fori_loop(0, L // TK, flip, 0)

    for di, d in enumerate(dlist):

        def q_step(i, carry):
            e = i // (BL // TQF)
            off = al(lax.rem(i, BL // TQF) * TQF, TQF)
            half = jnp.where(e == 0, s, 1 - s)
            q0 = al((half * G + lax.rem(g - d + G, G)) * BL + off, TQF)
            first, last = span_start(ends, q0), span_end(ends, q0 + TQF - 1, L)
            one = first == span_start(ends, q0 + TQF - 1)
            klo = first // TK
            khi = (last + TK - 1) // TK
            qm = []
            for p, h in heads:
                qt = q[p][pl.ds(q0, TQF), :] * jnp.asarray(HEAD_DIM ** (-0.5), BF)
                qm.append(jnp.where(head_mask(h, TQF), qt, jnp.zeros_like(qt)))
            acc[...] = jnp.zeros_like(acc)

            def scores(masked, j, ms):
                k0 = al(j * TK, TK)
                if masked:
                    bias = mask_bias(segk, segq, k0, q0, TQF)
                out = []
                for n, (p, h) in enumerate(heads):
                    st = nt(k[p][pl.ds(k0, TK), :], qm[n])
                    if masked:
                        st = st + bias
                    sc[n, pl.ds(k0, TK), :] = st
                    out.append(jnp.maximum(ms[n], jnp.max(st.reshape(TK // 8, 8, TQF), axis=0)))
                return tuple(out)

            ms = tuple(jnp.full((8, TQF), -3e38, F32) for _ in heads)
            for lo, hi, masked in ranges(first, last, one, klo, khi, TK):
                ms = lax.fori_loop(lo, hi, functools.partial(scores, masked), ms)
            ms = [jnp.max(m, axis=0, keepdims=True) for m in ms]
            ml = [m * LOG2E for m in ms]

            def values(j, c2):
                k0 = al(j * TK, TK)
                for n in range(len(heads)):
                    pr = jnp.exp2(sc[n, pl.ds(k0, TK), :] * LOG2E - ml[n])
                    hs = slice(n * HR, (n + 1) * HR)
                    acc[hs, :] += nn(vT[hs, pl.ds(k0, TK)], pr.astype(BF))
                return c2

            lax.fori_loop(klo, khi, values, 0)
            for p in range(NP):
                parts = []
                for n in (2 * p, 2 * p + 1):
                    ls = acc[n * HR + HEAD_DIM : n * HR + HEAD_DIM + 1, :]
                    parts.append(acc[n * HR : n * HR + HEAD_DIM, :] * (1.0 / ls))
                    lses[di][e, n : n + 1, pl.ds(off, TQF)] = ms[n] + jnp.log(ls)
                res = jnp.transpose(jnp.concatenate(parts, axis=0)).astype(BF)
                outs[di][p, e, pl.ds(off, TQF), :] = res
            return carry

        lax.fori_loop(0, 2 * BL // TQF, q_step, 0)


def attn_back_kernel(geo, p, meta, doc, segk, segq, q, k, v, *refs):
    G, L, BL = geo.G, geo.L, geo.BL
    lses, mixed, grads = refs[:G], refs[G : 2 * G], refs[2 * G : 3 * G]
    out, sends = refs[3 * G], refs[3 * G + 1 : 4 * G]
    qm, gm, kT, dqT, delta, lse, dk, dv = refs[4 * G :]
    s, g = geo.where(meta)
    ends = doc_ends(doc, s)
    scale = HEAD_DIM ** (-0.5)
    for e in range(2):
        for d in range(G):
            base = geo.block(s, g, e, d) * BL

            def load(i, carry):
                src = pl.ds(al(i * 256, 256), 256)
                dst = pl.ds(al(base + i * 256, 256), 256)
                gt = grads[d][e, src, :]
                zero = jnp.zeros_like(gt)
                prod = jnp.transpose(gt.astype(F32) * mixed[d][p, e, src, :].astype(F32))
                qt = q[dst, :] * jnp.asarray(scale, BF)
                for h in range(2):
                    hs = slice(h * HEAD_DIM, (h + 1) * HEAD_DIM)
                    keep = head_mask(h, 256)
                    gm[h, dst, :] = jnp.where(keep, gt, zero)
                    qm[h, dst, :] = jnp.where(keep, qt, zero)
                    delta[h : h + 1, dst] = jnp.sum(prod[hs, :], axis=0, keepdims=True)
                lse[:, dst] = lses[d][e, :, src]
                kT[:, dst] = jnp.transpose(k[dst, :])
                dqT[:, dst] = jnp.zeros((PW, 256), F32)
                return carry

            lax.fori_loop(0, BL // 256, load, 0)

    def k_step(j, carry):
        k0 = al(j * TK, TK)
        first, last = span_start(ends, k0), span_end(ends, k0 + TK - 1, L)
        one = first == span_start(ends, k0 + TK - 1)
        qlo = first // TQ
        qhi = (last + TQ - 1) // TQ
        kt = k[pl.ds(k0, TK), :]
        vt = v[pl.ds(k0, TK), :]
        dk[...] = jnp.zeros_like(dk)
        dv[...] = jnp.zeros_like(dv)

        def q_step(masked, i, c2):
            q0 = al(i * TQ, TQ)
            qs = pl.ds(q0, TQ)
            if masked:
                bias = mask_bias(segk, segq, k0, q0, TQ)
            for h in range(2):
                hs = slice(h * HEAD_DIM, (h + 1) * HEAD_DIM)
                qh, gh = qm[h, qs, :], gm[h, qs, :]
                n = 2 * p + h
                st = nt(kt, qh) - lse[n : n + 1, qs]
                if masked:
                    st = st + bias
                pr = jnp.exp(st)
                ds = (pr * (nt(vt, gh) - delta[h : h + 1, qs])).astype(BF)
                dv[...] += nn(pr.astype(BF), gh)
                dk[...] += nn(ds, qh)
                dqT[hs, qs] += nn(kT[hs, pl.ds(k0, TK)], ds)
            return c2

        for lo, hi, masked in ranges(first, last, one, qlo, qhi, TQ):
            lax.fori_loop(lo, hi, functools.partial(q_step, masked), 0)
        out[pl.ds(k0, TK), PW : 2 * PW] = dk[...].astype(BF)
        out[pl.ds(k0, TK), 2 * PW : 3 * PW] = dv[...].astype(BF)
        return carry

    lax.fori_loop(0, L // TK, k_step, 0)

    def last_step(i, carry):
        rows = pl.ds(al(i * TQ, TQ), TQ)
        out[rows, 0:PW] = (jnp.transpose(dqT[:, rows]) * scale).astype(BF)
        return carry

    lax.fori_loop(0, L // TQ, last_step, 0)
    for d in range(1, G):
        for e in range(2):
            sends[d - 1][e] = out[pl.ds(al(geo.block(s, g, e, d) * BL, 256), BL), :]


def attend_call(geo, dlist, meta, doc, segs, q, k, v):
    NP, L, BL, nd = geo.NP, geo.L, geo.BL, len(dlist)
    share = nd / geo.G
    res = call(
        functools.partial(attn_kernel, geo, dlist),
        "attend",
        [(meta, SM), (doc, SM), (segs[0], VM), (segs[1], VM)] + [(t, VM) for t in (*q, *k, *v)],
        [sds((NP, 2, BL, PW), BF)] * nd + [sds((2, 8, BL), F32)] * nd,
        scratch=[
            pltpu.VMEM((2 * NP * HR, L), BF),
            pltpu.VMEM((2 * NP * HR, geo.TQ), F32),
            pltpu.VMEM((2 * NP, L, geo.TQ), F32),
        ],
        flops=int(2 * L * L * geo.HL * 4 * share),
        nbytes=L * geo.HL * 8,
        trans=int(L * L * NP * share),
    )
    return res[:nd], res[nd:]


def attend_back_call(geo, p, meta, doc, segs, q, k, v, lses, mixed, grads):
    L = geo.L
    return call(
        functools.partial(attn_back_kernel, geo, p),
        "attend_back",
        [(meta, SM), (doc, SM), (segs[0], VM), (segs[1], VM), (q, VM), (k, VM), (v, VM)]
        + [(t, VM) for t in (*lses, *mixed, *grads)],
        [sds((L, 3 * PW), BF)] + [sds((2, geo.BL, 3 * PW), BF)] * (geo.G - 1),
        scratch=[
            pltpu.VMEM((2, L, PW), BF),
            pltpu.VMEM((2, L, PW), BF),
            pltpu.VMEM((PW, L), BF),
            pltpu.VMEM((PW, L), F32),
            pltpu.VMEM((8, L), F32),
            pltpu.VMEM((8, L), F32),
            pltpu.VMEM((TK, PW), F32),
            pltpu.VMEM((TK, PW), F32),
        ],
        flops=2 * L * L * PW * 10,
        nbytes=L * PW * 20,
        trans=L * L,
    )


def gelu_parts(u):
    phi = 0.5 + 0.5 * lax.erf(u * (2.0 ** -0.5))
    pdf = jnp.exp(-0.5 * (u * u)) * 0.3989422804014327
    return phi, pdf


def ffn_kernel(geo, meta, *refs):
    G, HL, D, FF, BL, T, NP = geo.G, geo.HL, geo.D, geo.FF, geo.BL, geo.T, geo.NP
    s, g = geo.where(meta)
    pairs = [(d, p) for d in range(G) for p in range(NP)]
    x0, x1, cot, cot1, mixb, gain, shift, upb, downb = refs[:9]
    refs = refs[9:]
    mixed, refs = refs[:G], refs[G:]
    nw = 8 if geo.fast else 3
    wts, refs = refs[:nw], refs[nw:]
    out_own, out_send, g_resid = refs[:3]
    refs = refs[3:]
    gmix, refs = refs[: G * NP], refs[G * NP :]
    ng = 2 if geo.fast else 3
    packs, refs = refs[:ng], refs[ng:]
    vec, refs = refs[0], refs[1:]
    resid, h2, ffn, gh2, act_s, gu_s, ga_s, mg = refs[:8]
    refs = refs[8:]
    if geo.fast:
        wo, wu, wd, wg, sems = refs
        x, z = meta[0], meta[2]
        y, c = meta[1] // 2, meta[1] % 2
        groups = [[], [], []]
        for quad in range(4):
            yy = y if quad < 2 else 1 - y
            hh = x if quad % 2 == 0 else 1 - x
            for cc in range(2):
                cl = 2 * yy + (c if cc == 0 else 1 - c)
                src = wts[quad * 2 + cc]
                for d in range(4):
                    zz = lax.rem(z - d + 4, 4)
                    groups[0].append(
                        pltpu.make_async_copy(
                            src.at[d, pl.ds(512, 64), :],
                            wo.at[pl.ds(al(zz * 128 + hh * 64, 64), 64), pl.ds(al(cl * 128, 128), 128)],
                            sems.at[0],
                        )
                    )
                    for b in range(4):
                        groups[1].append(
                            pltpu.make_async_copy(
                                src.at[d, pl.ds(b * 64, 64), :],
                                wu.at[
                                    pl.ds(al(zz * 128 + hh * 64, 64), 64),
                                    pl.ds(al(cl * 512 + b * 128, 128), 128),
                                ],
                                sems.at[1],
                            )
                        )
                    groups[2].append(
                        pltpu.make_async_copy(
                            src.at[d, pl.ds(256, 256), :],
                            wd.at[pl.ds(al(zz * 512 + hh * 256, 256), 256), pl.ds(al(cl * 128, 128), 128)],
                            sems.at[2],
                        )
                    )
        for group in groups:
            for cpy in group:
                cpy.start()
        for cpy in groups[0]:
            cpy.wait()
    else:
        wo, wu, wd = wts
        (wg,) = refs

    zrow = jnp.zeros((1, D), F32)
    vec[...] = jnp.zeros_like(vec)

    for e in range(2):
        xe = x0 if e == 0 else x1
        ce = cot if e == 0 else cot1

        def first(i, carry):
            rows = pl.ds(al(i * RT, RT), RT)
            to = pl.ds(al(e * BL + i * RT, RT), RT)
            r = xe[rows, :].astype(F32) + mixb[...]
            for d, p in pairs:
                gp = lax.rem(g - d + G, G)
                r = r + nn(mixed[d][p, e, rows, :], wo[pl.ds(al(gp * HL + p * PW, 128), PW), :])
            resid[to, :] = r
            xhat, _ = normed(r)
            h2[to, :] = (xhat * gain[...] + shift[...]).astype(BF)
            ffn[to, :] = jnp.zeros((RT, D), F32)
            gh2[to, :] = jnp.zeros((RT, D), F32)
            return carry

        lax.fori_loop(0, BL // RT, first, 0)
    ga_s[0:BL, :] = cot[...]
    ga_s[BL:T, :] = cot1[...]
    if geo.fast:
        for group in groups[1:]:
            for cpy in group:
                cpy.wait()

    ft = FT if T % FT == 0 else RT

    def chunk(f, carry):
        f0 = al(f * FC, FC)
        fs = pl.ds(f0, FC)

        def rows_step(i, hs):
            rows = pl.ds(al(i * ft, ft), ft)
            u = nn(h2[rows, :], wu[:, fs]) + upb[:, fs]
            phi, pdf = gelu_parts(u)
            act = (u * phi).astype(BF)
            gu = (nt(ga_s[rows, :], wd[fs, :]) * (phi + u * pdf)).astype(BF)
            act_s[rows, :] = act
            gu_s[rows, :] = gu
            ffn[rows, :] += nn(act, wd[fs, :])
            gh2[rows, :] += nt(gu, wu[:, fs])
            return hs + jnp.sum(gu.astype(F32), axis=0, keepdims=True)

        hsum = lax.fori_loop(0, T // ft, rows_step, jnp.zeros((1, FC), F32))
        per = D // FC
        vec[pl.ds(8 + f // per, 1), pl.ds(al(lax.rem(f, per) * FC, 128), FC)] = hsum
        dn = tn(act_s[...], ga_s[...])
        if geo.fast:
            wg[...] = dn.astype(BF)
            zr = lax.rem(f - z + 4, 4)
            for cr in range(2):
                for yr in range(2):
                    cl = 2 * (y if yr == 0 else 1 - y) + (c if cr == 0 else 1 - c)
                    for hr in range(2):
                        hh = x if hr == 0 else 1 - x
                        packs[cr][yr * 2 + hr, zr, 256:512, :] = wg[
                            pl.ds(al(hh * 256, 256), 256), pl.ds(al(cl * 128, 128), 128)
                        ]
        else:
            packs[1][fs, :] = dn.astype(BF)
        up = tn(h2[...], gu_s[...])
        if geo.fast:
            wg[...] = up.astype(BF)
            fy, fcr = f // 2, lax.rem(f, 2)
            yr = jnp.where(fy == y, 0, 1)
            for cr in range(2):
                @pl.when((fcr == c) if cr == 0 else (fcr != c))
                def _():
                    for hr in range(2):
                        hh = x if hr == 0 else 1 - x
                        for k in range(4):
                            zz = lax.rem(z + k, 4)
                            for b in range(4):
                                packs[cr][yr * 2 + hr, k, b * 64 : b * 64 + 64, :] = wg[
                                    pl.ds(al(zz * 128 + hh * 64, 64), 64), b * 128 : b * 128 + 128
                                ]
        else:
            packs[0][:, fs] = up.astype(BF)
        return carry

    lax.fori_loop(0, FF // FC, chunk, 0)

    sums = (zrow, zrow, zrow, zrow)
    for e in range(2):
        ce = cot if e == 0 else cot1
        oe = out_own if e == 0 else out_send

        def back(i, carry):
            mb, fg, fs_, db = carry
            rows = pl.ds(al(i * RT, RT), RT)
            to = pl.ds(al(e * BL + i * RT, RT), RT)
            r = resid[to, :]
            oe[rows, :] = (r + ffn[to, :] + downb[...]).astype(BF)
            xhat, rstd = normed(r)
            gh = gh2[to, :]
            ct = ce[rows, :].astype(F32)
            gx = gh * gain[...]
            gr = ct + rstd * (
                gx
                - jnp.mean(gx, axis=-1, keepdims=True)
                - xhat * jnp.mean(gx * xhat, axis=-1, keepdims=True)
            )
            g_resid[to, :] = gr
            ga = gr.astype(BF)
            gu_s[to, 0:D] = ga
            for n, (d, p) in enumerate(pairs):
                gp = lax.rem(g + d, G)
                gmix[n][e, rows, :] = nt(ga, wo[pl.ds(al(gp * HL + p * PW, 128), PW), :]).astype(BF)
            return (
                mb + jnp.sum(ga.astype(F32), axis=0, keepdims=True),
                fg + jnp.sum(gh * xhat, axis=0, keepdims=True),
                fs_ + jnp.sum(gh, axis=0, keepdims=True),
                db + jnp.sum(ct, axis=0, keepdims=True),
            )

        sums = lax.fori_loop(0, BL // RT, back, sums)
    for i in range(4):
        vec[4 + i : 5 + i, :] = sums[i]
    for d, p in pairs:
        gp = lax.rem(g - d + G, G)
        part = tn(mixed[d][p, 0], gu_s[0:BL, 0:D]) + tn(mixed[d][p, 1], gu_s[BL:T, 0:D])
        mg[pl.ds(al(gp * HL + p * PW, 128), PW), :] = part.astype(BF)
    if geo.fast:
        for cr in range(2):
            for yr in range(2):
                cl = 2 * (y if yr == 0 else 1 - y) + (c if cr == 0 else 1 - c)
                for hr in range(2):
                    hh = x if hr == 0 else 1 - x
                    for k in range(4):
                        zz = lax.rem(z + k, 4)
                        packs[cr][yr * 2 + hr, k, 512:576, :] = mg[
                            pl.ds(al(zz * 128 + hh * 64, 64), 64), pl.ds(al(cl * 128, 128), 128)
                        ]
    else:
        packs[2][...] = mg[...]


def put_vec(ref, base, v):
    hi = v.astype(BF)
    lo = (v - hi.astype(F32)).astype(BF)
    for n, t in enumerate((hi, lo)):
        for b in range(4):
            at = base + (n * 4 + b) * 16
            ref[at : at + 16, :] = t[:, b * 128 : b * 128 + 128]


def get_vec(ref, base):
    def term(n):
        at = base + n * 64
        return jnp.concatenate([ref[at + b * 16 : at + b * 16 + 16, :] for b in range(4)], axis=1).astype(F32)

    return term(0) + term(1)


def wgrad_kernel(geo, meta, vec_in, gain, shift, h1, *refs):
    G, HL, D, NP = geo.G, geo.HL, geo.D, geo.NP
    s, g = geo.where(meta)
    gq, w, refs = refs[:NP], refs[NP : 2 * NP], refs[2 * NP :]
    if geo.fast:
        a, b, c, d, *refs = refs
        refs[2][...] = add4(a[...], b[...], c[...], d[...]).astype(BF)
        refs = refs[:2] + refs[3:]
    packs, (wg, vec, acc) = refs[:-3], refs[-3:]
    vec[...] = vec_in[...]
    ones = jnp.ones((16, geo.L), BF)
    back = jnp.zeros((16, D), F32)
    for p in range(NP):
        part = tn(h1[...], gq[p][...])
        wg[:, p * 3 * PW : (p + 1) * 3 * PW] = part.astype(BF)
        prod = part * w[p][...].astype(F32)
        prod = prod[:, 0:PW] + prod[:, PW : 2 * PW] + prod[:, 2 * PW : 3 * PW]
        if p == 0:
            acc[...] = prod
        else:
            acc[...] += prod
        total = nn(ones, gq[p][...])
        hi = total.astype(BF)
        lo = (total - hi.astype(F32)).astype(BF)
        back = back + nt(hi, w[p][...]) + nt(lo, w[p][...])
        cols = pl.ds(al(g * HL + p * PW, 128), PW)
        vec[2:3, cols] = total[0:1, 0:PW]
        vec[3:4, cols] = total[0:1, 2 * PW : 3 * PW]
    first = jnp.sum(jnp.transpose(acc[...]), axis=0, keepdims=True)
    vec[0:1, :] = (first - shift[...] * back[0:1, :]) / gain[...]
    vec[1:2, :] = back[0:1, :]
    if geo.fast:
        x, z, c = meta[0], meta[2], meta[1] % 2
        for cr, table in ((0, KEEP_LB), (1, SEND_LB)):
            for b in range(3):
                lb = [(t[b] % 2) * 3 + t[b] // 2 for t in table]
                at = jnp.where(c == 0, lb[0], lb[1])
                for hr in range(2):
                    hh = x if hr == 0 else 1 - x
                    for k in range(4):
                        zz = lax.rem(z + k, 4)
                        to = ((b * 2 + hr) * 4 + k) * 64
                        packs[cr][to : to + 64, :] = wg[
                            pl.ds(al(zz * 128 + hh * 64, 64), 64), pl.ds(al(at * 128, 128), 128)
                        ]
            put_vec(packs[cr], 1536, vec[...])
    else:
        packs[1][...] = vec[...]
        packs[0][...] = jnp.zeros_like(packs[0])
        for p in range(NP):
            for part in range(3):
                packs[0][:, pl.ds(al(part * D + g * HL + p * PW, 128), PW)] = wg[
                    :, (3 * p + part) * PW : (3 * p + part + 1) * PW
                ]


def token_back_kernel(geo, meta, gain, g_resid, x0, x1, *refs):
    G, BL, NP = geo.G, geo.BL, geo.NP
    s, g = geo.where(meta)
    gq, recv, w = refs[:NP], refs[NP : G * NP], refs[G * NP : 2 * G * NP]
    out, send = refs[2 * G * NP :]
    for e in range(2):
        xe = x0 if e == 0 else x1
        base = geo.block(s, g, e, 0) * BL

        def step(i, carry):
            rows = pl.ds(al(i * RT, RT), RT)
            to = pl.ds(al(e * BL + i * RT, RT), RT)
            at = pl.ds(al(base + i * RT, RT), RT)
            total = nt(gq[0][at, :], w[0][...])
            for p in range(1, NP):
                total = total + nt(gq[p][at, :], w[p][...])
            for n, r in enumerate(recv):
                total = total + nt(r[e, rows, :], w[NP + n][...])
            xhat, rstd = normed(xe[rows, :].astype(F32))
            gx = total * gain[...]
            res = g_resid[to, :] + rstd * (
                gx
                - jnp.mean(gx, axis=-1, keepdims=True)
                - xhat * jnp.mean(gx * xhat, axis=-1, keepdims=True)
            )
            if e == 0:
                out[s, rows, :] = res.astype(BF)
            else:
                send[rows, :] = res.astype(BF)
            return carry

        lax.fori_loop(0, BL // RT, step, 0)


def core_sum_kernel(own, recv, *outs):
    for q in range(4):
        outs[q][...] = (own[q].astype(F32) + recv[q].astype(F32)).astype(BF)


def arrange_kernel(geo, meta, keep, recv, *outs):
    y, c = meta[1] // 2, meta[1] % 2
    total = get_vec(keep, 1536) + get_vec(recv, 1536)
    for out in outs:
        put_vec(out, 768, total)
    for cs in range(2):
        mine = sorted((lb // 2) * 4 + 2 * cs + lb % 2 for lb in KEEP_LB[cs])
        theirs = sorted((lb // 2) * 4 + 2 * (1 - cs) + lb % 2 for lb in SEND_LB[1 - cs])
        for ys in range(2):
            @pl.when(jnp.logical_and(c == cs, y == ys))
            def _():
                for yr in range(2):
                    first = 3 * (2 * (ys ^ yr) + cs)
                    for o in range(3):
                        b = first + o
                        src, slot = (keep, mine.index(b)) if b in mine else (recv, theirs.index(b))
                        for hr in range(2):
                            for k in range(4):
                                at = ((slot * 2 + hr) * 4 + k) * 64
                                to = k * 192 + o * 64
                                outs[yr * 2 + hr][to : to + 64, :] = src[at : at + 64, :]


def add4(a, b, c, d):
    return (a.astype(F32) + b.astype(F32)) + (c.astype(F32) + d.astype(F32))


def plane_sum_kernel(a, b, c, d, *outs):
    for k in range(4):
        outs[k][...] = add4(a[k], b[k], c[k], d[k]).astype(BF)


def plane_sum_qkv_kernel(a, b, c, d, *outs):
    va, vb, vc, vd = (get_vec(t, 768) for t in (a, b, c, d))
    total = (va + vb) + (vc + vd)
    for k in range(4):
        at = slice(k * 192, k * 192 + 192)
        outs[k][0:192, :] = add4(a[at, :], b[at, :], c[at, :], d[at, :]).astype(BF)
        put_vec(outs[k], 192, total)


def line_sum_qkv_kernel(a, b, c, d, out, vec):
    va, vb, vc, vd = (get_vec(t, 192) for t in (a, b, c, d))
    vec[...] = (va + vc) + (vb + vd)
    out[...] = add4(a[0:192, :], b[0:192, :], c[0:192, :], d[0:192, :]).astype(BF)


def finish_kernel(meta, r, o, mix, up, down):
    x = meta[0]
    for src, h in ((r, x), (o, 1 - x)):
        rows = pl.ds(al(h * 64, 64), 64)
        for b in range(4):
            up[rows, b * 128 : b * 128 + 128] = src[b * 64 : b * 64 + 64, :].astype(F32)
        down[pl.ds(al(h * 256, 256), 256), :] = src[256:512, :].astype(F32)
        mix[rows, :] = src[512:576, :].astype(F32)


def finish_qkv_kernel(meta, r, o, qkv):
    x = meta[0]
    for src, h in ((r, x), (o, 1 - x)):
        for b in range(3):
            qkv[pl.ds(al(h * 64, 64), 64), b * 128 : b * 128 + 128] = src[b * 64 : b * 64 + 64, :].astype(F32)


def pack_kernel(meta, mix, up, down, rest):
    h = meta[0]
    rows = pl.ds(al(h * 64, 64), 64)
    for b in range(4):
        rest[b * 64 : b * 64 + 64, :] = up[rows, b * 128 : b * 128 + 128].astype(BF)
    rest[256:512, :] = down[pl.ds(al(h * 256, 256), 256), :].astype(BF)
    rest[512:576, :] = mix[rows, :].astype(BF)


def body(
    tokens,
    doc_lengths,
    norm_gain,
    norm_shift,
    qkv_weight,
    query_bias,
    value_bias,
    mix_weight,
    mix_bias,
    ffn_gain,
    ffn_shift,
    up_weight,
    up_bias,
    down_weight,
    down_bias,
    cotangent,
):
    DP, C, R = lax.axis_size("dp"), lax.axis_size("col"), lax.axis_size("row")
    _, BL, D = tokens.shape
    FF = up_bias.shape[0]
    geo = Geo(DP, C, R, BL, D, FF)
    G, HL, L, T = geo.G, geo.HL, geo.L, geo.T
    ix, ic, iz = lax.axis_index("dp"), lax.axis_index("col"), lax.axis_index("row")
    s = ic // G
    meta = jnp.stack([ix, ic, iz]).astype(jnp.int32)

    def swap_half(v):
        return lax.ppermute(v, "col", [(i, (i + G) % C) for i in range(C)])

    def turn(v, d):
        return lax.ppermute(v, "col", [(i, (i // G) * G + (i % G + d) % G) for i in range(C)])

    def plane(v, dx, dy):
        pairs = [
            (i * C + j, ((i + dx) % 2) * C + (j + dy * G) % C) for i in range(2) for j in range(C)
        ]
        return lax.ppermute(v, ("dp", "col"), pairs)

    def line(v, d):
        return lax.ppermute(v, "row", [(i, (i + d) % R) for i in range(R)])

    def row2(v):
        return v.reshape(1, v.shape[0])

    def pick(v, i):
        return lax.dynamic_index_in_dim(v, i, 0, keepdims=False)

    def after(v, dep):
        return lax.optimization_barrier((v, dep))[0]

    NP = geo.NP
    if geo.fast:
        def lines(v):
            return [v] + [line(v, d) for d in range(1, 4)]

        wq = qkv_weight.astype(BF)
        lines_qkv = lines(wq)
        x0 = pick(after(tokens, wq), s)
        x1 = swap_half(pick(after(tokens, wq), 1 - s))
        (half_rest,) = call(
            pack_kernel,
            "pack",
            [(after(meta, wq), SM), (mix_weight, VM), (up_weight, VM), (down_weight, VM)],
            [sds((576, 128), BF)],
            nbytes=2 << 20,
        )
        cot1 = swap_half(pick(after(cotangent, wq), 1 - s))
        own_qkv = jnp.stack(after(tuple(lines_qkv), half_rest))
        turns = [turn(after(t, own_qkv), 1) for t in (x0, x1)]
        across = swap_half(own_qkv)
        lines_rest = lines(after(half_rest, (own_qkv, *turns)))
    else:
        x0 = pick(tokens, s)
        x1 = swap_half(pick(tokens, 1 - s))

        def whole(w):
            w = lax.all_gather(w.astype(BF), "row", axis=0, tiled=True)
            return lax.all_gather(w, "col", axis=1, tiled=True)

        w_qkv = [whole(qkv_weight)]
        w_rest = [whole(mix_weight), whole(up_weight), whole(down_weight)]
    if geo.fast:
        pieces = [x0, turns[0], x1, turns[1]]
    else:
        pieces = [x0] + [turn(x0, d) for d in range(1, G)] + [x1] + [turn(x1, d) for d in range(1, G)]
    gain1, shift1 = row2(norm_gain), row2(norm_shift)
    h1, segk, segq = call(
        functools.partial(norm_kernel, geo),
        "norm_one",
        [(meta, SM), (doc_lengths, SM), (gain1, VM), (shift1, VM)] + [(p, VM) for p in pieces],
        [sds((L, D), BF), sds((L, 128), jnp.int32), sds((8, L), jnp.int32)],
        flops=L * D * 10,
        nbytes=L * D * 4,
    )
    segs = (segk, segq)
    if geo.fast:
        own_turned = turn(after(own_qkv, h1), 1)
        w_qkv = [own_qkv, own_turned, across, turn(after(across, (h1, *lines_rest)), 1)]
    bias = row2(jnp.concatenate([query_bias, jnp.zeros_like(query_bias), value_bias]))
    wspec = HBM if geo.fast else VM
    res = call(
        functools.partial(qkv_kernel, geo),
        "qkv",
        [(meta, SM), (h1, VM), (bias, VM)] + [(w, wspec) for w in w_qkv],
        [sds((L, PW), BF)] * (3 * NP) + [sds((D, 3 * PW), BF)] * (G * NP),
        scratch=[pltpu.VMEM((D, 3 * D), BF), pltpu.SemaphoreType.DMA(())] if geo.fast else [],
        flops=0,
        nbytes=0,
    )
    q, k, v, w_own = (res[n * NP : (n + 1) * NP] for n in range(4))
    w_all = res[3 * NP :]
    cot0 = pick(cotangent, s)
    if not geo.fast:
        cot1 = swap_half(pick(cotangent, 1 - s))
    if geo.fast:
        rest = jnp.stack(after(tuple(lines_rest), (q[0], cot1)))
        quads_rest = [plane(rest, 1, 0), plane(rest, 0, 1), plane(rest, 1, 1)]
    far, lse_far = attend_call(geo, tuple(range(1, G)), meta, doc_lengths, segs, q, k, v)
    if geo.fast:
        w_rest = [rest, turn(rest, 1)]
        w_rest += [t for u in after(tuple(quads_rest[:2]), (far[0], w_rest[1])) for t in (u, turn(u, 1))]
        q_own = list(after(tuple(q), (far[0], w_rest[2], w_rest[4])))
    else:
        q_own = list(after(tuple(q), far[0]))
    own, lse_own = attend_call(geo, (0,), meta, doc_lengths, segs, q_own, k, v)
    if geo.fast:
        diag = after(quads_rest[2], own[0])
        w_rest += [diag, turn(diag, 1)]
    made = [own[0]] + list(far)
    lses = list(lse_own) + list(lse_far)
    mixed = [made[0]] + [turn(made[G - d], d) for d in range(1, G)]
    packs_out = (
        [sds((4, 4, 576, 128), BF)] * 2
        if geo.fast
        else [sds((D, FF), BF), sds((FF, D), BF), sds((D, D), BF)]
    )
    weights_scr = (
        [
            pltpu.VMEM((D, D), BF),
            pltpu.VMEM((D, FF), BF),
            pltpu.VMEM((FF, D), BF),
            pltpu.VMEM((FC, FC), BF),
            pltpu.SemaphoreType.DMA((3,)),
        ]
        if geo.fast
        else [pltpu.VMEM((8, 128), BF)]
    )
    res = call(
        functools.partial(ffn_kernel, geo),
        "ffn",
        [(meta, SM), (x0, VM), (x1, VM), (cot0, VM), (cot1, VM)]
        + [(row2(a), VM) for a in (mix_bias, ffn_gain, ffn_shift, up_bias, down_bias)]
        + [(m, VM) for m in mixed]
        + [(w, wspec) for w in w_rest],
        [sds((BL, D), BF), sds((BL, D), BF), sds((T, D), F32)]
        + [sds((2, BL, PW), BF)] * (G * NP)
        + packs_out
        + [sds((16, D), F32)],
        scratch=[
            pltpu.VMEM((T, D), F32),
            pltpu.VMEM((T, D), BF),
            pltpu.VMEM((T, D), F32),
            pltpu.VMEM((T, D), F32),
            pltpu.VMEM((T, FC), BF),
            pltpu.VMEM((T, FC), BF),
            pltpu.VMEM((T, D), BF),
            pltpu.VMEM((D, D), BF),
        ]
        + weights_scr,
        flops=6 * T * D * (2 * FF + D),
        nbytes=20 << 20,
        trans=2 * T * FF,
    )
    out_own, out_send, g_resid = res[:3]
    gmix = [res[3 + d * NP : 3 + (d + 1) * NP] for d in range(G)]
    packs = res[3 + G * NP : -1]
    vec1 = res[-1]

    def back(p, q_p):
        return attend_back_call(
            geo, p, meta, doc_lengths, segs, q_p, k[p], v[p], lses, made, ghead[p]
        )

    def turned(p, dep):
        return [gmix[0][p]] + [turn(after(gmix[d][p], dep), d) for d in range(1, G)]

    def exchanged(p, dep):
        return [turn(after(made_back[p][G - d], dep), d) for d in range(1, G)]

    def step_plane(parts):
        return (parts[0], plane(parts[1], 1, 0), plane(parts[2], 0, 1), plane(parts[3], 1, 1))

    def step_line(parts):
        return (parts[0],) + tuple(line(parts[d], d) for d in range(1, 4))

    def add(kernel, name, arrays, outs):
        return call(kernel, name, [(t, VM) for t in arrays], outs, nbytes=4 << 20)

    if geo.fast:
        sums = add(core_sum_kernel, "core_sum", (packs[0], turn(packs[1], 1)), [sds((4, 576, 128), BF)] * 4)
        a1 = step_plane(sums)
        ghead = [turned(0, sums[0])]
        made_back = [back(0, after(q[0], sums[0]))]
        q1 = add(plane_sum_kernel, "plane_sum", after(a1, made_back[0][0]), [sds((576, 128), BF)] * 4)
        b1 = step_line(q1)
        out_recv = swap_half(after(out_send, q1[0]))
        ghead.append(turned(1, q1[0]))
        made_back += [back(1, after(q[1], q1[0]))]
        packs2_out = [sds((1664, 128), BF)] * 2 + [sds((576, 128), BF)]
    else:
        b1 = ()
        ghead = [turned(p, q[p]) for p in range(NP)]
        made_back = [back(p, q[p]) for p in range(NP)]
        gq_recv = [turn(made_back[p][G - d], d) for d in range(1, G) for p in range(NP)]
        out_recv = swap_half(out_send)
        packs2_out = [sds((D, 3 * D), BF), sds((16, D), F32)]
    gq = [t[0] for t in made_back]
    packs2 = call(
        functools.partial(wgrad_kernel, geo),
        "wgrad",
        [(meta, SM), (vec1, VM), (gain1, VM), (shift1, VM), (after(h1, out_recv), VM)]
        + [(t, VM) for t in (*gq, *w_own, *b1)],
        packs2_out,
        scratch=[pltpu.VMEM((D, 3 * HL), BF), pltpu.VMEM((16, D), F32), pltpu.VMEM((D, PW), F32)],
        flops=2 * L * D * 3 * HL,
        nbytes=8 << 20,
    )
    if geo.fast:
        recv2, r1 = turn(packs2[1], 1), packs2[2]
        gq_recv = exchanged(0, recv2) + exchanged(1, recv2)
        own2 = packs2[0]
        parts2 = call(
            functools.partial(arrange_kernel, geo),
            "arrange",
            [(meta, SM), (own2, VM), (recv2, VM)],
            [sds((896, 128), BF)] * 4,
            nbytes=2 << 20,
        )
        a2 = step_plane(parts2)
        other1 = plane(after(r1, parts2[0]), 1, 0)

        gq = list(after(tuple(gq), parts2[0]))
    tgrad, tgrad_send = call(
        functools.partial(token_back_kernel, geo),
        "token_back",
        [(meta, SM), (gain1, VM), (g_resid, VM), (x0, VM), (x1, VM)]
        + [(t, VM) for t in (*gq, *gq_recv, *w_all)],
        [sds((2, BL, D), BF), sds((BL, D), BF)],
        flops=2 * T * D * 3 * D,
        nbytes=8 << 20,
    )
    tgrad = lax.dynamic_update_slice(tgrad, swap_half(tgrad_send)[None], (1 - s, 0, 0))
    if geo.fast:
        q2 = add(plane_sum_qkv_kernel, "plane_sum_qkv", after(a2, tgrad_send), [sds((320, 128), BF)] * 4)
        b2 = step_line(q2)
        mix_g, up_g, down_g = call(
            finish_kernel,
            "finish",
            [(meta, SM), (after(r1, q2[0]), VM), (other1, VM)],
            [sds(w.shape, F32) for w in (mix_weight, up_weight, down_weight)],
            nbytes=2 << 20,
        )
        r2, vec = add(
            line_sum_qkv_kernel, "line_sum_qkv", after(b2, mix_g), [sds((192, 128), BF), sds((16, D), F32)]
        )
        (qkv_g,) = call(
            finish_qkv_kernel,
            "finish_qkv",
            [(meta, SM), (r2, VM), (after(plane(r2, 1, 0), tgrad), VM)],
            [sds(qkv_weight.shape, F32)],
            nbytes=1 << 20,
        )
        grads = (qkv_g, mix_g, up_g, down_g)
    else:
        def reduced(w):
            w = lax.psum_scatter(w, "col", scatter_dimension=1, tiled=True)
            w = lax.psum_scatter(w, "row", scatter_dimension=0, tiled=True)
            return lax.psum(w, "dp").astype(F32)

        grads = (reduced(packs2[0]), reduced(packs[2]), reduced(packs[0]), reduced(packs[1]))
        vec = lax.psum(packs2[1], ("dp", "col", "row"))

    out_pair = jnp.where(s == 0, jnp.stack([out_own, out_recv]), jnp.stack([out_recv, out_own]))
    return (
        out_pair,
        tgrad,
        *grads,
        vec[:8],
        vec[8 : 8 + FF // D].reshape(FF),
    )


def solution(mesh):
    return jax.shard_map(
        body,
        mesh=mesh,
        in_specs=(
            P(("dp", "row"), "col", None),
            P(("dp", "row"), None),
            P(),
            P(),
            P("row", "col"),
            P(),
            P(),
            P("row", "col"),
            P(),
            P(),
            P(),
            P("row", "col"),
            P(),
            P("row", "col"),
            P(),
            P(("dp", "row"), "col", None),
        ),
        out_specs=(
            P(("dp", "row"), "col", None),
            P(("dp", "row"), "col", None),
            P("row", "col"),
            P("row", "col"),
            P("row", "col"),
            P("row", "col"),
            P(),
            P(),
        ),
        check_vma=False,
    )
```

```python
import functools

import jax
import jax.numpy as jnp
from jax import lax
from jax.experimental import pallas as pl
from jax.experimental.pallas import tpu as pltpu
from jax.sharding import PartitionSpec as P

HEAD_DIM = 64
EPS = 1e-05
NEG = -1e30
LOG2E = 1.4426950408889634
PW = 128

BF = jnp.bfloat16
F32 = jnp.float32
VM = pl.BlockSpec(memory_space=pltpu.VMEM)
SM = pl.BlockSpec(memory_space=pltpu.SMEM)
HBM = pl.BlockSpec(memory_space=pl.ANY)
TQ = 256
TK = 256
FC = 512
FT = 1024
RT = 512
KEEP_LB = ((0, 1, 4), (1, 4, 5))
SEND_LB = ((2, 3, 5), (0, 2, 3))


def sds(shape, dtype):
    return jax.ShapeDtypeStruct(shape, dtype)


NEAR = ('core_sum', 'plane_sum', 'arrange', 'plane_sum_qkv', 'line_sum_qkv', 'finish', 'finish_qkv', 'token_back')


def near(a):
    return pltpu.with_memory_space_constraint(a, pltpu.VMEM)


def call(kernel, name, ins, outs, scratch=(), flops=0, nbytes=0, trans=0, **kw):
    return pl.pallas_call(
        kernel,
        name=name,
        out_shape=tuple(o for o in outs),
        in_specs=[spec for _, spec in ins],
        out_specs=tuple(VM for _ in outs),
        scratch_shapes=list(scratch),
        compiler_params=pltpu.CompilerParams(vmem_limit_bytes=36 * 1024 * 1024, **kw),
        cost_estimate=pl.CostEstimate(flops=flops, bytes_accessed=nbytes, transcendentals=trans),
    )(*[near(a) if spec is VM and name in NEAR and a.ndim > 1 else a for a, spec in ins])


def nt(a, b):
    return lax.dot_general(a, b, (((1,), (1,)), ((), ())), preferred_element_type=F32)


def nn(a, b):
    return lax.dot_general(a, b, (((1,), (0,)), ((), ())), preferred_element_type=F32)


def tn(a, b):
    return lax.dot_general(a, b, (((0,), (0,)), ((), ())), preferred_element_type=F32)


def al(value, unit):
    return pl.multiple_of(value, unit)


def normed(v):
    mean = jnp.mean(v, axis=-1, keepdims=True)
    center = v - mean
    rstd = lax.rsqrt(jnp.mean(center * center, axis=-1, keepdims=True) + EPS)
    return center * rstd, rstd


class Geo:
    def __init__(self, dp, col, row, block_len, width, hidden):
        self.dp, self.C, self.R = dp, col, row
        self.G = col // 2
        self.BL = block_len
        self.L = block_len * col
        self.T = 2 * block_len
        self.D = width
        self.FF = hidden
        self.HL = width // self.G
        self.NP = self.HL // PW
        self.TQ = min(512, block_len)
        self.fast = (
            dp == 2 and col == 4 and row == 4 and width == 512 and hidden == 2048 and block_len % 512 == 0
        )

    def where(self, meta):
        col = meta[1]
        return col // self.G, col % self.G

    def block(self, s, g, e, d):
        half = s if e == 0 else 1 - s
        return half * self.G + lax.rem(g - d + self.G, self.G)


def norm_kernel(geo, meta, doc, gain, shift, *refs):
    s, g = geo.where(meta)
    pieces, (out, segk, segq) = refs[:-3], refs[-3:]
    fill_segments(geo, doc_ends(doc, s), segk, segq)
    for e in range(2):
        for d in range(geo.G):
            src = pieces[e * geo.G + d]
            base = geo.block(s, g, e, d) * geo.BL

            def step(i, carry):
                v = src[pl.ds(al(i * 128, 128), 128), :].astype(F32)
                xhat, _ = normed(v)
                out[pl.ds(al(base + i * 128, 128), 128), :] = (xhat * gain[...] + shift[...]).astype(BF)
                return carry

            lax.fori_loop(0, geo.BL // 128, step, 0, unroll=2)


def qkv_kernel(geo, meta, h1, bias, *refs):
    s, g = geo.where(meta)
    HL, D, NP = geo.HL, geo.D, geo.NP
    no = (3 + geo.G) * NP
    outs = refs[-no - 2 : -2] if geo.fast else refs[-no:]
    if geo.fast:
        pieces, (wscr, sem) = refs[:4], refs[-2:]
        z = meta[2]
        y, c = meta[1] // 2, meta[1] % 2
        copies = []
        for n in range(4):
            yy = y if n < 2 else 1 - y
            cp = c if n % 2 == 0 else 1 - c
            for d in range(4):
                zz = lax.rem(z - d + 4, 4)
                copies.append(
                    pltpu.make_async_copy(
                        pieces[n].at[d],
                        wscr.at[pl.ds(al(zz * 128, 128), 128), pl.ds(al((2 * yy + cp) * 384, 128), 384)],
                        sem,
                    )
                )
        for cpy in copies:
            cpy.start()
        for cpy in copies:
            cpy.wait()
    else:
        wscr = refs[0]

    def cols(part, p):
        return pl.ds(al(part * D + g * HL + p * PW, 128), PW)

    for d in range(geo.G):
        gd = lax.rem(g - d + geo.G, geo.G)
        for p in range(NP):
            for part in range(3):
                at = pl.ds(al(part * D + gd * HL + p * PW, 128), PW)
                outs[(3 + d) * NP + p][:, part * PW : (part + 1) * PW] = wscr[:, at]

    def step(i, carry):
        rows = pl.ds(al(i * 512, 512), 512)
        a = h1[rows, :]
        for p in range(NP):
            res = nn(a, outs[3 * NP + p][...])
            for part in range(3):
                outs[part * NP + p][rows, :] = (
                    res[:, part * PW : (part + 1) * PW] + bias[:, cols(part, p)]
                ).astype(BF)
        return carry

    lax.fori_loop(0, geo.L // 512, step, 0)


def doc_ends(doc, s):
    ends, total = [], 0
    for i in range(8):
        total = total + doc[s, i]
        ends.append(total)
    return ends


def span_start(ends, t):
    best = 0
    for e in ends:
        best = jnp.where(e <= t, e, best)
    return best


def span_end(ends, t, full):
    best = full
    for e in reversed(ends):
        best = jnp.where(e > t, e, best)
    return best


def fill_segments(geo, ends, segk, segq):
    def step(i, carry):
        rows = lax.broadcasted_iota(jnp.int32, (TK, 128), 0) + i * TK
        cols = lax.broadcasted_iota(jnp.int32, (8, TQ), 1) + i * TQ
        a = jnp.zeros((TK, 128), jnp.int32)
        b = jnp.zeros((8, TQ), jnp.int32)
        for e in ends:
            a += (rows >= e).astype(jnp.int32)
            b += (cols >= e).astype(jnp.int32)
        segk[pl.ds(al(i * TK, TK), TK), :] = a
        segq[:, pl.ds(al(i * TQ, TQ), TQ)] = b
        return carry

    lax.fori_loop(0, geo.L // TK, step, 0)


def mask_bias(segk, segq, k0, q0, tq):
    a = segk[pl.ds(k0, TK), :]
    b = segq[0:1, pl.ds(q0, tq)]
    same = jnp.concatenate([a] * (tq // 128), axis=1) == b
    return jnp.where(same, 0.0, NEG)


def head_mask(h, rows):
    lane = lax.broadcasted_iota(jnp.int32, (rows, PW), 1)
    return (lane // HEAD_DIM) == h


def ranges(first, last, one, lo, hi, tile):
    a = jnp.where(one, jnp.minimum((first + tile - 1) // tile, hi), hi)
    b = jnp.where(one, jnp.minimum(jnp.maximum(last // tile, a), hi), hi)
    return ((lo, a, True), (a, b, False), (b, hi, True))


HR = HEAD_DIM + 16


def attn_kernel(geo, dlist, meta, doc, segk, segq, *refs):
    G, NP, L, BL, TQF = geo.G, geo.NP, geo.L, geo.BL, geo.TQ
    q, k, v, refs = refs[:NP], refs[NP : 2 * NP], refs[2 * NP : 3 * NP], refs[3 * NP :]
    nd = len(dlist)
    outs, lses = refs[:nd], refs[nd : 2 * nd]
    vT, acc, sc = refs[2 * nd :]
    s, g = geo.where(meta)
    ends = doc_ends(doc, s)
    heads = [(p, h) for p in range(NP) for h in range(2)]

    def flip(i, carry):
        rows = pl.ds(al(i * TK, TK), TK)
        for p in range(NP):
            t = jnp.transpose(v[p][rows, :])
            for h in range(2):
                b = (2 * p + h) * HR
                vT[b : b + HEAD_DIM, rows] = t[h * HEAD_DIM : (h + 1) * HEAD_DIM, :]
                vT[b + HEAD_DIM : b + HR, rows] = jnp.ones((16, TK), BF)
        return carry

    lax.fori_loop(0, L // TK, flip, 0)

    for di, d in enumerate(dlist):

        def q_step(i, carry):
            e = i // (BL // TQF)
            off = al(lax.rem(i, BL // TQF) * TQF, TQF)
            half = jnp.where(e == 0, s, 1 - s)
            q0 = al((half * G + lax.rem(g - d + G, G)) * BL + off, TQF)
            first, last = span_start(ends, q0), span_end(ends, q0 + TQF - 1, L)
            one = first == span_start(ends, q0 + TQF - 1)
            klo = first // TK
            khi = (last + TK - 1) // TK
            qm = []
            for p, h in heads:
                qt = q[p][pl.ds(q0, TQF), :] * jnp.asarray(HEAD_DIM ** (-0.5), BF)
                qm.append(jnp.where(head_mask(h, TQF), qt, jnp.zeros_like(qt)))
            acc[...] = jnp.zeros_like(acc)

            def scores(masked, j, ms):
                k0 = al(j * TK, TK)
                if masked:
                    bias = mask_bias(segk, segq, k0, q0, TQF)
                out = []
                for n, (p, h) in enumerate(heads):
                    st = nt(k[p][pl.ds(k0, TK), :], qm[n])
                    if masked:
                        st = st + bias
                    sc[n, pl.ds(k0, TK), :] = st
                    out.append(jnp.maximum(ms[n], jnp.max(st.reshape(TK // 8, 8, TQF), axis=0)))
                return tuple(out)

            ms = tuple(jnp.full((8, TQF), -3e38, F32) for _ in heads)
            for lo, hi, masked in ranges(first, last, one, klo, khi, TK):
                ms = lax.fori_loop(lo, hi, functools.partial(scores, masked), ms)
            ms = [jnp.max(m, axis=0, keepdims=True) for m in ms]
            ml = [m * LOG2E for m in ms]

            def values(j, c2):
                k0 = al(j * TK, TK)
                for n in range(len(heads)):
                    pr = jnp.exp2(sc[n, pl.ds(k0, TK), :] * LOG2E - ml[n])
                    hs = slice(n * HR, (n + 1) * HR)
                    acc[hs, :] += nn(vT[hs, pl.ds(k0, TK)], pr.astype(BF))
                return c2

            lax.fori_loop(klo, khi, values, 0)
            for p in range(NP):
                parts = []
                for n in (2 * p, 2 * p + 1):
                    ls = acc[n * HR + HEAD_DIM : n * HR + HEAD_DIM + 1, :]
                    parts.append(acc[n * HR : n * HR + HEAD_DIM, :] * (1.0 / ls))
                    lses[di][e, n : n + 1, pl.ds(off, TQF)] = ms[n] + jnp.log(ls)
                res = jnp.transpose(jnp.concatenate(parts, axis=0)).astype(BF)
                outs[di][p, e, pl.ds(off, TQF), :] = res
            return carry

        lax.fori_loop(0, 2 * BL // TQF, q_step, 0)


def attn_back_kernel(geo, p, meta, doc, segk, segq, q, k, v, *refs):
    G, L, BL = geo.G, geo.L, geo.BL
    lses, mixed, grads = refs[:G], refs[G : 2 * G], refs[2 * G : 3 * G]
    out, sends = refs[3 * G], refs[3 * G + 1 : 4 * G]
    qm, gm, kT, dqT, delta, lse, dk, dv = refs[4 * G :]
    s, g = geo.where(meta)
    ends = doc_ends(doc, s)
    scale = HEAD_DIM ** (-0.5)
    for e in range(2):
        for d in range(G):
            base = geo.block(s, g, e, d) * BL

            def load(i, carry):
                src = pl.ds(al(i * 256, 256), 256)
                dst = pl.ds(al(base + i * 256, 256), 256)
                gt = grads[d][e, src, :]
                zero = jnp.zeros_like(gt)
                prod = jnp.transpose(gt.astype(F32) * mixed[d][p, e, src, :].astype(F32))
                qt = q[dst, :] * jnp.asarray(scale, BF)
                for h in range(2):
                    hs = slice(h * HEAD_DIM, (h + 1) * HEAD_DIM)
                    keep = head_mask(h, 256)
                    gm[h, dst, :] = jnp.where(keep, gt, zero)
                    qm[h, dst, :] = jnp.where(keep, qt, zero)
                    delta[h : h + 1, dst] = jnp.sum(prod[hs, :], axis=0, keepdims=True)
                lse[:, dst] = lses[d][e, :, src]
                kT[:, dst] = jnp.transpose(k[dst, :])
                dqT[:, dst] = jnp.zeros((PW, 256), F32)
                return carry

            lax.fori_loop(0, BL // 256, load, 0)

    def k_step(j, carry):
        k0 = al(j * TK, TK)
        first, last = span_start(ends, k0), span_end(ends, k0 + TK - 1, L)
        one = first == span_start(ends, k0 + TK - 1)
        qlo = first // TQ
        qhi = (last + TQ - 1) // TQ
        kt = k[pl.ds(k0, TK), :]
        vt = v[pl.ds(k0, TK), :]
        dk[...] = jnp.zeros_like(dk)
        dv[...] = jnp.zeros_like(dv)

        def q_step(masked, i, c2):
            q0 = al(i * TQ, TQ)
            qs = pl.ds(q0, TQ)
            if masked:
                bias = mask_bias(segk, segq, k0, q0, TQ)
            for h in range(2):
                hs = slice(h * HEAD_DIM, (h + 1) * HEAD_DIM)
                qh, gh = qm[h, qs, :], gm[h, qs, :]
                n = 2 * p + h
                st = nt(kt, qh) - lse[n : n + 1, qs]
                if masked:
                    st = st + bias
                pr = jnp.exp(st)
                ds = (pr * (nt(vt, gh) - delta[h : h + 1, qs])).astype(BF)
                dv[...] += nn(pr.astype(BF), gh)
                dk[...] += nn(ds, qh)
                dqT[hs, qs] += nn(kT[hs, pl.ds(k0, TK)], ds)
            return c2

        for lo, hi, masked in ranges(first, last, one, qlo, qhi, TQ):
            lax.fori_loop(lo, hi, functools.partial(q_step, masked), 0)
        out[pl.ds(k0, TK), PW : 2 * PW] = dk[...].astype(BF)
        out[pl.ds(k0, TK), 2 * PW : 3 * PW] = dv[...].astype(BF)
        return carry

    lax.fori_loop(0, L // TK, k_step, 0)

    def last_step(i, carry):
        rows = pl.ds(al(i * TQ, TQ), TQ)
        out[rows, 0:PW] = (jnp.transpose(dqT[:, rows]) * scale).astype(BF)
        return carry

    lax.fori_loop(0, L // TQ, last_step, 0)
    for d in range(1, G):
        for e in range(2):
            sends[d - 1][e] = out[pl.ds(al(geo.block(s, g, e, d) * BL, 256), BL), :]


def attend_call(geo, dlist, meta, doc, segs, q, k, v):
    NP, L, BL, nd = geo.NP, geo.L, geo.BL, len(dlist)
    share = nd / geo.G
    res = call(
        functools.partial(attn_kernel, geo, dlist),
        "attend",
        [(meta, SM), (doc, SM), (segs[0], VM), (segs[1], VM)] + [(t, VM) for t in (*q, *k, *v)],
        [sds((NP, 2, BL, PW), BF)] * nd + [sds((2, 8, BL), F32)] * nd,
        scratch=[
            pltpu.VMEM((2 * NP * HR, L), BF),
            pltpu.VMEM((2 * NP * HR, geo.TQ), F32),
            pltpu.VMEM((2 * NP, L, geo.TQ), F32),
        ],
        flops=int(2 * L * L * geo.HL * 4 * share),
        nbytes=L * geo.HL * 8,
        trans=int(L * L * NP * share),
    )
    return res[:nd], res[nd:]


def attend_back_call(geo, p, meta, doc, segs, q, k, v, lses, mixed, grads):
    L = geo.L
    return call(
        functools.partial(attn_back_kernel, geo, p),
        "attend_back",
        [(meta, SM), (doc, SM), (segs[0], VM), (segs[1], VM), (q, VM), (k, VM), (v, VM)]
        + [(t, VM) for t in (*lses, *mixed, *grads)],
        [sds((L, 3 * PW), BF)] + [sds((2, geo.BL, 3 * PW), BF)] * (geo.G - 1),
        scratch=[
            pltpu.VMEM((2, L, PW), BF),
            pltpu.VMEM((2, L, PW), BF),
            pltpu.VMEM((PW, L), BF),
            pltpu.VMEM((PW, L), F32),
            pltpu.VMEM((8, L), F32),
            pltpu.VMEM((8, L), F32),
            pltpu.VMEM((TK, PW), F32),
            pltpu.VMEM((TK, PW), F32),
        ],
        flops=2 * L * L * PW * 10,
        nbytes=L * PW * 20,
        trans=L * L,
    )


def gelu_parts(u):
    phi = 0.5 + 0.5 * lax.erf(u * (2.0 ** -0.5))
    pdf = jnp.exp(-0.5 * (u * u)) * 0.3989422804014327
    return phi, pdf


def ffn_kernel(geo, meta, *refs):
    G, HL, D, FF, BL, T, NP = geo.G, geo.HL, geo.D, geo.FF, geo.BL, geo.T, geo.NP
    s, g = geo.where(meta)
    pairs = [(d, p) for d in range(G) for p in range(NP)]
    x0, x1, cot, cot1, mixb, gain, shift, upb, downb = refs[:9]
    refs = refs[9:]
    mixed, refs = refs[:G], refs[G:]
    nw = 8 if geo.fast else 3
    wts, refs = refs[:nw], refs[nw:]
    out_own, out_send, g_resid = refs[:3]
    refs = refs[3:]
    gmix, refs = refs[: G * NP], refs[G * NP :]
    ng = 2 if geo.fast else 3
    packs, refs = refs[:ng], refs[ng:]
    vec, refs = refs[0], refs[1:]
    resid, h2, ffn, gh2, act_s, gu_s, ga_s, mg = refs[:8]
    refs = refs[8:]
    if geo.fast:
        wo, wu, wd, wg, sems = refs
        x, z = meta[0], meta[2]
        y, c = meta[1] // 2, meta[1] % 2
        groups = [[], [], []]
        for quad in range(4):
            yy = y if quad < 2 else 1 - y
            hh = x if quad % 2 == 0 else 1 - x
            for cc in range(2):
                cl = 2 * yy + (c if cc == 0 else 1 - c)
                src = wts[quad * 2 + cc]
                for d in range(4):
                    zz = lax.rem(z - d + 4, 4)
                    groups[0].append(
                        pltpu.make_async_copy(
                            src.at[d, pl.ds(512, 64), :],
                            wo.at[pl.ds(al(zz * 128 + hh * 64, 64), 64), pl.ds(al(cl * 128, 128), 128)],
                            sems.at[0],
                        )
                    )
                    for b in range(4):
                        groups[1].append(
                            pltpu.make_async_copy(
                                src.at[d, pl.ds(b * 64, 64), :],
                                wu.at[
                                    pl.ds(al(zz * 128 + hh * 64, 64), 64),
                                    pl.ds(al(cl * 512 + b * 128, 128), 128),
                                ],
                                sems.at[1],
                            )
                        )
                    groups[2].append(
                        pltpu.make_async_copy(
                            src.at[d, pl.ds(256, 256), :],
                            wd.at[pl.ds(al(zz * 512 + hh * 256, 256), 256), pl.ds(al(cl * 128, 128), 128)],
                            sems.at[2],
                        )
                    )
        for group in groups:
            for cpy in group:
                cpy.start()
        for cpy in groups[0]:
            cpy.wait()
    else:
        wo, wu, wd = wts
        (wg,) = refs

    zrow = jnp.zeros((1, D), F32)
    vec[...] = jnp.zeros_like(vec)

    for e in range(2):
        xe = x0 if e == 0 else x1
        ce = cot if e == 0 else cot1

        def first(i, carry):
            rows = pl.ds(al(i * RT, RT), RT)
            to = pl.ds(al(e * BL + i * RT, RT), RT)
            r = xe[rows, :].astype(F32) + mixb[...]
            for d, p in pairs:
                gp = lax.rem(g - d + G, G)
                r = r + nn(mixed[d][p, e, rows, :], wo[pl.ds(al(gp * HL + p * PW, 128), PW), :])
            resid[to, :] = r
            xhat, _ = normed(r)
            h2[to, :] = (xhat * gain[...] + shift[...]).astype(BF)
            ffn[to, :] = jnp.zeros((RT, D), F32)
            gh2[to, :] = jnp.zeros((RT, D), F32)
            return carry

        lax.fori_loop(0, BL // RT, first, 0)
    ga_s[0:BL, :] = cot[...]
    ga_s[BL:T, :] = cot1[...]
    if geo.fast:
        for group in groups[1:]:
            for cpy in group:
                cpy.wait()

    ft = FT if T % FT == 0 else RT

    def chunk(f, carry):
        f0 = al(f * FC, FC)
        fs = pl.ds(f0, FC)

        def rows_step(i, hs):
            rows = pl.ds(al(i * ft, ft), ft)
            u = nn(h2[rows, :], wu[:, fs]) + upb[:, fs]
            phi, pdf = gelu_parts(u)
            act = (u * phi).astype(BF)
            gu = (nt(ga_s[rows, :], wd[fs, :]) * (phi + u * pdf)).astype(BF)
            act_s[rows, :] = act
            gu_s[rows, :] = gu
            ffn[rows, :] += nn(act, wd[fs, :])
            gh2[rows, :] += nt(gu, wu[:, fs])
            return hs + jnp.sum(gu.astype(F32), axis=0, keepdims=True)

        hsum = lax.fori_loop(0, T // ft, rows_step, jnp.zeros((1, FC), F32))
        per = D // FC
        vec[pl.ds(8 + f // per, 1), pl.ds(al(lax.rem(f, per) * FC, 128), FC)] = hsum
        dn = tn(act_s[...], ga_s[...])
        if geo.fast:
            wg[...] = dn.astype(BF)
            zr = lax.rem(f - z + 4, 4)
            for cr in range(2):
                for yr in range(2):
                    cl = 2 * (y if yr == 0 else 1 - y) + (c if cr == 0 else 1 - c)
                    for hr in range(2):
                        hh = x if hr == 0 else 1 - x
                        packs[cr][yr * 2 + hr, zr, 256:512, :] = wg[
                            pl.ds(al(hh * 256, 256), 256), pl.ds(al(cl * 128, 128), 128)
                        ]
        else:
            packs[1][fs, :] = dn.astype(BF)
        up = tn(h2[...], gu_s[...])
        if geo.fast:
            wg[...] = up.astype(BF)
            fy, fcr = f // 2, lax.rem(f, 2)
            yr = jnp.where(fy == y, 0, 1)
            for cr in range(2):
                @pl.when((fcr == c) if cr == 0 else (fcr != c))
                def _():
                    for hr in range(2):
                        hh = x if hr == 0 else 1 - x
                        for k in range(4):
                            zz = lax.rem(z + k, 4)
                            for b in range(4):
                                packs[cr][yr * 2 + hr, k, b * 64 : b * 64 + 64, :] = wg[
                                    pl.ds(al(zz * 128 + hh * 64, 64), 64), b * 128 : b * 128 + 128
                                ]
        else:
            packs[0][:, fs] = up.astype(BF)
        return carry

    lax.fori_loop(0, FF // FC, chunk, 0)

    sums = (zrow, zrow, zrow, zrow)
    for e in range(2):
        ce = cot if e == 0 else cot1
        oe = out_own if e == 0 else out_send

        def back(i, carry):
            mb, fg, fs_, db = carry
            rows = pl.ds(al(i * RT, RT), RT)
            to = pl.ds(al(e * BL + i * RT, RT), RT)
            r = resid[to, :]
            oe[rows, :] = (r + ffn[to, :] + downb[...]).astype(BF)
            xhat, rstd = normed(r)
            gh = gh2[to, :]
            ct = ce[rows, :].astype(F32)
            gx = gh * gain[...]
            gr = ct + rstd * (
                gx
                - jnp.mean(gx, axis=-1, keepdims=True)
                - xhat * jnp.mean(gx * xhat, axis=-1, keepdims=True)
            )
            g_resid[to, :] = gr
            ga = gr.astype(BF)
            gu_s[to, 0:D] = ga
            for n, (d, p) in enumerate(pairs):
                gp = lax.rem(g + d, G)
                gmix[n][e, rows, :] = nt(ga, wo[pl.ds(al(gp * HL + p * PW, 128), PW), :]).astype(BF)
            return (
                mb + jnp.sum(ga.astype(F32), axis=0, keepdims=True),
                fg + jnp.sum(gh * xhat, axis=0, keepdims=True),
                fs_ + jnp.sum(gh, axis=0, keepdims=True),
                db + jnp.sum(ct, axis=0, keepdims=True),
            )

        sums = lax.fori_loop(0, BL // RT, back, sums)
    for i in range(4):
        vec[4 + i : 5 + i, :] = sums[i]
    for d, p in pairs:
        gp = lax.rem(g - d + G, G)
        part = tn(mixed[d][p, 0], gu_s[0:BL, 0:D]) + tn(mixed[d][p, 1], gu_s[BL:T, 0:D])
        mg[pl.ds(al(gp * HL + p * PW, 128), PW), :] = part.astype(BF)
    if geo.fast:
        for cr in range(2):
            for yr in range(2):
                cl = 2 * (y if yr == 0 else 1 - y) + (c if cr == 0 else 1 - c)
                for hr in range(2):
                    hh = x if hr == 0 else 1 - x
                    for k in range(4):
                        zz = lax.rem(z + k, 4)
                        packs[cr][yr * 2 + hr, k, 512:576, :] = mg[
                            pl.ds(al(zz * 128 + hh * 64, 64), 64), pl.ds(al(cl * 128, 128), 128)
                        ]
    else:
        packs[2][...] = mg[...]


def put_vec(ref, base, v):
    hi = v.astype(BF)
    lo = (v - hi.astype(F32)).astype(BF)
    for n, t in enumerate((hi, lo)):
        for b in range(4):
            at = base + (n * 4 + b) * 16
            ref[at : at + 16, :] = t[:, b * 128 : b * 128 + 128]


def get_vec(ref, base):
    def term(n):
        at = base + n * 64
        return jnp.concatenate([ref[at + b * 16 : at + b * 16 + 16, :] for b in range(4)], axis=1).astype(F32)

    return term(0) + term(1)


def wgrad_kernel(geo, meta, vec_in, gain, shift, h1, *refs):
    G, HL, D, NP = geo.G, geo.HL, geo.D, geo.NP
    s, g = geo.where(meta)
    gq, w, refs = refs[:NP], refs[NP : 2 * NP], refs[2 * NP :]
    if geo.fast:
        a, b, c, d, *refs = refs
        refs[2][...] = add4(a[...], b[...], c[...], d[...]).astype(BF)
        refs = refs[:2] + refs[3:]
    packs, (wg, vec, acc) = refs[:-3], refs[-3:]
    vec[...] = vec_in[...]
    ones = jnp.ones((16, geo.L), BF)
    back = jnp.zeros((16, D), F32)
    for p in range(NP):
        part = tn(h1[...], gq[p][...])
        wg[:, p * 3 * PW : (p + 1) * 3 * PW] = part.astype(BF)
        prod = part * w[p][...].astype(F32)
        prod = prod[:, 0:PW] + prod[:, PW : 2 * PW] + prod[:, 2 * PW : 3 * PW]
        if p == 0:
            acc[...] = prod
        else:
            acc[...] += prod
        total = nn(ones, gq[p][...])
        hi = total.astype(BF)
        lo = (total - hi.astype(F32)).astype(BF)
        back = back + nt(hi, w[p][...]) + nt(lo, w[p][...])
        cols = pl.ds(al(g * HL + p * PW, 128), PW)
        vec[2:3, cols] = total[0:1, 0:PW]
        vec[3:4, cols] = total[0:1, 2 * PW : 3 * PW]
    first = jnp.sum(jnp.transpose(acc[...]), axis=0, keepdims=True)
    vec[0:1, :] = (first - shift[...] * back[0:1, :]) / gain[...]
    vec[1:2, :] = back[0:1, :]
    if geo.fast:
        x, z, c = meta[0], meta[2], meta[1] % 2
        for cr, table in ((0, KEEP_LB), (1, SEND_LB)):
            for b in range(3):
                lb = [(t[b] % 2) * 3 + t[b] // 2 for t in table]
                at = jnp.where(c == 0, lb[0], lb[1])
                for hr in range(2):
                    hh = x if hr == 0 else 1 - x
                    for k in range(4):
                        zz = lax.rem(z + k, 4)
                        to = ((b * 2 + hr) * 4 + k) * 64
                        packs[cr][to : to + 64, :] = wg[
                            pl.ds(al(zz * 128 + hh * 64, 64), 64), pl.ds(al(at * 128, 128), 128)
                        ]
            put_vec(packs[cr], 1536, vec[...])
    else:
        packs[1][...] = vec[...]
        packs[0][...] = jnp.zeros_like(packs[0])
        for p in range(NP):
            for part in range(3):
                packs[0][:, pl.ds(al(part * D + g * HL + p * PW, 128), PW)] = wg[
                    :, (3 * p + part) * PW : (3 * p + part + 1) * PW
                ]


def token_back_kernel(geo, meta, gain, g_resid, x0, x1, *refs):
    G, BL, NP = geo.G, geo.BL, geo.NP
    s, g = geo.where(meta)
    gq, recv, w = refs[:NP], refs[NP : G * NP], refs[G * NP : 2 * G * NP]
    out, send = refs[2 * G * NP :]
    for e in range(2):
        xe = x0 if e == 0 else x1
        base = geo.block(s, g, e, 0) * BL

        def step(i, carry):
            rows = pl.ds(al(i * RT, RT), RT)
            to = pl.ds(al(e * BL + i * RT, RT), RT)
            at = pl.ds(al(base + i * RT, RT), RT)
            total = nt(gq[0][at, :], w[0][...])
            for p in range(1, NP):
                total = total + nt(gq[p][at, :], w[p][...])
            for n, r in enumerate(recv):
                total = total + nt(r[e, rows, :], w[NP + n][...])
            xhat, rstd = normed(xe[rows, :].astype(F32))
            gx = total * gain[...]
            res = g_resid[to, :] + rstd * (
                gx
                - jnp.mean(gx, axis=-1, keepdims=True)
                - xhat * jnp.mean(gx * xhat, axis=-1, keepdims=True)
            )
            if e == 0:
                out[s, rows, :] = res.astype(BF)
            else:
                send[rows, :] = res.astype(BF)
            return carry

        lax.fori_loop(0, BL // RT, step, 0)


def core_sum_kernel(own, recv, *outs):
    for q in range(4):
        outs[q][...] = (own[q].astype(F32) + recv[q].astype(F32)).astype(BF)


def arrange_kernel(geo, meta, keep, recv, *outs):
    y, c = meta[1] // 2, meta[1] % 2
    total = get_vec(keep, 1536) + get_vec(recv, 1536)
    for out in outs:
        put_vec(out, 768, total)
    for cs in range(2):
        mine = sorted((lb // 2) * 4 + 2 * cs + lb % 2 for lb in KEEP_LB[cs])
        theirs = sorted((lb // 2) * 4 + 2 * (1 - cs) + lb % 2 for lb in SEND_LB[1 - cs])
        for ys in range(2):
            @pl.when(jnp.logical_and(c == cs, y == ys))
            def _():
                for yr in range(2):
                    first = 3 * (2 * (ys ^ yr) + cs)
                    for o in range(3):
                        b = first + o
                        src, slot = (keep, mine.index(b)) if b in mine else (recv, theirs.index(b))
                        for hr in range(2):
                            for k in range(4):
                                at = ((slot * 2 + hr) * 4 + k) * 64
                                to = k * 192 + o * 64
                                outs[yr * 2 + hr][to : to + 64, :] = src[at : at + 64, :]


def add4(a, b, c, d):
    return (a.astype(F32) + b.astype(F32)) + (c.astype(F32) + d.astype(F32))


def plane_sum_kernel(a, b, c, d, *outs):
    for k in range(4):
        outs[k][...] = add4(a[k], b[k], c[k], d[k]).astype(BF)


def plane_sum_qkv_kernel(a, b, c, d, *outs):
    va, vb, vc, vd = (get_vec(t, 768) for t in (a, b, c, d))
    total = (va + vb) + (vc + vd)
    for k in range(4):
        at = slice(k * 192, k * 192 + 192)
        outs[k][0:192, :] = add4(a[at, :], b[at, :], c[at, :], d[at, :]).astype(BF)
        put_vec(outs[k], 192, total)


def line_sum_qkv_kernel(a, b, c, d, out, vec):
    va, vb, vc, vd = (get_vec(t, 192) for t in (a, b, c, d))
    vec[...] = (va + vc) + (vb + vd)
    out[...] = add4(a[0:192, :], b[0:192, :], c[0:192, :], d[0:192, :]).astype(BF)


def finish_kernel(meta, r, o, mix, up, down):
    x = meta[0]
    for src, h in ((r, x), (o, 1 - x)):
        rows = pl.ds(al(h * 64, 64), 64)
        for b in range(4):
            up[rows, b * 128 : b * 128 + 128] = src[b * 64 : b * 64 + 64, :].astype(F32)
        down[pl.ds(al(h * 256, 256), 256), :] = src[256:512, :].astype(F32)
        mix[rows, :] = src[512:576, :].astype(F32)


def finish_qkv_kernel(meta, r, o, qkv):
    x = meta[0]
    for src, h in ((r, x), (o, 1 - x)):
        for b in range(3):
            qkv[pl.ds(al(h * 64, 64), 64), b * 128 : b * 128 + 128] = src[b * 64 : b * 64 + 64, :].astype(F32)


def pack_kernel(meta, mix, up, down, rest):
    h = meta[0]
    rows = pl.ds(al(h * 64, 64), 64)
    for b in range(4):
        rest[b * 64 : b * 64 + 64, :] = up[rows, b * 128 : b * 128 + 128].astype(BF)
    rest[256:512, :] = down[pl.ds(al(h * 256, 256), 256), :].astype(BF)
    rest[512:576, :] = mix[rows, :].astype(BF)


def body(
    tokens,
    doc_lengths,
    norm_gain,
    norm_shift,
    qkv_weight,
    query_bias,
    value_bias,
    mix_weight,
    mix_bias,
    ffn_gain,
    ffn_shift,
    up_weight,
    up_bias,
    down_weight,
    down_bias,
    cotangent,
):
    DP, C, R = lax.axis_size("dp"), lax.axis_size("col"), lax.axis_size("row")
    _, BL, D = tokens.shape
    FF = up_bias.shape[0]
    geo = Geo(DP, C, R, BL, D, FF)
    G, HL, L, T = geo.G, geo.HL, geo.L, geo.T
    ix, ic, iz = lax.axis_index("dp"), lax.axis_index("col"), lax.axis_index("row")
    s = ic // G
    meta = jnp.stack([ix, ic, iz]).astype(jnp.int32)

    def swap_half(v):
        return lax.ppermute(v, "col", [(i, (i + G) % C) for i in range(C)])

    def turn(v, d):
        return lax.ppermute(v, "col", [(i, (i // G) * G + (i % G + d) % G) for i in range(C)])

    def plane(v, dx, dy):
        pairs = [
            (i * C + j, ((i + dx) % 2) * C + (j + dy * G) % C) for i in range(2) for j in range(C)
        ]
        return lax.ppermute(v, ("dp", "col"), pairs)

    def line(v, d):
        return lax.ppermute(v, "row", [(i, (i + d) % R) for i in range(R)])

    def row2(v):
        return v.reshape(1, v.shape[0])

    def pick(v, i):
        return lax.dynamic_index_in_dim(v, i, 0, keepdims=False)

    def after(v, dep):
        return lax.optimization_barrier((v, dep))[0]

    NP = geo.NP
    if geo.fast:
        def lines(v):
            return [v] + [line(v, d) for d in range(1, 4)]

        wq = qkv_weight.astype(BF)
        lines_qkv = lines(wq)
        x0 = pick(after(tokens, wq), s)
        x1 = swap_half(pick(after(tokens, wq), 1 - s))
        (half_rest,) = call(
            pack_kernel,
            "pack",
            [(after(meta, wq), SM), (mix_weight, VM), (up_weight, VM), (down_weight, VM)],
            [sds((576, 128), BF)],
            nbytes=2 << 20,
        )
        cot1 = swap_half(pick(after(cotangent, wq), 1 - s))
        own_qkv = jnp.stack(after(tuple(lines_qkv), half_rest))
        turns = [turn(after(t, own_qkv), 1) for t in (x0, x1)]
        across = swap_half(own_qkv)
        lines_rest = lines(after(half_rest, (own_qkv, *turns)))
    else:
        x0 = pick(tokens, s)
        x1 = swap_half(pick(tokens, 1 - s))

        def whole(w):
            w = lax.all_gather(w.astype(BF), "row", axis=0, tiled=True)
            return lax.all_gather(w, "col", axis=1, tiled=True)

        w_qkv = [whole(qkv_weight)]
        w_rest = [whole(mix_weight), whole(up_weight), whole(down_weight)]
    if geo.fast:
        pieces = [x0, turns[0], x1, turns[1]]
    else:
        pieces = [x0] + [turn(x0, d) for d in range(1, G)] + [x1] + [turn(x1, d) for d in range(1, G)]
    gain1, shift1 = row2(norm_gain), row2(norm_shift)
    h1, segk, segq = call(
        functools.partial(norm_kernel, geo),
        "norm_one",
        [(meta, SM), (doc_lengths, SM), (gain1, VM), (shift1, VM)] + [(p, VM) for p in pieces],
        [sds((L, D), BF), sds((L, 128), jnp.int32), sds((8, L), jnp.int32)],
        flops=L * D * 10,
        nbytes=L * D * 4,
    )
    segs = (segk, segq)
    if geo.fast:
        own_turned = turn(after(own_qkv, h1), 1)
        w_qkv = [own_qkv, own_turned, across, turn(after(across, (h1, *lines_rest)), 1)]
    bias = row2(jnp.concatenate([query_bias, jnp.zeros_like(query_bias), value_bias]))
    wspec = HBM if geo.fast else VM
    res = call(
        functools.partial(qkv_kernel, geo),
        "qkv",
        [(meta, SM), (h1, VM), (bias, VM)] + [(w, wspec) for w in w_qkv],
        [sds((L, PW), BF)] * (3 * NP) + [sds((D, 3 * PW), BF)] * (G * NP),
        scratch=[pltpu.VMEM((D, 3 * D), BF), pltpu.SemaphoreType.DMA(())] if geo.fast else [],
        flops=0,
        nbytes=0,
    )
    q, k, v, w_own = (res[n * NP : (n + 1) * NP] for n in range(4))
    w_all = res[3 * NP :]
    cot0 = pick(cotangent, s)
    if not geo.fast:
        cot1 = swap_half(pick(cotangent, 1 - s))
    if geo.fast:
        rest = jnp.stack(after(tuple(lines_rest), (q[0], cot1)))
        quads_rest = [plane(rest, 1, 0), plane(rest, 0, 1), plane(rest, 1, 1)]
    far, lse_far = attend_call(geo, tuple(range(1, G)), meta, doc_lengths, segs, q, k, v)
    if geo.fast:
        w_rest = [rest, turn(rest, 1)]
        w_rest += [t for u in after(tuple(quads_rest[:2]), (far[0], w_rest[1])) for t in (u, turn(u, 1))]
        q_own = list(after(tuple(q), (far[0], w_rest[2], w_rest[4])))
    else:
        q_own = list(after(tuple(q), far[0]))
    own, lse_own = attend_call(geo, (0,), meta, doc_lengths, segs, q_own, k, v)
    if geo.fast:
        diag = after(quads_rest[2], own[0])
        w_rest += [diag, turn(diag, 1)]
    made = [own[0]] + list(far)
    lses = list(lse_own) + list(lse_far)
    mixed = [made[0]] + [turn(made[G - d], d) for d in range(1, G)]
    packs_out = (
        [sds((4, 4, 576, 128), BF)] * 2
        if geo.fast
        else [sds((D, FF), BF), sds((FF, D), BF), sds((D, D), BF)]
    )
    weights_scr = (
        [
            pltpu.VMEM((D, D), BF),
            pltpu.VMEM((D, FF), BF),
            pltpu.VMEM((FF, D), BF),
            pltpu.VMEM((FC, FC), BF),
            pltpu.SemaphoreType.DMA((3,)),
        ]
        if geo.fast
        else [pltpu.VMEM((8, 128), BF)]
    )
    res = call(
        functools.partial(ffn_kernel, geo),
        "ffn",
        [(meta, SM), (x0, VM), (x1, VM), (cot0, VM), (cot1, VM)]
        + [(row2(a), VM) for a in (mix_bias, ffn_gain, ffn_shift, up_bias, down_bias)]
        + [(m, VM) for m in mixed]
        + [(w, wspec) for w in w_rest],
        [sds((BL, D), BF), sds((BL, D), BF), sds((T, D), F32)]
        + [sds((2, BL, PW), BF)] * (G * NP)
        + packs_out
        + [sds((16, D), F32)],
        scratch=[
            pltpu.VMEM((T, D), F32),
            pltpu.VMEM((T, D), BF),
            pltpu.VMEM((T, D), F32),
            pltpu.VMEM((T, D), F32),
            pltpu.VMEM((T, FC), BF),
            pltpu.VMEM((T, FC), BF),
            pltpu.VMEM((T, D), BF),
            pltpu.VMEM((D, D), BF),
        ]
        + weights_scr,
        flops=6 * T * D * (2 * FF + D),
        nbytes=20 << 20,
        trans=2 * T * FF,
    )
    out_own, out_send, g_resid = res[:3]
    gmix = [res[3 + d * NP : 3 + (d + 1) * NP] for d in range(G)]
    packs = res[3 + G * NP : -1]
    vec1 = res[-1]

    def back(p, q_p):
        return attend_back_call(
            geo, p, meta, doc_lengths, segs, q_p, k[p], v[p], lses, made, ghead[p]
        )

    def turned(p, dep):
        return [gmix[0][p]] + [turn(after(gmix[d][p], dep), d) for d in range(1, G)]

    def exchanged(p, dep):
        return [turn(after(made_back[p][G - d], dep), d) for d in range(1, G)]

    def step_plane(parts):
        return (parts[0], plane(parts[1], 1, 0), plane(parts[2], 0, 1), plane(parts[3], 1, 1))

    def step_line(parts):
        return (parts[0],) + tuple(line(parts[d], d) for d in range(1, 4))

    def add(kernel, name, arrays, outs):
        return call(kernel, name, [(t, VM) for t in arrays], outs, nbytes=4 << 20)

    if geo.fast:
        sums = add(core_sum_kernel, "core_sum", (packs[0], turn(packs[1], 1)), [sds((4, 576, 128), BF)] * 4)
        a1 = step_plane(sums)
        ghead = [turned(0, sums[0])]
        made_back = [back(0, after(q[0], sums[0]))]
        q1 = add(plane_sum_kernel, "plane_sum", after(a1, made_back[0][0]), [sds((576, 128), BF)] * 4)
        b1 = step_line(q1)
        out_recv = swap_half(after(out_send, q1[0]))
        ghead.append(turned(1, q1[0]))
        made_back += [back(1, after(q[1], q1[0]))]
        packs2_out = [sds((1664, 128), BF)] * 2 + [sds((576, 128), BF)]
    else:
        b1 = ()
        ghead = [turned(p, q[p]) for p in range(NP)]
        made_back = [back(p, q[p]) for p in range(NP)]
        gq_recv = [turn(made_back[p][G - d], d) for d in range(1, G) for p in range(NP)]
        out_recv = swap_half(out_send)
        packs2_out = [sds((D, 3 * D), BF), sds((16, D), F32)]
    gq = [t[0] for t in made_back]
    packs2 = call(
        functools.partial(wgrad_kernel, geo),
        "wgrad",
        [(meta, SM), (vec1, VM), (gain1, VM), (shift1, VM), (after(h1, out_recv), VM)]
        + [(t, VM) for t in (*gq, *w_own, *b1)],
        packs2_out,
        scratch=[pltpu.VMEM((D, 3 * HL), BF), pltpu.VMEM((16, D), F32), pltpu.VMEM((D, PW), F32)],
        flops=2 * L * D * 3 * HL,
        nbytes=8 << 20,
    )
    if geo.fast:
        recv2, r1 = turn(packs2[1], 1), packs2[2]
        gq_recv = exchanged(0, recv2) + exchanged(1, recv2)
        own2 = packs2[0]
        parts2 = call(
            functools.partial(arrange_kernel, geo),
            "arrange",
            [(meta, SM), (own2, VM), (recv2, VM)],
            [sds((896, 128), BF)] * 4,
            nbytes=2 << 20,
        )
        a2 = step_plane(parts2)
        other1 = plane(after(r1, parts2[0]), 1, 0)

        gq = list(after(tuple(gq), parts2[0]))
    tgrad, tgrad_send = call(
        functools.partial(token_back_kernel, geo),
        "token_back",
        [(meta, SM), (gain1, VM), (g_resid, VM), (x0, VM), (x1, VM)]
        + [(t, VM) for t in (*gq, *gq_recv, *w_all)],
        [sds((2, BL, D), BF), sds((BL, D), BF)],
        flops=2 * T * D * 3 * D,
        nbytes=8 << 20,
    )
    tgrad = lax.dynamic_update_slice(tgrad, swap_half(tgrad_send)[None], (1 - s, 0, 0))
    if geo.fast:
        q2 = add(plane_sum_qkv_kernel, "plane_sum_qkv", after(a2, tgrad_send), [sds((320, 128), BF)] * 4)
        b2 = step_line(q2)
        mix_g, up_g, down_g = call(
            finish_kernel,
            "finish",
            [(meta, SM), (after(r1, q2[0]), VM), (other1, VM)],
            [sds(w.shape, F32) for w in (mix_weight, up_weight, down_weight)],
            nbytes=2 << 20,
        )
        r2, vec = add(
            line_sum_qkv_kernel, "line_sum_qkv", after(b2, mix_g), [sds((192, 128), BF), sds((16, D), F32)]
        )
        (qkv_g,) = call(
            finish_qkv_kernel,
            "finish_qkv",
            [(meta, SM), (r2, VM), (after(plane(r2, 1, 0), tgrad), VM)],
            [sds(qkv_weight.shape, F32)],
            nbytes=1 << 20,
        )
        grads = (qkv_g, mix_g, up_g, down_g)
    else:
        def reduced(w):
            w = lax.psum_scatter(w, "col", scatter_dimension=1, tiled=True)
            w = lax.psum_scatter(w, "row", scatter_dimension=0, tiled=True)
            return lax.psum(w, "dp").astype(F32)

        grads = (reduced(packs2[0]), reduced(packs[2]), reduced(packs[0]), reduced(packs[1]))
        vec = lax.psum(packs2[1], ("dp", "col", "row"))

    out_pair = jnp.where(s == 0, jnp.stack([out_own, out_recv]), jnp.stack([out_recv, out_own]))
    return (
        out_pair,
        tgrad,
        *grads,
        vec[:8],
        vec[8 : 8 + FF // D].reshape(FF),
    )


def solution(mesh):
    return jax.shard_map(
        body,
        mesh=mesh,
        in_specs=(
            P(("dp", "row"), "col", None),
            P(("dp", "row"), None),
            P(),
            P(),
            P("row", "col"),
            P(),
            P(),
            P("row", "col"),
            P(),
            P(),
            P(),
            P("row", "col"),
            P(),
            P("row", "col"),
            P(),
            P(("dp", "row"), "col", None),
        ),
        out_specs=(
            P(("dp", "row"), "col", None),
            P(("dp", "row"), "col", None),
            P("row", "col"),
            P("row", "col"),
            P("row", "col"),
            P("row", "col"),
            P(),
            P(),
        ),
        check_vma=False,
    )
```
